32 devices in a mesh: rows: 16 (over z, x, core), seq: 2 (over y).
Axes of the slice: x: 2, y: 2, z: 4, core: 2. Of those that a mesh axis runs over, the one named last changes fastest.
Arguments:
- inputs: bfloat16 [64, 1024, 768], P('rows', 'seq'), may hold values from -6 to 6
- split_point: int32 [64], P('rows'), may hold values from 256 to 767
- keep_mask: int32 [64, 1024], P('rows', 'seq'), may hold values from 0 to 1, as said below
- norm_gain: float32 [768], replicated, may hold values from 0.5 to 1.5
- proj_in: bfloat16 [768, 2304], replicated, may hold values from -0.21875 to 0.21875
- short_filter: float32 [3, 1536], replicated, may hold values from -3 to 3
- cond_filter: float32 [3, 768], replicated, may hold values from -0.109375 to 0.109375
- spec_slope: float32 [768], replicated, may hold values from -2 to 2
- spec_shift: float32 [768], replicated, may hold values from -3 to 3
- skip_gain: float32 [768], replicated, may hold values from -2.5 to 2.5
- proj_out: bfloat16 [768, 768], replicated, may hold values from -0.21875 to 0.21875
- ffn_gain: float32 [768], replicated, may hold values from 0.5 to 1.5
- ffn_in: bfloat16 [768, 6144], replicated, may hold values from -0.21875 to 0.21875
- ffn_out: bfloat16 [3072, 768], replicated, may hold values from -0.109375 to 0.109375
- out_grad: bfloat16 [64, 1024, 768], P('rows', 'seq'), may hold values from -6 to 6
Outputs:
- output: bfloat16 [64, 1024, 768], P('rows', 'seq')
- input_grad: float32 [64, 1024, 768], P('rows', 'seq')
- norm_gain_grad: float32 [768], replicated
- proj_in_grad: float32 [768, 2304], P('rows')
- short_filter_grad: float32 [3, 1536], replicated
- cond_filter_grad: float32 [3, 768], replicated
- spec_slope_grad: float32 [768], replicated
- spec_shift_grad: float32 [768], replicated
- skip_gain_grad: float32 [768], replicated
- proj_out_grad: float32 [768, 768], P('rows')
- ffn_gain_grad: float32 [768], replicated
- ffn_in_grad: float32 [768, 6144], P('rows')
- ffn_out_grad: float32 [3072, 768], P(None, 'rows')
The draws below stay inside these ranges and needn't reach their ends.
Inputs may be any that keep to these rules, and one draw needn't show every extreme that they name: `keep_mask`: each row keeps its first positions, at least 768 and at most 1023 of them, and masks the rest.
All inputs are finite; a program needn't handle non-finite values.
Results may differ from the reference program's by a relative error of at most 0.019.
Values may be sent and summed in bfloat16 or wider, within the bound.
A program may use at most 512 MiB of HBM per device.

```python
import jax
import jax.numpy as jnp
from jax import lax

D = 768
F = 3072
L = 1024
ROWS = 64


def draw_keep_mask(key, part):
    padding = jax.random.randint(key, (ROWS,), 1, L // 4 + 1)
    lengths = L - padding
    positions = jnp.arange(L, dtype=jnp.int32)
    return (positions[None, :] < lengths[:, None]).astype(jnp.int32)


def with_ends(values, own_key, smallest, high):
    dims = values.shape
    spot = [jax.random.randint(jax.random.fold_in(own_key, axis), (), 0, dims[axis]) for axis in range(len(dims))]
    values = values.at[tuple(spot)].set(smallest)
    longest = dims.index(max(dims))
    spot[longest] = (spot[longest] + 1) % dims[longest]
    return values.at[tuple(spot)].set(high)


def level_of(rng, dims, cuts, least, top_value):
    factor_of, own = 1.0, jax.random.fold_in(rng, 6)
    for position, parts in cuts:
        steps = jnp.exp(jax.random.uniform(jax.random.fold_in(own, position), (parts,), jnp.float32, least / len(cuts), top_value / len(cuts)))
        factor_of = factor_of * jnp.repeat(steps, dims[position] // parts).reshape([-1 if axis == position else 1 for axis in range(len(dims))])
    return factor_of


def noise(rng, dims, deviation, most, pieces=(), kind=jnp.bfloat16):
    loudness = level_of(rng, dims, pieces, -0.22, 0.18) if pieces else 1.0
    values = jax.random.normal(rng, dims, jnp.float32) * deviation * loudness
    return jnp.minimum(jnp.maximum(values, -most), most).astype(kind)


def setup_inputs(seed: int = 0) -> dict:
    keys = jax.random.split(jax.random.key(seed), 16)
    return {
        "inputs": noise(keys[0], (ROWS, L, D), 1.0, 6.0, ((0, 16), (1, 2))),
        "split_point": with_ends(jax.random.randint(keys[1], (ROWS,), L // 4, 3 * L // 4), jax.random.fold_in(keys[1], 1), L // 4, (3 * L // 4) - 1).astype(jnp.int32),
        "keep_mask": draw_keep_mask(jax.random.fold_in(keys[15], 71), 0),
        "norm_gain": jnp.clip(1.0 + 0.1 * jax.random.normal(keys[3], (D,), jnp.float32), 0.5, 1.5),
        "proj_in": noise(keys[4], (D, 3 * D), D ** -0.5, 0.21875),
        "short_filter": noise(keys[5], (3, 2 * D), 0.6, 3.0, (), jnp.float32),
        "cond_filter": noise(keys[6], (3, D), (3 * L) ** -0.5, 0.109375, (), jnp.float32),
        "spec_slope": jnp.clip(jax.random.uniform(keys[7], (D,), jnp.float32, -2.0, 2.0), -2.0, 2.0),
        "spec_shift": noise(keys[8], (D,), 1.0, 3.0, (), jnp.float32),
        "skip_gain": noise(keys[9], (D,), 0.5, 2.5, (), jnp.float32),
        "proj_out": noise(keys[10], (D, D), D ** -0.5, 0.21875),
        "ffn_gain": jnp.clip(1.0 + 0.1 * jax.random.normal(keys[11], (D,), jnp.float32), 0.5, 1.5),
        "ffn_in": noise(keys[12], (D, 2 * F), D ** -0.5, 0.21875),
        "ffn_out": noise(keys[13], (F, D), F ** -0.5, 0.109375),
        "out_grad": noise(keys[14], (ROWS, L, D), 1.0, 6.0, ((0, 16), (1, 2))),
    }


EPSILON = 1e-05
HIGHEST = lax.Precision.HIGHEST

@jax.custom_vjp
def low(v):
    return lax.optimization_barrier(v.astype(jnp.bfloat16)).astype(jnp.float32)

@jax.custom_vjp
def low_back(v):
    return v

def low_keep(v):
    return (low(v), None)

def low_pass(kept, grad):
    return (grad,)

def back_keep(v):
    return (v, None)

def back_low(kept, grad):
    return (low(grad),)
low.defvjp(low_keep, low_pass)
low_back.defvjp(back_keep, back_low)

def matmul(left, right):
    return jnp.dot(left, right, precision=HIGHEST)

def layer_norm(values, scaling):
    center = values - lax.optimization_barrier(jnp.mean(values, axis=-1, keepdims=True))
    spread = lax.optimization_barrier(jnp.mean(center * center, axis=-1, keepdims=True))
    return center * lax.rsqrt(spread + EPSILON) * scaling

def short_conv(signal, weights, same_one, same_two):
    prev_one = jnp.pad(signal, ((1, 0), (0, 0)))[:-1] * same_one
    prev_two = jnp.pad(signal, ((2, 0), (0, 0)))[:-2] * same_two
    return weights[0] * signal + weights[1] * prev_one + weights[2] * prev_two

def long_conv(values, conds, slopes, shifts):
    seq_length = values.shape[0]
    fft_size = 2 * seq_length
    value_spec = jnp.fft.rfft(values, n=fft_size, axis=0)
    cond_spec = jnp.fft.rfft(conds, n=fft_size, axis=0)
    power = jnp.real(cond_spec) * jnp.real(cond_spec) + jnp.imag(cond_spec) * jnp.imag(cond_spec)
    filter_spec = cond_spec * jax.nn.sigmoid(slopes * power + shifts)
    return jnp.fft.irfft(value_spec * filter_spec, n=fft_size, axis=0)[:seq_length]

def forward(params, values, split, keep):
    norm_gain, proj_in, short_filter, cond_filter, spec_slope, spec_shift, skip_gain, proj_out, ffn_gain, ffn_in, ffn_out = params
    seq_length, model_width = values.shape
    hidden_width = ffn_out.shape[0]
    positions = jnp.arange(seq_length, dtype=jnp.int32)
    segment = positions >= split
    same_one = (segment == (positions - 1 >= split)).astype(jnp.float32)[:, None]
    same_two = (segment == (positions - 2 >= split)).astype(jnp.float32)[:, None]
    keep_float = keep.astype(jnp.float32)[:, None]
    first_act = low(layer_norm(values, norm_gain))
    projected = low_back(low(matmul(first_act, proj_in)))
    query_in = projected[:, :model_width]
    key_in = projected[:, model_width:2 * model_width]
    value_in = projected[:, 2 * model_width:]
    conv_both = short_conv(jnp.concatenate([query_in, value_in], axis=1), short_filter, same_one, same_two)
    query_conv = conv_both[:, :model_width]
    value_low = low_back(low(conv_both[:, model_width:] * keep_float))
    cond_low = low_back(low(short_conv(key_in, cond_filter, same_one, same_two) * keep_float))
    mixed = long_conv(value_low, cond_low, spec_slope, spec_shift) + skip_gain * value_low
    mixed_low = low(low_back(mixed))
    gated = low(query_conv * mixed_low)
    resid = values + low_back(matmul(gated, proj_out))
    second_act = low(layer_norm(resid, ffn_gain))
    gate_up = low_back(matmul(second_act, ffn_in))
    hidden = low(jax.nn.gelu(gate_up[:, :hidden_width], approximate=False) * gate_up[:, hidden_width:])
    return resid + matmul(hidden, ffn_out)

def reference(inputs, split_point, keep_mask, norm_gain, proj_in, short_filter, cond_filter, spec_slope, spec_shift, skip_gain, proj_out, ffn_gain, ffn_in, ffn_out, out_grad):
    params = (norm_gain, proj_in.astype(jnp.float32), short_filter, cond_filter, spec_slope, spec_shift, skip_gain, proj_out.astype(jnp.float32), ffn_gain, ffn_in.astype(jnp.float32), ffn_out.astype(jnp.float32))

    def one_row(totals, row_data):
        row_in, row_split, row_keep, row_grad = row_data

        def apply_row(weights, values):
            return forward(weights, values, row_split, row_keep)
        result, pull = jax.vjp(apply_row, params, row_in.astype(jnp.float32))
        param_grads, value_grad = pull(row_grad.astype(jnp.float32))
        totals = jax.tree.map(lambda a, b: a + b, totals, param_grads)
        return (totals, (result.astype(jnp.bfloat16), value_grad))
    zeros = jax.tree.map(jnp.zeros_like, params)
    totals, (output, input_grad) = lax.scan(one_row, zeros, (inputs, split_point, keep_mask, out_grad))
    return (output, input_grad, totals[0], totals[1], totals[2], totals[3], totals[4], totals[5], totals[6], totals[7], totals[8], totals[9], totals[10])
```

```python
import functools
import math

import jax
import jax.numpy as jnp
from jax import lax
from jax.experimental import pallas as pl
from jax.experimental.pallas import tpu as pltpu
from jax.sharding import PartitionSpec as P

EPSILON = 1e-05
BF = jnp.bfloat16
F32 = jnp.float32
ROOT_HALF = math.sqrt(0.5)
LIMIT = 67043328


def mm(a, b):
    return lax.dot_general(a, b, (((1,), (0,)), ((), ())), preferred_element_type=F32)


def mm_t(a, b):
    return lax.dot_general(a, b, (((1,), (1,)), ((), ())), preferred_element_type=F32)


def spectral_tables(length, offset):
    quarter = length // 4
    two_n = 2 * length
    m = lax.broadcasted_iota(jnp.int32, (quarter, quarter), 0)
    s = lax.broadcasted_iota(jnp.int32, (quarter, quarter), 1)

    def cos_sin(freq):
        angle = ((freq * s + offset) % two_n).astype(F32) * (2.0 * math.pi / two_n)
        return jnp.cos(angle), jnp.sin(angle)

    half = quarter // 2
    forward, inverse = [], []
    for r in (1, 2, 3):
        c, sn = cos_sin(8 * m + r)
        forward.append(jnp.concatenate([jnp.concatenate([c, sn], 1), jnp.concatenate([-sn, c], 1)], 0))
        inverse.append(forward[-1].T * (2.0 / two_n))
    row = m % half
    low = m < half
    c, sn = cos_sin(8 * jnp.where(m == half, half, row))
    zero = jnp.where(low | (m == half), c, -sn)
    c4, sn4 = cos_sin(8 * row + 4)
    four = jnp.where(low, c4, -sn4)
    edge = jnp.where((m == 0) | (m == half), 1.0, 2.0) / two_n
    fwd_real = jnp.concatenate([zero, four], 0)
    inv_real = jnp.concatenate([(zero * edge).T, four.T * (2.0 / two_n)], 0)
    return (
        fwd_real.astype(BF),
        jnp.concatenate(forward, 0).astype(BF),
        inv_real.astype(BF),
        jnp.concatenate(inverse, 0).astype(BF),
    )


def loop(count, body):
    lax.fori_loop(0, count, lambda i, c: (body(i), c)[1], 0)


def rows_of(i, size):
    return pl.ds(pl.multiple_of(i * size, size), size)


def norm_stats(v):
    center = v - jnp.mean(v, axis=-1, keepdims=True)
    scale = lax.rsqrt(jnp.mean(center * center, axis=-1, keepdims=True) + EPSILON)
    return center * scale, scale


def same_masks(position, split):
    same_one = position != split
    return same_one, same_one & (position != split + 1)


def butterfly(x_ref, y_ref, lane, width, quarter):
    tile = 32
    lanes = slice(lane, lane + width)

    def body(i):
        x0, x1, x2, x3 = [
            x_ref[pl.ds(pl.multiple_of(q * quarter + i * tile, tile), tile), :].astype(F32) for q in range(4)
        ]
        a, b, c, d = x0 + x2, x1 + x3, x0 - x2, x1 - x3
        sd, sb = d * ROOT_HALF, b * ROOT_HALF
        out = (a + b, a - b, x0 + sd, -x2 - sb, c, -d, x0 - sd, x2 - sb)
        for k, value in enumerate(out):
            y_ref[pl.ds(pl.multiple_of(k * quarter + i * tile, tile), tile), lanes] = value.astype(BF)

    loop(quarter // tile, body)


def blockwise(y_ref, spec_ref, fwd_real_ref, fwd_ref, quarter):
    q = quarter
    for k in range(2):
        spec_ref[k * q : (k + 1) * q, :] = mm(fwd_real_ref[k * q : (k + 1) * q, :], y_ref[k * q : (k + 1) * q, :])
    for k in range(3):
        spec_ref[2 * q + 2 * k * q : 2 * q + 2 * (k + 1) * q, :] = mm(
            fwd_ref[2 * k * q : 2 * (k + 1) * q, :], y_ref[2 * q + 2 * k * q : 2 * q + 2 * (k + 1) * q, :]
        )


def resynth(u_ref, out_ref, inv_real_ref, inv_ref, quarter):
    blockwise(u_ref, out_ref, inv_real_ref, inv_ref, quarter)


def each_bin(quarter, body, tile=16):
    half = quarter // 2
    body(0, half, True)

    def run(base, span, skip):
        def step(i):
            start = base + (i + skip) * tile
            body(start, start + span, False)

        loop(span // tile - skip, step)

    run(0, half, 1)
    run(quarter, half, 0)
    for k in range(3):
        run(2 * quarter + 2 * k * quarter, quarter, 0)


def recombine(o_ref, lanes, i, tile, quarter):
    def part(k):
        return o_ref[pl.ds(pl.multiple_of(k * quarter + i * tile, tile), tile), lanes]

    u0, u4, a1, b1, a2, b2, a3, b3 = [part(k) for k in range(8)]
    even, odd = u0 + u4, u0 - u4
    return (
        even + a1 + a2 + a3,
        odd + (a1 - b1 - a3 - b3) * ROOT_HALF - b2,
        even - b1 - a2 + b3,
        odd + (a3 - b3 - a1 - b1) * ROOT_HALF + b2,
    )


def conv_back(ref, t, tile, weights, split):
    block = ref[pl.ds(pl.multiple_of(t, tile), tile + 8), :]
    width = block.shape[1]
    position = t + lax.broadcasted_iota(jnp.int32, (tile, width), 0)
    one, two = same_masks(position, split)
    return (
        weights[0:1, :] * block[8 : tile + 8]
        + jnp.where(one, weights[1:2, :] * block[7 : tile + 7], 0.0)
        + jnp.where(two, weights[2:3, :] * block[6 : tile + 6], 0.0)
    )


def mixer_forward_kernel(
    split_ref, keep_ref, x_ref, norm_gain_ref, wq_ref, wk_ref, wv_ref, fq_ref, fv_ref, fk_ref, slope_ref, shift_ref,
    skip_ref, wo_ref, ffn_gain_ref, fwd_real_ref, fwd_ref, inv_real_ref, inv_ref,
    first_ref, q_ref, k_ref, v_ref, mixed_ref, gated_ref, resid_ref, second_ref,
    qs, ks, vs, xv, xc, y_s, spec_s, u_s, o_s, qc,
):
    r, j = pl.program_id(0), pl.program_id(1)
    length, width = q_ref.shape
    quarter = length // 4
    split, keep = split_ref[r], keep_ref[r]
    tile = 64

    @pl.when(j == 0)
    def _():
        def body(i):
            rows = rows_of(i, tile)
            v = x_ref[rows, :].astype(F32)
            n, _ = norm_stats(v)
            first_ref[rows, :] = (n * norm_gain_ref[...]).astype(BF)
            resid_ref[rows, :] = v

        loop(length // tile, body)
        for ref in (qs, ks, vs):
            ref[0:8, :] = jnp.zeros((8, width), F32)

    for w_ref, out_ref, ref in ((wq_ref, q_ref, qs), (wk_ref, k_ref, ks), (wv_ref, v_ref, vs)):
        value = mm(first_ref[...], w_ref[...]).astype(BF)
        out_ref[...] = value
        ref[8 : 8 + length, :] = value.astype(F32)

    def conv(i):
        t = i * tile
        rows = rows_of(i, tile)
        kept = t + lax.broadcasted_iota(jnp.int32, (tile, width), 0) < keep
        qc[rows, :] = conv_back(qs, t, tile, fq_ref, split)
        xv[rows, :] = jnp.where(kept, conv_back(vs, t, tile, fv_ref, split), 0.0).astype(BF)
        xc[rows, :] = jnp.where(kept, conv_back(ks, t, tile, fk_ref, split), 0.0).astype(BF)

    loop(length // tile, conv)
    butterfly(xv, y_s, 0, width, quarter)
    butterfly(xc, y_s, width, width, quarter)
    blockwise(y_s, spec_s, fwd_real_ref, fwd_ref, quarter)

    def bins(re, im, first):
        n = 16
        re, im = pl.ds(pl.multiple_of(re, n), n), pl.ds(pl.multiple_of(im, n), n)
        vr, vi = spec_s[re, 0:width], spec_s[im, 0:width]
        cr, ci = spec_s[re, width : 2 * width], spec_s[im, width : 2 * width]
        slope, shift = slope_ref[...], shift_ref[...]
        rr, ii = cr * cr, ci * ci
        if first:
            edge = lax.broadcasted_iota(jnp.int32, (n, width), 0) == 0
            hr = cr * jax.nn.sigmoid(slope * jnp.where(edge, rr, rr + ii) + shift)
            hi = ci * jax.nn.sigmoid(slope * jnp.where(edge, ii, rr + ii) + shift)
            ur = vr * hr - jnp.where(edge, 0.0, vi * hi)
            ui = jnp.where(edge, vi * hi, vr * hi + vi * hr)
        else:
            gain = jax.nn.sigmoid(slope * (rr + ii) + shift)
            hr, hi = cr * gain, ci * gain
            ur, ui = vr * hr - vi * hi, vr * hi + vi * hr
        u_s[re, :] = ur.astype(BF)
        u_s[im, :] = ui.astype(BF)

    each_bin(quarter, bins)
    resynth(u_s, o_s, inv_real_ref, inv_ref, quarter)

    def finish(i):
        n = 32
        parts = recombine(o_s, slice(0, width), i, n, quarter)
        for k, part in enumerate(parts):
            rows = pl.ds(pl.multiple_of(k * quarter + i * n, n), n)
            mixed = (part + skip_ref[...] * xv[rows, :].astype(F32)).astype(BF)
            mixed_ref[rows, :] = mixed
            gated_ref[rows, :] = (qc[rows, :] * mixed.astype(F32)).astype(BF)

    loop(quarter // 32, finish)
    resid_ref[...] += mm(gated_ref[...], wo_ref[...])

    @pl.when(j == pl.num_programs(1) - 1)
    def _():
        def body(i):
            rows = rows_of(i, tile)
            n, _ = norm_stats(resid_ref[rows, :])
            second_ref[rows, :] = (n * ffn_gain_ref[...]).astype(BF)

        loop(length // tile, body)


def once(shape, index):
    return pl.BlockSpec(shape, index, pipeline_mode=pl.Buffered(1))


def mixer_specs(length, model, width):
    blocks = model // width
    row = pl.BlockSpec((None, length, model), lambda r, j, *_: (r, 0, 0))
    part = pl.BlockSpec((None, length, width), lambda r, j, *_: (r, 0, j))

    def columns(rows, offset):
        return pl.BlockSpec((rows, width), lambda r, j, *_: (0, j + offset * blocks))

    out_rows = pl.BlockSpec((width, model), lambda r, j, *_: (j, 0))
    gain = once((1, model), lambda r, j, *_: (0, 0))
    q = length // 4
    tables = [once((2 * q, q), lambda r, j, *_: (0, 0)), once((6 * q, 2 * q), lambda r, j, *_: (0, 0))]
    return blocks, row, part, columns, out_rows, gain, tables + tables


def mixer_forward(x, split, keep, norm_gain, proj_in, short_filter, cond_filter, slope, shift, skip, proj_out, ffn_gain, tables, width=256):
    rows, length, model = x.shape
    blocks, row, part, columns, out_rows, gain, table_specs = mixer_specs(length, model, width)
    one = columns(1, 0)
    shape = jax.ShapeDtypeStruct
    low, full = shape((rows, length, model), BF), shape((rows, length, model), F32)
    pad = pltpu.VMEM((length + 8, width), F32)
    flops = rows * (2 * length * model * (3 * model + model) + 2 * 3 * model * (2 * length) * length // 2)
    return pl.pallas_call(
        mixer_forward_kernel,
        out_shape=[low, low, low, low, low, low, full, low],
        grid_spec=pltpu.PrefetchScalarGridSpec(
            num_scalar_prefetch=2,
            grid=(rows, blocks),
            in_specs=[row, gain, columns(model, 0), columns(model, 1), columns(model, 2), columns(3, 0), columns(3, 1), columns(3, 0), one, one, one, out_rows, gain] + table_specs,
            out_specs=[row, part, part, part, part, part, row, row],
            scratch_shapes=[pad, pad, pad] + [pltpu.VMEM((length, width), BF)] * 2 + [
                pltpu.VMEM((2 * length, 2 * width), BF),
                pltpu.VMEM((2 * length, 2 * width), F32),
                pltpu.VMEM((2 * length, width), BF),
                pltpu.VMEM((2 * length, width), F32),
                pltpu.VMEM((length, width), F32),
            ],
        ),
        compiler_params=pltpu.CompilerParams(dimension_semantics=("arbitrary", "arbitrary"), vmem_limit_bytes=LIMIT),
        cost_estimate=pl.CostEstimate(flops=flops, bytes_accessed=rows * length * model * 20, transcendentals=rows * length * model),
        name="mixer_forward",
    )(split, keep, x, norm_gain, proj_in, proj_in, proj_in, short_filter, short_filter, cond_filter, slope, shift, skip, proj_out, ffn_gain, *tables)


def normal_cdf_pdf(x):
    z = jnp.abs(x) * ROOT_HALF
    t = 1.0 / (1.0 + 0.3275911 * z)
    e = jnp.exp(-z * z)
    poly = t * (0.127414796 + t * (-0.142248368 + t * (0.7107068705 + t * (-0.7265760135 + t * 0.5307027145))))
    tail = poly * e
    return jnp.where(x >= 0, 1.0 - tail, tail), x * e * (1.0 / math.sqrt(2.0 * math.pi))


def ffn_kernel(
    sa_ref, og_ref, sat_ref, ogt_ref, wg_ref, wu_ref, wo_ref, out_ref, back_ref, grads_ref, gs, us, ds, hid, gg, ug
):
    j = pl.program_id(0)
    tokens, model = sa_ref.shape
    tile = gs.shape[0]
    chunk = 32

    @pl.when(j == 0)
    def _():
        def body(i):
            out_ref[rows_of(i, tile), :] = jnp.zeros((tile, model), F32)
            back_ref[rows_of(i, tile), :] = jnp.zeros((tile, model), F32)

        loop(tokens // tile, body)

    def body(i):
        rows = rows_of(i, tile)
        sa = sa_ref[rows, :]
        gs[...] = mm(sa, wg_ref[...])
        us[...] = mm(sa, wu_ref[...])
        ds[...] = mm_t(og_ref[rows, :], wo_ref[...])
        for c in range(tile // chunk):
            part = slice(c * chunk, (c + 1) * chunk)
            gate, up, dh = gs[part, :], us[part, :], ds[part, :]
            cdf, xpdf = normal_cdf_pdf(gate)
            act = gate * cdf
            target = pl.ds(pl.multiple_of(i * tile + c * chunk, chunk), chunk)
            hid[target, :] = (act * up).astype(BF)
            gg[target, :] = (dh * up * (cdf + xpdf)).astype(BF)
            ug[target, :] = (dh * act).astype(BF)
        out_ref[rows, :] += mm(hid[rows, :], wo_ref[...])
        back_ref[rows, :] += mm_t(gg[rows, :], wg_ref[...]) + mm_t(ug[rows, :], wu_ref[...])

    loop(tokens // tile, body)
    grads_ref[0] = mm(sat_ref[...], gg[...]).astype(BF)
    grads_ref[1] = mm(sat_ref[...], ug[...]).astype(BF)
    grads_ref[2] = mm(ogt_ref[...], hid[...]).astype(BF)


def ffn_both(second_act, out_grad, ffn_in, ffn_out, width=512, tile=256):
    tokens, model = second_act.shape
    hidden = ffn_out.shape[0]
    blocks = hidden // width
    shape = jax.ShapeDtypeStruct
    whole = once((tokens, model), lambda j: (0, 0))
    turned = once((model, tokens), lambda j: (0, 0))
    return pl.pallas_call(
        ffn_kernel,
        out_shape=[shape((tokens, model), F32), shape((tokens, model), F32), shape((3, model, hidden), BF)],
        grid=(blocks,),
        in_specs=[
            whole, whole, turned, turned,
            pl.BlockSpec((model, width), lambda j: (0, j)),
            pl.BlockSpec((model, width), lambda j: (0, j + blocks)),
            pl.BlockSpec((width, model), lambda j: (j, 0)),
        ],
        out_specs=[whole, whole, pl.BlockSpec((3, model, width), lambda j: (0, 0, j))],
        scratch_shapes=[pltpu.VMEM((tile, width), F32)] * 3 + [pltpu.VMEM((tokens, width), BF)] * 3,
        compiler_params=pltpu.CompilerParams(dimension_semantics=("arbitrary",), vmem_limit_bytes=LIMIT),
        cost_estimate=pl.CostEstimate(flops=18 * tokens * model * hidden, bytes_accessed=tokens * model * 24 + model * hidden * 12, transcendentals=tokens * hidden),
        name="ffn_both",
    )(second_act, out_grad, second_act.T, out_grad.T, ffn_in, ffn_in, ffn_out)


def norm_back_kernel(resid_ref, sum_ref, back_ref, og_ref, gain_ref, out_ref, grad_ref, low_ref, gain_grad_ref):
    @pl.when(pl.program_id(0) == 0)
    def _():
        gain_grad_ref[...] = jnp.zeros_like(gain_grad_ref)

    tile = 64

    def body(i):
        rows = rows_of(i, tile)
        resid = resid_ref[rows, :]
        n, scale = norm_stats(resid)
        u = back_ref[rows, :]
        ug = u * gain_ref[...]
        un = u * n
        part = ug - jnp.mean(ug, axis=-1, keepdims=True) - n * jnp.mean(ug * n, axis=-1, keepdims=True)
        grad = og_ref[rows, :].astype(F32) + scale * part
        out_ref[rows, :] = (resid + sum_ref[rows, :]).astype(BF)
        grad_ref[rows, :] = grad
        low_ref[rows, :] = grad.astype(BF)
        gain_grad_ref[...] += jnp.sum(un.reshape(tile // 8, 8, un.shape[1]), axis=0)

    loop(resid_ref.shape[0] // tile, body)


def norm_back(resid, total, back, out_grad, gain, tile=512):
    tokens, model = resid.shape
    shape = jax.ShapeDtypeStruct
    block = pl.BlockSpec((tile, model), lambda i: (i, 0))
    fixed = pl.BlockSpec((8, model), lambda i: (0, 0))
    return pl.pallas_call(
        norm_back_kernel,
        out_shape=[shape((tokens, model), BF), shape((tokens, model), F32), shape((tokens, model), BF), shape((8, model), F32)],
        grid=(tokens // tile,),
        in_specs=[block, block, block, block, pl.BlockSpec((1, model), lambda i: (0, 0))],
        out_specs=[block, block, block, fixed],
        compiler_params=pltpu.CompilerParams(dimension_semantics=("arbitrary",), vmem_limit_bytes=LIMIT),
        cost_estimate=pl.CostEstimate(flops=20 * tokens * model, bytes_accessed=tokens * model * 22, transcendentals=tokens),
        name="norm_back",
    )(resid, total, back, out_grad, gain)


def eight_sum(v):
    return jnp.sum(v.reshape(v.shape[0] // 8, 8, v.shape[1]), axis=0)


def mixer_backward_kernel(
    split_ref, keep_ref, x_ref, grad_ref, low_ref, norm_gain_ref, q_ref, k_ref, v_ref, mixed_ref, wo_ref, wq_ref, wk_ref, wv_ref,
    fq_ref, fv_ref, fk_ref, slope_ref, shift_ref, skip_ref, fwd_real_ref, fwd_ref, inv_real_ref, inv_ref,
    in_grad_ref, pq_ref, pk_ref, pv_ref, gain_grad_ref, chan_ref,
    qs, ks, vs, xv, xc, xy, y_s, spec_s, u_s, o_s, acc,
):
    r, j = pl.program_id(0), pl.program_id(1)
    length, width = q_ref.shape
    quarter = length // 4
    split, keep = split_ref[r], keep_ref[r]
    tile = 64
    lanes = pl.ds(pl.multiple_of(j * width, width), width)

    @pl.when((r == 0) & (j == 0))
    def _():
        gain_grad_ref[...] = jnp.zeros_like(gain_grad_ref)
        chan_ref[...] = jnp.zeros_like(chan_ref)

    @pl.when(j == 0)
    def _():
        acc[...] = jnp.zeros_like(acc)

    for ref, source in ((qs, q_ref), (ks, k_ref), (vs, v_ref)):
        ref[0:8, :] = jnp.zeros((8, width), F32)

        def widen(i, ref=ref, source=source):
            ref[pl.ds(pl.multiple_of(8 + i * tile, 8), tile), :] = source[rows_of(i, tile), :].astype(F32)

        loop(length // tile, widen)

    o_s[0:length, 0:width] = mm_t(low_ref[...], wo_ref[...])

    def conv(i):
        t = i * tile
        rows = rows_of(i, tile)
        kept = t + lax.broadcasted_iota(jnp.int32, (tile, width), 0) < keep
        gated_grad = o_s[rows, 0:width]
        low = (gated_grad * conv_back(qs, t, tile, fq_ref, split)).astype(BF)
        xy[rows, :] = low
        value = jnp.where(kept, conv_back(vs, t, tile, fv_ref, split), 0.0).astype(BF)
        xv[rows, :] = value
        xc[rows, :] = jnp.where(kept, conv_back(ks, t, tile, fk_ref, split), 0.0).astype(BF)
        chan_ref[2, :, lanes] += eight_sum(low.astype(F32) * value.astype(F32))

    loop(length // tile, conv)
    butterfly(xv, y_s, 0, width, quarter)
    butterfly(xc, y_s, width, width, quarter)
    butterfly(xy, y_s, 2 * width, width, quarter)

    def query(i):
        rows = rows_of(i, tile)
        qs[rows, :] = o_s[rows, 0:width] * mixed_ref[rows, :].astype(F32)

    loop(length // tile, query)
    blockwise(y_s, spec_s, fwd_real_ref, fwd_ref, quarter)

    def bins(re, im, first):
        n = 16
        re, im = pl.ds(pl.multiple_of(re, n), n), pl.ds(pl.multiple_of(im, n), n)
        vr, vi = spec_s[re, 0:width], spec_s[im, 0:width]
        cr, ci = spec_s[re, width : 2 * width], spec_s[im, width : 2 * width]
        yr, yi = spec_s[re, 2 * width : 3 * width], spec_s[im, 2 * width : 3 * width]
        slope, shift = slope_ref[...], shift_ref[...]
        rr, ii = cr * cr, ci * ci
        if first:
            edge = lax.broadcasted_iota(jnp.int32, (n, width), 0) == 0
            pr, pi = jnp.where(edge, rr, rr + ii), jnp.where(edge, ii, rr + ii)
            gr, gi = jax.nn.sigmoid(slope * pr + shift), jax.nn.sigmoid(slope * pi + shift)
            ar = vr * yr + jnp.where(edge, 0.0, vi * yi)
            ai = jnp.where(edge, -vi * yi, vi * yr - vr * yi)
            br = ar * cr - jnp.where(edge, 0.0, ai * ci)
            bi = jnp.where(edge, -ai * ci, br)
            wr, wi = br * gr * (1.0 - gr), bi * gi * (1.0 - gi)
            ws = jnp.where(edge, 0.5 * (wr + wi), wr)
            wp = jnp.where(edge, 0.5 * (wr * pr + wi * pi), wr * pr)
            hr, hi = gr * cr, gi * ci
            er = hr * yr + jnp.where(edge, 0.0, hi * yi)
            ei = jnp.where(edge, hi * yi, hr * yi - hi * yr)
            dr = gr * ar + 2.0 * slope * wr * cr
            di = 2.0 * slope * wi * ci - gi * ai
        else:
            p = rr + ii
            g = jax.nn.sigmoid(slope * p + shift)
            ar, ai = vr * yr + vi * yi, vi * yr - vr * yi
            ws = (ar * cr - ai * ci) * (g * (1.0 - g))
            wp = ws * p
            hr, hi = g * cr, g * ci
            er, ei = hr * yr + hi * yi, hr * yi - hi * yr
            k = 2.0 * slope * ws
            dr, di = g * ar + k * cr, k * ci - g * ai
        chan_ref[0, :, lanes] += eight_sum(wp)
        chan_ref[1, :, lanes] += eight_sum(ws)
        u_s[re, 0:width] = er.astype(BF)
        u_s[im, 0:width] = ei.astype(BF)
        u_s[re, width : 2 * width] = dr.astype(BF)
        u_s[im, width : 2 * width] = di.astype(BF)

    each_bin(quarter, bins)
    resynth(u_s, o_s, inv_real_ref, inv_ref, quarter)

    def finish(i):
        n = 32
        value = recombine(o_s, slice(0, width), i, n, quarter)
        cond = recombine(o_s, slice(width, 2 * width), i, n, quarter)
        for k in range(4):
            rows = pl.ds(pl.multiple_of(k * quarter + i * n, n), n)
            kept = k * quarter + i * n + lax.broadcasted_iota(jnp.int32, (n, width), 0) < keep
            grad = (value[k] + skip_ref[...] * xy[rows, :].astype(F32)).astype(BF).astype(F32)
            vs[rows, :] = jnp.where(kept, grad, 0.0)
            ks[rows, :] = jnp.where(kept, cond[k].astype(BF).astype(F32), 0.0)

    loop(quarter // 32, finish)
    for ref in (qs, ks, vs):
        ref[length : length + 8, :] = jnp.zeros((8, width), F32)

    for slot, (ref, source, f_ref, out_ref) in enumerate(((qs, q_ref, fq_ref, pq_ref), (vs, v_ref, fv_ref, pv_ref), (ks, k_ref, fk_ref, pk_ref))):

        def adjoint(i, slot=slot, ref=ref, source=source, f_ref=f_ref, out_ref=out_ref):
            t = i * tile
            rows = rows_of(i, tile)
            block = ref[pl.ds(pl.multiple_of(t, tile), tile + 8), :]
            position = t + lax.broadcasted_iota(jnp.int32, (tile, width), 0)
            g0 = block[0:tile]
            g1 = jnp.where(position + 1 != split, block[1 : tile + 1], 0.0)
            g2 = jnp.where((position + 2 != split) & (position + 1 != split), block[2 : tile + 2], 0.0)
            s = source[rows, :].astype(F32)
            out_ref[rows, :] = (f_ref[0:1, :] * g0 + f_ref[1:2, :] * g1 + f_ref[2:3, :] * g2).astype(BF)
            for k, g in enumerate((g0, g1, g2)):
                chan_ref[3 + 3 * slot + k, :, lanes] += eight_sum(g * s)

        loop(length // tile, adjoint)

    acc[...] += mm_t(pq_ref[...], wq_ref[...]) + mm_t(pk_ref[...], wk_ref[...]) + mm_t(pv_ref[...], wv_ref[...])

    @pl.when(j == pl.num_programs(1) - 1)
    def _():
        def body(i):
            rows = rows_of(i, tile)
            n, scale = norm_stats(x_ref[rows, :].astype(F32))
            u = acc[rows, :]
            ug = u * norm_gain_ref[...]
            part = ug - jnp.mean(ug, axis=-1, keepdims=True) - n * jnp.mean(ug * n, axis=-1, keepdims=True)
            in_grad_ref[rows, :] = (grad_ref[rows, :] + scale * part).astype(in_grad_ref.dtype)
            gain_grad_ref[...] += eight_sum(u * n)

        loop(length // tile, body)


def mixer_backward(x, resid_grad, branch_low, split, keep, norm_gain, q, k, v, mixed, proj_out, proj_in, short_filter, cond_filter, slope, shift, skip, tables, width=256):
    rows, length, model = x.shape
    blocks, row, part, columns, out_rows, gain, table_specs = mixer_specs(length, model, width)
    one = columns(1, 0)
    shape = jax.ShapeDtypeStruct
    low = shape((rows, length, model), BF)
    pad = pltpu.VMEM((length + 8, width), F32)
    single = once((None, length, model), lambda r, j, *_: (r, 0, 0))
    flops = rows * (2 * length * model * (3 * model + model) + 2 * 5 * model * (2 * length) * length // 2)
    return pl.pallas_call(
        mixer_backward_kernel,
        out_shape=[low, low, low, low, shape((8, model), F32), shape((12, 8, model), F32)],
        grid_spec=pltpu.PrefetchScalarGridSpec(
            num_scalar_prefetch=2,
            grid=(rows, blocks),
            in_specs=[row, single, row, gain, part, part, part, part, out_rows, columns(model, 0), columns(model, 1), columns(model, 2), columns(3, 0), columns(3, 1), columns(3, 0), one, one, one] + table_specs,
            out_specs=[row, part, part, part, once((8, model), lambda r, j, *_: (0, 0)), once((12, 8, model), lambda r, j, *_: (0, 0, 0))],
            scratch_shapes=[pad, pad, pad] + [pltpu.VMEM((length, width), BF)] * 3 + [
                pltpu.VMEM((2 * length, 3 * width), BF),
                pltpu.VMEM((2 * length, 3 * width), F32),
                pltpu.VMEM((2 * length, 2 * width), BF),
                pltpu.VMEM((2 * length, 2 * width), F32),
                pltpu.VMEM((length, model), F32),
            ],
        ),
        compiler_params=pltpu.CompilerParams(dimension_semantics=("arbitrary", "arbitrary"), vmem_limit_bytes=LIMIT),
        cost_estimate=pl.CostEstimate(flops=flops, bytes_accessed=rows * length * model * 26, transcendentals=rows * length * model),
        name="mixer_backward",
    )(split, keep, x, resid_grad, branch_low, norm_gain, q, k, v, mixed, proj_out, proj_in, proj_in, proj_in, short_filter, short_filter, cond_filter, slope, shift, skip, *tables)


def layer_rows(x, split, keep, out_grad, p, tables):
    rows, length, model = x.shape
    norm_gain, proj_in, short_filter, cond_filter, slope, shift, skip, proj_out, ffn_gain, ffn_in, ffn_out = p
    lift = lambda a: a.reshape(1, -1)
    first, q, k, v, mixed, gated, resid, second = mixer_forward(
        x, split, keep, lift(norm_gain), proj_in, short_filter, cond_filter, lift(slope), lift(shift), lift(skip), proj_out, lift(ffn_gain), tables
    )
    tokens = rows * length
    flat = lambda a: a.reshape(tokens, model)
    total, back, ffn_grads = ffn_both(flat(second), flat(out_grad), ffn_in, ffn_out)
    output, resid_grad, branch_low, ffn_gain_part = norm_back(flat(resid), total, back, flat(out_grad), lift(ffn_gain))
    shaped = lambda a: a.reshape(rows, length, model)
    input_grad, pq, pk, pv, norm_gain_part, chan = mixer_backward(
        x, shaped(resid_grad), shaped(branch_low), split, keep, lift(norm_gain), q, k, v, mixed, proj_out, proj_in, short_filter, cond_filter, lift(slope), lift(shift), lift(skip), tables
    )
    turn = lambda a, b: lax.dot_general(flat(a), flat(b), (((0,), (0,)), ((), ())), preferred_element_type=F32).astype(BF)
    out_grads = turn(gated, branch_low)
    in_grads = [turn(first, g) for g in (pq, pk, pv)]
    small = jnp.sum(jnp.concatenate([ffn_gain_part[None], norm_gain_part[None], chan], 0), axis=1)
    return shaped(output), input_grad, ffn_grads, out_grads, in_grads, small


def per_device_rows(inputs, split_point, keep_mask, norm_gain, proj_in, short_filter, cond_filter, spec_slope, spec_shift, skip_gain, proj_out, ffn_gain, ffn_in, ffn_out, out_grad):
    local_rows, local_len, model = inputs.shape
    count = lax.axis_size("seq")
    own = local_rows // count
    first_row = lax.axis_index("seq") * own
    gather = functools.partial(lax.all_to_all, axis_name="seq", split_axis=0, concat_axis=1, tiled=True)
    scatter = functools.partial(lax.all_to_all, axis_name="seq", split_axis=1, concat_axis=0, tiled=True)
    x = gather(inputs)
    whole_grad = gather(out_grad)
    keep = lax.dynamic_slice_in_dim(lax.psum(jnp.sum(keep_mask, axis=1), "seq"), first_row, own)
    split = lax.dynamic_slice_in_dim(split_point, first_row, own)
    params = (norm_gain, proj_in, short_filter, cond_filter, spec_slope, spec_shift, skip_gain, proj_out, ffn_gain, ffn_in, ffn_out)
    length = local_len * count
    tables = spectral_tables(length, lax.axis_index("seq") * (2 * length))
    output, input_grad, ffn_grads, out_grads, in_grads, small = layer_rows(x, split, keep, whole_grad, params, tables)
    output = scatter(output)
    input_grad = scatter(input_grad).astype(F32)
    ffn_share = lax.psum_scatter(ffn_grads, "rows", scatter_dimension=1, tiled=True)
    ffn_share = lax.psum(ffn_share, "seq").astype(F32)
    mix_share = lax.psum_scatter(jnp.concatenate(in_grads + [out_grads], axis=1), "rows", scatter_dimension=0, tiled=True)
    mix_share = lax.psum(mix_share, "seq").astype(F32)
    small = lax.psum(small, ("rows", "seq"))
    scale = 1.0 / length
    return (
        output,
        input_grad,
        small[1],
        mix_share[:, : 3 * model],
        jnp.concatenate([small[5:8], small[8:11]], axis=1),
        small[11:14],
        small[2] * scale,
        small[3] * scale,
        small[4],
        mix_share[:, 3 * model :],
        small[0],
        jnp.concatenate([ffn_share[0], ffn_share[1]], axis=1),
        ffn_share[2].T,
    )


PRECISE = lax.Precision.HIGH


def passed_along(value, axis, steps):
    count = lax.axis_size(axis)
    leading, last = (max(0, -steps), min(count, count - steps))
    return lax.ppermute(value, axis, [(source, source + steps) for source in range(leading, last)])


def layer_norm(values, scaling):
    center = values - jnp.mean(values, axis=-1, keepdims=True)
    spread = jnp.mean(center * center, axis=-1, keepdims=True)
    return center * lax.rsqrt(spread + EPSILON) * scaling


def conv_three(extended, weights, same_one, same_two):
    length = extended.shape[1] - 2
    return (
        weights[0] * extended[:, 2:]
        + weights[1] * extended[:, 1 : length + 1] * same_one
        + weights[2] * extended[:, :length] * same_two
    )


def dft_tables(seq_length):
    table_shape = (seq_length + 1, seq_length)
    product = lax.broadcasted_iota(jnp.int32, table_shape, 0) * lax.broadcasted_iota(
        jnp.int32, table_shape, 1
    )
    angles = (product % (2 * seq_length)).astype(jnp.float32) * (math.pi / seq_length)
    freq = lax.broadcasted_iota(jnp.int32, (seq_length + 1, 1), 0)
    edge = jnp.logical_or(freq == 0, freq == seq_length)
    weights = jnp.where(edge, 1.0, 2.0).astype(jnp.float32) / (2.0 * seq_length)
    return (jnp.cos(angles), jnp.sin(angles), weights)


def analyze(values, conds, cos_table, sin_table):
    value_real = jnp.einsum("ft,ktd->kfd", cos_table, values, precision=PRECISE)
    value_imag = -jnp.einsum("ft,ktd->kfd", sin_table, values, precision=PRECISE)
    cond_real = jnp.einsum("ft,ktd->kfd", cos_table, conds, precision=PRECISE)
    cond_imag = -jnp.einsum("ft,ktd->kfd", sin_table, conds, precision=PRECISE)
    return (value_real, value_imag, cond_real, cond_imag)


def synth(
    value_real,
    value_imag,
    cond_real,
    cond_imag,
    values,
    slopes,
    shifts,
    skip_gains,
    cos_table,
    sin_table,
    freq_weights,
):
    factor = jax.nn.sigmoid(slopes * (cond_real * cond_real + cond_imag * cond_imag) + shifts)
    filter_real = cond_real * factor
    filter_imag = cond_imag * factor
    prod_real = (value_real * filter_real - value_imag * filter_imag) * freq_weights
    prod_imag = (value_real * filter_imag + value_imag * filter_real) * freq_weights
    mixed_out = jnp.einsum("ft,kfd->ktd", cos_table, prod_real, precision=PRECISE) - jnp.einsum(
        "ft,kfd->ktd", sin_table, prod_imag, precision=PRECISE
    )
    return mixed_out + skip_gains * values


def times_transpose(left, right):
    return lax.dot_general(
        left, right, (((1,), (1,)), ((), ())), preferred_element_type=jnp.float32
    )


def transpose_times(left, right):
    return lax.dot_general(
        left, right, (((0,), (0,)), ((), ())), preferred_element_type=jnp.float32
    )


def per_device(
    inputs,
    split_point,
    keep_mask,
    norm_gain,
    proj_in,
    short_filter,
    cond_filter,
    spec_slope,
    spec_shift,
    skip_gain,
    proj_out,
    ffn_gain,
    ffn_in,
    ffn_out,
    out_grad,
):
    local_rows, local_len, model_width = inputs.shape
    hidden_width = ffn_out.shape[0]
    seq_count = lax.axis_size("seq")
    seq_index = lax.axis_index("seq")
    full_len = local_len * seq_count
    chan_width = model_width // seq_count
    token_count = local_rows * local_len
    positions = seq_index * local_len + lax.broadcasted_iota(jnp.int32, (local_rows, local_len), 1)
    splits = split_point[:, None]
    segment = positions >= splits
    same_one = (segment == (positions - 1 >= splits)).astype(jnp.float32)[:, :, None]
    same_two = (segment == (positions - 2 >= splits)).astype(jnp.float32)[:, :, None]
    keep_float = keep_mask.astype(jnp.float32)[:, :, None]
    flat_in = inputs.reshape(token_count, model_width).astype(jnp.float32)
    normed_one, norm_one_back = jax.vjp(layer_norm, flat_in, norm_gain)
    first_act = normed_one.astype(jnp.bfloat16)
    projected = jnp.dot(first_act, proj_in, preferred_element_type=jnp.float32).astype(jnp.bfloat16)
    proj_rows = projected.reshape(local_rows, local_len, 3 * model_width)
    edge_values = passed_along(proj_rows[:, local_len - 2 :, :], "seq", 1)
    extended = jnp.concatenate([edge_values, proj_rows], axis=1).astype(jnp.float32)

    def mixer_local(ext_values, short_weights, cond_weights):
        query_value = jnp.concatenate(
            [ext_values[:, :, :model_width], ext_values[:, :, 2 * model_width :]], axis=2
        )
        conv_both = conv_three(query_value, short_weights, same_one, same_two)
        cond_conv = conv_three(
            ext_values[:, :, model_width : 2 * model_width], cond_weights, same_one, same_two
        )
        return (
            conv_both[:, :, :model_width],
            conv_both[:, :, model_width:] * keep_float,
            cond_conv * keep_float,
        )

    (query_conv, value_masked, cond_masked), mixer_back = jax.vjp(
        mixer_local, extended, short_filter, cond_filter
    )
    value_low = value_masked.astype(jnp.bfloat16)
    cond_low = cond_masked.astype(jnp.bfloat16)
    slope_part = lax.dynamic_slice_in_dim(spec_slope, seq_index * chan_width, chan_width)
    shift_part = lax.dynamic_slice_in_dim(spec_shift, seq_index * chan_width, chan_width)
    skip_part = lax.dynamic_slice_in_dim(skip_gain, seq_index * chan_width, chan_width)
    cos_table, sin_table, freq_weights = dft_tables(full_len)

    def synth_local(
        value_real, value_imag, cond_real, cond_imag, values, slopes, shifts, skip_gains
    ):
        return synth(
            value_real,
            value_imag,
            cond_real,
            cond_imag,
            values,
            slopes,
            shifts,
            skip_gains,
            cos_table,
            sin_table,
            freq_weights,
        )

    value_chan = lax.all_to_all(value_low, "seq", split_axis=2, concat_axis=1, tiled=True)
    cond_chan = lax.all_to_all(cond_low, "seq", split_axis=2, concat_axis=1, tiled=True)
    value_float = value_chan.astype(jnp.float32)
    spectra = analyze(value_float, cond_chan.astype(jnp.float32), cos_table, sin_table)
    mixed_chan = synth_local(
        spectra[0],
        spectra[1],
        spectra[2],
        spectra[3],
        value_float,
        slope_part,
        shift_part,
        skip_part,
    ).astype(jnp.bfloat16)
    mixed_home = lax.all_to_all(mixed_chan, "seq", split_axis=1, concat_axis=2, tiled=True)
    mixed_float = mixed_home.astype(jnp.float32)
    gated = (query_conv * mixed_float).astype(jnp.bfloat16).reshape(token_count, model_width)
    branch = jnp.dot(gated, proj_out, preferred_element_type=jnp.float32)
    resid = flat_in + branch
    normed_two, norm_two_back = jax.vjp(layer_norm, resid, ffn_gain)
    second_act = normed_two.astype(jnp.bfloat16)
    gate_up = jnp.dot(second_act, ffn_in, preferred_element_type=jnp.float32)

    def glu_local(both_parts):
        return (
            jax.nn.gelu(both_parts[:, :hidden_width], approximate=False)
            * both_parts[:, hidden_width:]
        )

    hidden, glu_back = jax.vjp(glu_local, gate_up)
    hidden_low = hidden.astype(jnp.bfloat16)
    result = resid + jnp.dot(hidden_low, ffn_out, preferred_element_type=jnp.float32)
    output = result.astype(jnp.bfloat16).reshape(local_rows, local_len, model_width)
    flat_grad = out_grad.reshape(token_count, model_width)
    hidden_grad = times_transpose(flat_grad, ffn_out)
    (gate_up_grad,) = glu_back(hidden_grad)
    gate_up_low = gate_up_grad.astype(jnp.bfloat16)
    second_grad = times_transpose(gate_up_low, ffn_in)
    resid_part, ffn_gain_part = norm_two_back(second_grad)
    resid_grad = flat_grad.astype(jnp.float32) + resid_part
    branch_low = resid_grad.astype(jnp.bfloat16)
    gated_grad = times_transpose(branch_low, proj_out).reshape(local_rows, local_len, model_width)
    query_grad = gated_grad * mixed_float
    mixed_grad = (gated_grad * query_conv).astype(jnp.bfloat16)
    grad_chan = lax.all_to_all(mixed_grad, "seq", split_axis=2, concat_axis=1, tiled=True)
    grad_float = grad_chan.astype(jnp.float32)
    item_count = grad_chan.shape[0]
    slope_items = jnp.broadcast_to(slope_part, (item_count, 1, chan_width))
    shift_items = jnp.broadcast_to(shift_part, (item_count, 1, chan_width))
    skip_items = jnp.broadcast_to(skip_part, (item_count, 1, chan_width))
    value_float = value_chan.astype(jnp.float32)

    def spectral(values, conds, slopes, shifts, skip_gains):
        spectra = analyze(values, conds, cos_table, sin_table)
        return synth_local(
            spectra[0], spectra[1], spectra[2], spectra[3], values, slopes, shifts, skip_gains
        )

    unused, pull = jax.vjp(
        spectral, value_float, cond_chan.astype(jnp.float32), slope_items, shift_items, skip_items
    )
    value_back, cond_back, slope_rows, shift_rows, skip_rows = pull(grad_float)
    value_grad, cond_grad = (
        lax.all_to_all(
            value_back.astype(jnp.bfloat16), "seq", split_axis=1, concat_axis=2, tiled=True
        ),
        lax.all_to_all(
            cond_back.astype(jnp.bfloat16), "seq", split_axis=1, concat_axis=2, tiled=True
        ),
    )
    start_chan = (seq_index * chan_width,)
    empty_width = jnp.zeros((model_width,), jnp.float32)
    slope_full = lax.dynamic_update_slice(empty_width, jnp.sum(slope_rows, axis=(0, 1)), start_chan)
    shift_full = lax.dynamic_update_slice(empty_width, jnp.sum(shift_rows, axis=(0, 1)), start_chan)
    skip_full = lax.dynamic_update_slice(empty_width, jnp.sum(skip_rows, axis=(0, 1)), start_chan)
    ext_grad, short_grad, cond_weight_grad = mixer_back(
        (query_grad, value_grad.astype(jnp.float32), cond_grad.astype(jnp.float32))
    )
    incoming = passed_along(ext_grad[:, :2, :].astype(jnp.bfloat16), "seq", -1).astype(jnp.float32)
    proj_grad = ext_grad[:, 2:, :] + jnp.pad(incoming, ((0, 0), (local_len - 2, 0), (0, 0)))
    proj_low = proj_grad.astype(jnp.bfloat16).reshape(token_count, 3 * model_width)
    first_grad = times_transpose(proj_low, proj_in)
    input_part, norm_gain_part = norm_one_back(first_grad)
    input_grad = (resid_grad + input_part).reshape(local_rows, local_len, model_width)
    share = lax.psum_scatter(
        jnp.concatenate(
            [
                transpose_times(first_act, proj_low),
                transpose_times(gated, branch_low),
                transpose_times(second_act, gate_up_low),
                transpose_times(flat_grad, hidden_low),
            ],
            axis=1,
        ).astype(jnp.bfloat16),
        "rows",
        scatter_dimension=0,
        tiled=True,
    )
    summed = lax.psum(share, "seq").astype(jnp.float32)
    small_sums = lax.psum(
        (
            norm_gain_part,
            short_grad,
            cond_weight_grad,
            slope_full,
            shift_full,
            skip_full,
            ffn_gain_part,
        ),
        ("rows", "seq"),
    )
    proj_in_grad = summed[:, : 3 * model_width]
    proj_out_grad = summed[:, 3 * model_width : 4 * model_width]
    ffn_in_grad = summed[:, 4 * model_width : 4 * model_width + 2 * hidden_width]
    ffn_out_grad = jnp.transpose(summed[:, 4 * model_width + 2 * hidden_width :])
    return (
        output,
        input_grad,
        small_sums[0],
        proj_in_grad,
        small_sums[1],
        small_sums[2],
        small_sums[3],
        small_sums[4],
        small_sums[5],
        proj_out_grad,
        small_sums[6],
        ffn_in_grad,
        ffn_out_grad,
    )


def per_device_any(*args):
    rows, width = args[0].shape[0], args[0].shape[2]
    even = rows % lax.axis_size("seq") == 0 and width % 256 == 0
    return (per_device_rows if even else per_device)(*args)


def solution(mesh):
    in_specs = (
        P("rows", "seq", None),
        P("rows"),
        P("rows", "seq"),
        P(),
        P(),
        P(),
        P(),
        P(),
        P(),
        P(),
        P(),
        P(),
        P(),
        P(),
        P("rows", "seq", None),
    )
    out_specs = (
        P("rows", "seq", None),
        P("rows", "seq", None),
        P(),
        P("rows", None),
        P(),
        P(),
        P(),
        P(),
        P(),
        P("rows", None),
        P(),
        P("rows", None),
        P(None, "rows"),
    )
    return jax.shard_map(
        per_device_any, mesh=mesh, in_specs=in_specs, out_specs=out_specs, check_vma=False
    )
```

```python
import functools
import math

import jax
import jax.numpy as jnp
from jax import lax
from jax.experimental import pallas as pl
from jax.experimental.pallas import tpu as pltpu
from jax.sharding import PartitionSpec as P

EPSILON = 1e-05
BF = jnp.bfloat16
F32 = jnp.float32
ROOT_HALF = math.sqrt(0.5)
LIMIT = 67043328


def mm(a, b):
    return lax.dot_general(a, b, (((1,), (0,)), ((), ())), preferred_element_type=F32)


def mm_t(a, b):
    return lax.dot_general(a, b, (((1,), (1,)), ((), ())), preferred_element_type=F32)


def spectral_tables(length, offset):
    quarter = length // 4
    two_n = 2 * length
    m = lax.broadcasted_iota(jnp.int32, (quarter, quarter), 0)
    s = lax.broadcasted_iota(jnp.int32, (quarter, quarter), 1)

    def cos_sin(freq):
        angle = ((freq * s + offset) % two_n).astype(F32) * (2.0 * math.pi / two_n)
        return jnp.cos(angle), jnp.sin(angle)

    half = quarter // 2
    forward, inverse = [], []
    for r in (1, 2, 3):
        c, sn = cos_sin(8 * m + r)
        forward.append(jnp.concatenate([jnp.concatenate([c, sn], 1), jnp.concatenate([-sn, c], 1)], 0))
        inverse.append(forward[-1].T * (2.0 / two_n))
    row = m % half
    low = m < half
    c, sn = cos_sin(8 * jnp.where(m == half, half, row))
    zero = jnp.where(low | (m == half), c, -sn)
    c4, sn4 = cos_sin(8 * row + 4)
    four = jnp.where(low, c4, -sn4)
    edge = jnp.where((m == 0) | (m == half), 1.0, 2.0) / two_n
    fwd_real = jnp.concatenate([zero, four], 0)
    inv_real = jnp.concatenate([(zero * edge).T, four.T * (2.0 / two_n)], 0)
    return (
        fwd_real.astype(BF),
        jnp.concatenate(forward, 0).astype(BF),
        inv_real.astype(BF),
        jnp.concatenate(inverse, 0).astype(BF),
    )


def loop(count, body):
    lax.fori_loop(0, count, lambda i, c: (body(i), c)[1], 0)


def rows_of(i, size):
    return pl.ds(pl.multiple_of(i * size, size), size)


def norm_stats(v):
    center = v - jnp.mean(v, axis=-1, keepdims=True)
    scale = lax.rsqrt(jnp.mean(center * center, axis=-1, keepdims=True) + EPSILON)
    return center * scale, scale


def same_masks(position, split):
    same_one = position != split
    return same_one, same_one & (position != split + 1)


def butterfly(x_ref, y_ref, lane, width, quarter):
    tile = 32
    lanes = slice(lane, lane + width)

    def body(i):
        x0, x1, x2, x3 = [
            x_ref[pl.ds(pl.multiple_of(q * quarter + i * tile, tile), tile), :].astype(F32) for q in range(4)
        ]
        a, b, c, d = x0 + x2, x1 + x3, x0 - x2, x1 - x3
        sd, sb = d * ROOT_HALF, b * ROOT_HALF
        out = (a + b, a - b, x0 + sd, -x2 - sb, c, -d, x0 - sd, x2 - sb)
        for k, value in enumerate(out):
            y_ref[pl.ds(pl.multiple_of(k * quarter + i * tile, tile), tile), lanes] = value.astype(BF)

    loop(quarter // tile, body)


def blockwise(y_ref, spec_ref, fwd_real_ref, fwd_ref, quarter):
    q = quarter
    for k in range(2):
        spec_ref[k * q : (k + 1) * q, :] = mm(fwd_real_ref[k * q : (k + 1) * q, :], y_ref[k * q : (k + 1) * q, :])
    for k in range(3):
        spec_ref[2 * q + 2 * k * q : 2 * q + 2 * (k + 1) * q, :] = mm(
            fwd_ref[2 * k * q : 2 * (k + 1) * q, :], y_ref[2 * q + 2 * k * q : 2 * q + 2 * (k + 1) * q, :]
        )


def resynth(u_ref, out_ref, inv_real_ref, inv_ref, quarter):
    blockwise(u_ref, out_ref, inv_real_ref, inv_ref, quarter)


def each_bin(quarter, body, tile=16):
    half = quarter // 2
    body(0, half, True)

    def run(base, span, skip):
        def step(i):
            start = base + (i + skip) * tile
            body(start, start + span, False)

        loop(span // tile - skip, step)

    run(0, half, 1)
    run(quarter, half, 0)
    for k in range(3):
        run(2 * quarter + 2 * k * quarter, quarter, 0)


def recombine(o_ref, lanes, i, tile, quarter):
    def part(k):
        return o_ref[pl.ds(pl.multiple_of(k * quarter + i * tile, tile), tile), lanes]

    u0, u4, a1, b1, a2, b2, a3, b3 = [part(k) for k in range(8)]
    even, odd = u0 + u4, u0 - u4
    return (
        even + a1 + a2 + a3,
        odd + (a1 - b1 - a3 - b3) * ROOT_HALF - b2,
        even - b1 - a2 + b3,
        odd + (a3 - b3 - a1 - b1) * ROOT_HALF + b2,
    )


def conv_back(ref, t, tile, weights, split):
    block = ref[pl.ds(pl.multiple_of(t, tile), tile + 8), :]
    width = block.shape[1]
    position = t + lax.broadcasted_iota(jnp.int32, (tile, width), 0)
    one, two = same_masks(position, split)
    return (
        weights[0:1, :] * block[8 : tile + 8]
        + jnp.where(one, weights[1:2, :] * block[7 : tile + 7], 0.0)
        + jnp.where(two, weights[2:3, :] * block[6 : tile + 6], 0.0)
    )


def mixer_forward_kernel(
    split_ref, keep_ref, x_ref, norm_gain_ref, wq_ref, wk_ref, wv_ref, fq_ref, fv_ref, fk_ref, slope_ref, shift_ref,
    skip_ref, wo_ref, ffn_gain_ref, fwd_real_ref, fwd_ref, inv_real_ref, inv_ref,
    first_ref, q_ref, k_ref, v_ref, mixed_ref, gated_ref, resid_ref, second_ref,
    qs, ks, vs, xv, xc, y_s, spec_s, u_s, o_s, qc,
):
    r, j = pl.program_id(0), pl.program_id(1)
    length, width = q_ref.shape
    quarter = length // 4
    split, keep = split_ref[r], keep_ref[r]
    tile = 64

    @pl.when(j == 0)
    def _():
        def body(i):
            rows = rows_of(i, tile)
            v = x_ref[rows, :].astype(F32)
            n, _ = norm_stats(v)
            first_ref[rows, :] = (n * norm_gain_ref[...]).astype(BF)
            resid_ref[rows, :] = v

        loop(length // tile, body)
        for ref in (qs, ks, vs):
            ref[0:8, :] = jnp.zeros((8, width), F32)

    for w_ref, out_ref, ref in ((wq_ref, q_ref, qs), (wk_ref, k_ref, ks), (wv_ref, v_ref, vs)):
        value = mm(first_ref[...], w_ref[...]).astype(BF)
        out_ref[...] = value
        ref[8 : 8 + length, :] = value.astype(F32)

    def conv(i):
        t = i * tile
        rows = rows_of(i, tile)
        kept = t + lax.broadcasted_iota(jnp.int32, (tile, width), 0) < keep
        qc[rows, :] = conv_back(qs, t, tile, fq_ref, split)
        xv[rows, :] = jnp.where(kept, conv_back(vs, t, tile, fv_ref, split), 0.0).astype(BF)
        xc[rows, :] = jnp.where(kept, conv_back(ks, t, tile, fk_ref, split), 0.0).astype(BF)

    loop(length // tile, conv)
    butterfly(xv, y_s, 0, width, quarter)
    butterfly(xc, y_s, width, width, quarter)
    blockwise(y_s, spec_s, fwd_real_ref, fwd_ref, quarter)

    def bins(re, im, first):
        n = 16
        re, im = pl.ds(pl.multiple_of(re, n), n), pl.ds(pl.multiple_of(im, n), n)
        vr, vi = spec_s[re, 0:width], spec_s[im, 0:width]
        cr, ci = spec_s[re, width : 2 * width], spec_s[im, width : 2 * width]
        slope, shift = slope_ref[...], shift_ref[...]
        rr, ii = cr * cr, ci * ci
        if first:
            edge = lax.broadcasted_iota(jnp.int32, (n, width), 0) == 0
            hr = cr * jax.nn.sigmoid(slope * jnp.where(edge, rr, rr + ii) + shift)
            hi = ci * jax.nn.sigmoid(slope * jnp.where(edge, ii, rr + ii) + shift)
            ur = vr * hr - jnp.where(edge, 0.0, vi * hi)
            ui = jnp.where(edge, vi * hi, vr * hi + vi * hr)
        else:
            gain = jax.nn.sigmoid(slope * (rr + ii) + shift)
            hr, hi = cr * gain, ci * gain
            ur, ui = vr * hr - vi * hi, vr * hi + vi * hr
        u_s[re, :] = ur.astype(BF)
        u_s[im, :] = ui.astype(BF)

    each_bin(quarter, bins)
    resynth(u_s, o_s, inv_real_ref, inv_ref, quarter)

    def finish(i):
        n = 32
        parts = recombine(o_s, slice(0, width), i, n, quarter)
        for k, part in enumerate(parts):
            rows = pl.ds(pl.multiple_of(k * quarter + i * n, n), n)
            mixed = (part + skip_ref[...] * xv[rows, :].astype(F32)).astype(BF)
            mixed_ref[rows, :] = mixed
            gated_ref[rows, :] = (qc[rows, :] * mixed.astype(F32)).astype(BF)

    loop(quarter // 32, finish)
    resid_ref[...] += mm(gated_ref[...], wo_ref[...])

    @pl.when(j == pl.num_programs(1) - 1)
    def _():
        def body(i):
            rows = rows_of(i, tile)
            n, _ = norm_stats(resid_ref[rows, :])
            second_ref[rows, :] = (n * ffn_gain_ref[...]).astype(BF)

        loop(length // tile, body)


def once(shape, index):
    return pl.BlockSpec(shape, index, pipeline_mode=pl.Buffered(1))


def mixer_specs(length, model, width):
    blocks = model // width
    row = pl.BlockSpec((None, length, model), lambda r, j, *_: (r, 0, 0))
    part = pl.BlockSpec((None, length, width), lambda r, j, *_: (r, 0, j))

    def columns(rows, offset):
        return pl.BlockSpec((rows, width), lambda r, j, *_: (0, j + offset * blocks))

    out_rows = pl.BlockSpec((width, model), lambda r, j, *_: (j, 0))
    gain = once((1, model), lambda r, j, *_: (0, 0))
    q = length // 4
    tables = [once((2 * q, q), lambda r, j, *_: (0, 0)), once((6 * q, 2 * q), lambda r, j, *_: (0, 0))]
    return blocks, row, part, columns, out_rows, gain, tables + tables


def mixer_forward(x, split, keep, norm_gain, proj_in, short_filter, cond_filter, slope, shift, skip, proj_out, ffn_gain, tables, width=256):
    rows, length, model = x.shape
    blocks, row, part, columns, out_rows, gain, table_specs = mixer_specs(length, model, width)
    one = columns(1, 0)
    shape = jax.ShapeDtypeStruct
    low, full = shape((rows, length, model), BF), shape((rows, length, model), F32)
    pad = pltpu.VMEM((length + 8, width), F32)
    flops = rows * (2 * length * model * (3 * model + model) + 2 * 3 * model * (2 * length) * length // 2)
    return pl.pallas_call(
        mixer_forward_kernel,
        out_shape=[low, low, low, low, low, low, full, low],
        grid_spec=pltpu.PrefetchScalarGridSpec(
            num_scalar_prefetch=2,
            grid=(rows, blocks),
            in_specs=[row, gain, columns(model, 0), columns(model, 1), columns(model, 2), columns(3, 0), columns(3, 1), columns(3, 0), one, one, one, out_rows, gain] + table_specs,
            out_specs=[row, part, part, part, part, part, row, row],
            scratch_shapes=[pad, pad, pad] + [pltpu.VMEM((length, width), BF)] * 2 + [
                pltpu.VMEM((2 * length, 2 * width), BF),
                pltpu.VMEM((2 * length, 2 * width), F32),
                pltpu.VMEM((2 * length, width), BF),
                pltpu.VMEM((2 * length, width), F32),
                pltpu.VMEM((length, width), F32),
            ],
        ),
        compiler_params=pltpu.CompilerParams(dimension_semantics=("arbitrary", "arbitrary"), vmem_limit_bytes=LIMIT),
        cost_estimate=pl.CostEstimate(flops=flops, bytes_accessed=rows * length * model * 20, transcendentals=rows * length * model),
        name="mixer_forward",
    )(split, keep, x, norm_gain, proj_in, proj_in, proj_in, short_filter, short_filter, cond_filter, slope, shift, skip, proj_out, ffn_gain, *tables)


def normal_cdf_pdf(x):
    z = jnp.abs(x) * ROOT_HALF
    t = 1.0 / (1.0 + 0.3275911 * z)
    e = jnp.exp(-z * z)
    poly = t * (0.127414796 + t * (-0.142248368 + t * (0.7107068705 + t * (-0.7265760135 + t * 0.5307027145))))
    tail = poly * e
    return jnp.where(x >= 0, 1.0 - tail, tail), x * e * (1.0 / math.sqrt(2.0 * math.pi))


def ffn_kernel(
    sa_ref, og_ref, sat_ref, ogt_ref, wg_ref, wu_ref, wo_ref, out_ref, back_ref, grads_ref, gs, us, ds, hid, gg, ug
):
    j = pl.program_id(0)
    tokens, model = sa_ref.shape
    tile = gs.shape[0]
    chunk = 32

    @pl.when(j == 0)
    def _():
        def body(i):
            out_ref[rows_of(i, tile), :] = jnp.zeros((tile, model), F32)
            back_ref[rows_of(i, tile), :] = jnp.zeros((tile, model), F32)

        loop(tokens // tile, body)

    def body(i):
        rows = rows_of(i, tile)
        sa = sa_ref[rows, :]
        gs[...] = mm(sa, wg_ref[...])
        us[...] = mm(sa, wu_ref[...])
        ds[...] = mm_t(og_ref[rows, :], wo_ref[...])
        for c in range(tile // chunk):
            part = slice(c * chunk, (c + 1) * chunk)
            gate, up, dh = gs[part, :], us[part, :], ds[part, :]
            cdf, xpdf = normal_cdf_pdf(gate)
            act = gate * cdf
            target = pl.ds(pl.multiple_of(i * tile + c * chunk, chunk), chunk)
            hid[target, :] = (act * up).astype(BF)
            gg[target, :] = (dh * up * (cdf + xpdf)).astype(BF)
            ug[target, :] = (dh * act).astype(BF)
        out_ref[rows, :] += mm(hid[rows, :], wo_ref[...])
        back_ref[rows, :] += mm_t(gg[rows, :], wg_ref[...]) + mm_t(ug[rows, :], wu_ref[...])

    loop(tokens // tile, body)
    grads_ref[0] = mm(sat_ref[...], gg[...]).astype(BF)
    grads_ref[1] = mm(sat_ref[...], ug[...]).astype(BF)
    grads_ref[2] = mm(ogt_ref[...], hid[...]).astype(BF)


def ffn_both(second_act, out_grad, second_turned, grad_turned, ffn_in, ffn_out, piece, pieces, width=512, tile=256):
    tokens, model = second_act.shape
    total_blocks = ffn_out.shape[0] // width
    blocks = total_blocks // pieces
    first = piece * blocks
    hidden = blocks * width
    shape = jax.ShapeDtypeStruct
    whole = once((tokens, model), lambda j: (0, 0))
    turned = once((model, tokens), lambda j: (0, 0))
    return pl.pallas_call(
        ffn_kernel,
        out_shape=[shape((tokens, model), F32), shape((tokens, model), F32), shape((3, model, hidden), BF)],
        grid=(blocks,),
        in_specs=[
            whole, whole, turned, turned,
            pl.BlockSpec((model, width), lambda j: (0, j + first)),
            pl.BlockSpec((model, width), lambda j: (0, j + first + total_blocks)),
            pl.BlockSpec((width, model), lambda j: (j + first, 0)),
        ],
        out_specs=[whole, whole, pl.BlockSpec((3, model, width), lambda j: (0, 0, j))],
        scratch_shapes=[pltpu.VMEM((tile, width), F32)] * 3 + [pltpu.VMEM((tokens, width), BF)] * 3,
        compiler_params=pltpu.CompilerParams(dimension_semantics=("arbitrary",), vmem_limit_bytes=LIMIT),
        cost_estimate=pl.CostEstimate(flops=18 * tokens * model * hidden, bytes_accessed=tokens * model * 24 + model * hidden * 12, transcendentals=tokens * hidden),
        name="ffn_both",
    )(second_act, out_grad, second_turned, grad_turned, ffn_in, ffn_in, ffn_out)


def norm_back_kernel(pieces, resid_ref, *refs):
    sum_refs, back_refs = refs[:pieces], refs[pieces : 2 * pieces]
    og_ref, gain_ref, out_ref, grad_ref, low_ref, gain_grad_ref = refs[2 * pieces :]

    @pl.when(pl.program_id(0) == 0)
    def _():
        gain_grad_ref[...] = jnp.zeros_like(gain_grad_ref)

    tile = 64

    def body(i):
        rows = rows_of(i, tile)
        resid = resid_ref[rows, :]
        n, scale = norm_stats(resid)
        u = sum(ref[rows, :] for ref in back_refs)
        ug = u * gain_ref[...]
        un = u * n
        part = ug - jnp.mean(ug, axis=-1, keepdims=True) - n * jnp.mean(ug * n, axis=-1, keepdims=True)
        grad = og_ref[rows, :].astype(F32) + scale * part
        out_ref[rows, :] = (resid + sum(ref[rows, :] for ref in sum_refs)).astype(BF)
        grad_ref[rows, :] = grad
        low_ref[rows, :] = grad.astype(BF)
        gain_grad_ref[...] += jnp.sum(un.reshape(tile // 8, 8, un.shape[1]), axis=0)

    loop(resid_ref.shape[0] // tile, body)


def norm_back(resid, totals, backs, out_grad, gain, tile=512):
    tokens, model = resid.shape
    pieces = len(totals)
    shape = jax.ShapeDtypeStruct
    block = pl.BlockSpec((tile, model), lambda i: (i, 0))
    fixed = pl.BlockSpec((8, model), lambda i: (0, 0))
    return pl.pallas_call(
        functools.partial(norm_back_kernel, pieces),
        out_shape=[shape((tokens, model), BF), shape((tokens, model), F32), shape((tokens, model), BF), shape((8, model), F32)],
        grid=(tokens // tile,),
        in_specs=[block] * (2 * pieces + 2) + [pl.BlockSpec((1, model), lambda i: (0, 0))],
        out_specs=[block, block, block, fixed],
        compiler_params=pltpu.CompilerParams(dimension_semantics=("arbitrary",), vmem_limit_bytes=LIMIT),
        cost_estimate=pl.CostEstimate(flops=20 * tokens * model, bytes_accessed=tokens * model * 22, transcendentals=tokens),
        name="norm_back",
    )(resid, *totals, *backs, out_grad, gain)


def eight_sum(v):
    return jnp.sum(v.reshape(v.shape[0] // 8, 8, v.shape[1]), axis=0)


def mixer_backward_kernel(
    split_ref, keep_ref, low_ref, q_ref, k_ref, v_ref, mixed_ref, wo_ref,
    fq_ref, fv_ref, fk_ref, slope_ref, shift_ref, skip_ref, fwd_real_ref, fwd_ref, inv_real_ref, inv_ref,
    p_ref, chan_ref,
    qs, ks, vs, xv, xc, xy, y_s, spec_s, u_s, o_s,
):
    r = pl.program_id(0)
    length, width = q_ref.shape
    quarter = length // 4
    split, keep = split_ref[r], keep_ref[r]
    tile = 64

    @pl.when(r == 0)
    def _():
        chan_ref[...] = jnp.zeros_like(chan_ref)

    for ref, source in ((qs, q_ref), (ks, k_ref), (vs, v_ref)):
        ref[0:8, :] = jnp.zeros((8, width), F32)

        def widen(i, ref=ref, source=source):
            ref[pl.ds(pl.multiple_of(8 + i * tile, 8), tile), :] = source[rows_of(i, tile), :].astype(F32)

        loop(length // tile, widen)

    o_s[0:length, 0:width] = mm_t(low_ref[...], wo_ref[...])

    def conv(i):
        t = i * tile
        rows = rows_of(i, tile)
        kept = t + lax.broadcasted_iota(jnp.int32, (tile, width), 0) < keep
        gated_grad = o_s[rows, 0:width]
        low = (gated_grad * conv_back(qs, t, tile, fq_ref, split)).astype(BF)
        xy[rows, :] = low
        value = jnp.where(kept, conv_back(vs, t, tile, fv_ref, split), 0.0).astype(BF)
        xv[rows, :] = value
        xc[rows, :] = jnp.where(kept, conv_back(ks, t, tile, fk_ref, split), 0.0).astype(BF)
        chan_ref[2, :, :] += eight_sum(low.astype(F32) * value.astype(F32))

    loop(length // tile, conv)
    butterfly(xv, y_s, 0, width, quarter)
    butterfly(xc, y_s, width, width, quarter)
    butterfly(xy, y_s, 2 * width, width, quarter)

    def query(i):
        rows = rows_of(i, tile)
        qs[rows, :] = o_s[rows, 0:width] * mixed_ref[rows, :].astype(F32)

    loop(length // tile, query)
    blockwise(y_s, spec_s, fwd_real_ref, fwd_ref, quarter)

    def bins(re, im, first):
        n = 16
        re, im = pl.ds(pl.multiple_of(re, n), n), pl.ds(pl.multiple_of(im, n), n)
        vr, vi = spec_s[re, 0:width], spec_s[im, 0:width]
        cr, ci = spec_s[re, width : 2 * width], spec_s[im, width : 2 * width]
        yr, yi = spec_s[re, 2 * width : 3 * width], spec_s[im, 2 * width : 3 * width]
        slope, shift = slope_ref[...], shift_ref[...]
        rr, ii = cr * cr, ci * ci
        if first:
            edge = lax.broadcasted_iota(jnp.int32, (n, width), 0) == 0
            pr, pi = jnp.where(edge, rr, rr + ii), jnp.where(edge, ii, rr + ii)
            gr, gi = jax.nn.sigmoid(slope * pr + shift), jax.nn.sigmoid(slope * pi + shift)
            ar = vr * yr + jnp.where(edge, 0.0, vi * yi)
            ai = jnp.where(edge, -vi * yi, vi * yr - vr * yi)
            br = ar * cr - jnp.where(edge, 0.0, ai * ci)
            bi = jnp.where(edge, -ai * ci, br)
            wr, wi = br * gr * (1.0 - gr), bi * gi * (1.0 - gi)
            ws = jnp.where(edge, 0.5 * (wr + wi), wr)
            wp = jnp.where(edge, 0.5 * (wr * pr + wi * pi), wr * pr)
            hr, hi = gr * cr, gi * ci
            er = hr * yr + jnp.where(edge, 0.0, hi * yi)
            ei = jnp.where(edge, hi * yi, hr * yi - hi * yr)
            dr = gr * ar + 2.0 * slope * wr * cr
            di = 2.0 * slope * wi * ci - gi * ai
        else:
            p = rr + ii
            g = jax.nn.sigmoid(slope * p + shift)
            ar, ai = vr * yr + vi * yi, vi * yr - vr * yi
            ws = (ar * cr - ai * ci) * (g * (1.0 - g))
            wp = ws * p
            hr, hi = g * cr, g * ci
            er, ei = hr * yr + hi * yi, hr * yi - hi * yr
            k = 2.0 * slope * ws
            dr, di = g * ar + k * cr, k * ci - g * ai
        chan_ref[0, :, :] += eight_sum(wp)
        chan_ref[1, :, :] += eight_sum(ws)
        u_s[re, 0:width] = er.astype(BF)
        u_s[im, 0:width] = ei.astype(BF)
        u_s[re, width : 2 * width] = dr.astype(BF)
        u_s[im, width : 2 * width] = di.astype(BF)

    each_bin(quarter, bins)
    resynth(u_s, o_s, inv_real_ref, inv_ref, quarter)

    def finish(i):
        n = 32
        value = recombine(o_s, slice(0, width), i, n, quarter)
        cond = recombine(o_s, slice(width, 2 * width), i, n, quarter)
        for k in range(4):
            rows = pl.ds(pl.multiple_of(k * quarter + i * n, n), n)
            kept = k * quarter + i * n + lax.broadcasted_iota(jnp.int32, (n, width), 0) < keep
            grad = (value[k] + skip_ref[...] * xy[rows, :].astype(F32)).astype(BF).astype(F32)
            vs[rows, :] = jnp.where(kept, grad, 0.0)
            ks[rows, :] = jnp.where(kept, cond[k].astype(BF).astype(F32), 0.0)

    loop(quarter // 32, finish)
    for ref in (qs, ks, vs):
        ref[length : length + 8, :] = jnp.zeros((8, width), F32)

    for slot, (ref, source, f_ref) in enumerate(((qs, q_ref, fq_ref), (vs, v_ref, fv_ref), (ks, k_ref, fk_ref))):

        def adjoint(i, slot=slot, ref=ref, source=source, f_ref=f_ref):
            t = i * tile
            rows = rows_of(i, tile)
            block = ref[pl.ds(pl.multiple_of(t, tile), tile + 8), :]
            position = t + lax.broadcasted_iota(jnp.int32, (tile, width), 0)
            g0 = block[0:tile]
            g1 = jnp.where(position + 1 != split, block[1 : tile + 1], 0.0)
            g2 = jnp.where((position + 2 != split) & (position + 1 != split), block[2 : tile + 2], 0.0)
            s = source[rows, :].astype(F32)
            place = slice((0, 2, 1)[slot] * width, ((0, 2, 1)[slot] + 1) * width)
            p_ref[rows, place] = (f_ref[0:1, :] * g0 + f_ref[1:2, :] * g1 + f_ref[2:3, :] * g2).astype(BF)
            for k, g in enumerate((g0, g1, g2)):
                chan_ref[3 + 3 * slot + k, :, :] += eight_sum(g * s)

        loop(length // tile, adjoint)


def mixer_backward(branch_low, split, keep, q, k, v, mixed, proj_out, short_filter, cond_filter, slope, shift, skip, tables, block, width=256):
    rows, length, model = q.shape
    blocks = model // width
    shape = jax.ShapeDtypeStruct
    pad = pltpu.VMEM((length + 8, width), F32)
    quarter = length // 4
    row = pl.BlockSpec((None, length, model), lambda r, *_: (r, 0, 0))
    part = pl.BlockSpec((None, length, width), lambda r, *_: (r, 0, block))

    def columns(size, offset):
        return pl.BlockSpec((size, width), lambda r, *_: (0, block + offset * blocks))

    fixed = lambda r, *_: (0, 0)
    table_specs = [once((2 * quarter, quarter), fixed), once((6 * quarter, 2 * quarter), fixed)] * 2
    one = columns(1, 0)
    flops = rows * (2 * length * model * width + 2 * 5 * width * (2 * length) * length // 2)
    return pl.pallas_call(
        mixer_backward_kernel,
        out_shape=[shape((rows, length, 3 * width), BF), shape((12, 8, width), F32)],
        grid_spec=pltpu.PrefetchScalarGridSpec(
            num_scalar_prefetch=2,
            grid=(rows,),
            in_specs=[row, part, part, part, part, pl.BlockSpec((width, model), lambda r, *_: (block, 0)), columns(3, 0), columns(3, 1), columns(3, 0), one, one, one] + table_specs,
            out_specs=[pl.BlockSpec((None, length, 3 * width), lambda r, *_: (r, 0, 0)), once((12, 8, width), lambda r, *_: (0, 0, 0))],
            scratch_shapes=[pad, pad, pad] + [pltpu.VMEM((length, width), BF)] * 3 + [
                pltpu.VMEM((2 * length, 3 * width), BF),
                pltpu.VMEM((2 * length, 3 * width), F32),
                pltpu.VMEM((2 * length, 2 * width), BF),
                pltpu.VMEM((2 * length, 2 * width), F32),
            ],
        ),
        compiler_params=pltpu.CompilerParams(dimension_semantics=("arbitrary",), vmem_limit_bytes=LIMIT),
        cost_estimate=pl.CostEstimate(flops=flops, bytes_accessed=rows * length * (model * 2 + width * 14), transcendentals=rows * length * width),
        name="mixer_backward",
    )(split, keep, branch_low, q, k, v, mixed, proj_out, short_filter, short_filter, cond_filter, slope, shift, skip, *tables)


def input_back_kernel(blocks, x_ref, grad_ref, gain_ref, w_ref, *refs):
    p_refs, (in_grad_ref, gain_grad_ref, acc) = refs[:blocks], refs[blocks:]
    model = x_ref.shape[1]
    width = model // blocks
    tile = 64

    @pl.when(pl.program_id(0) == 0)
    def _():
        gain_grad_ref[...] = jnp.zeros_like(gain_grad_ref)

    total = None
    for b, p_ref in enumerate(p_refs):
        for k in range(3):
            lanes = slice(k * model + b * width, k * model + (b + 1) * width)
            term = mm_t(p_ref[:, k * width : (k + 1) * width], w_ref[:, lanes])
            total = term if total is None else total + term
    acc[...] = total

    def body(i):
        rows = rows_of(i, tile)
        n, scale = norm_stats(x_ref[rows, :].astype(F32))
        u = acc[rows, :]
        ug = u * gain_ref[...]
        part = ug - jnp.mean(ug, axis=-1, keepdims=True) - n * jnp.mean(ug * n, axis=-1, keepdims=True)
        in_grad_ref[rows, :] = (grad_ref[rows, :] + scale * part).astype(in_grad_ref.dtype)
        gain_grad_ref[...] += eight_sum(u * n)

    loop(x_ref.shape[0] // tile, body)


def input_back(x, resid_grad, gain, proj_in, parts, tile=512):
    tokens, model = x.shape
    shape = jax.ShapeDtypeStruct
    block = pl.BlockSpec((tile, model), lambda i: (i, 0))
    return pl.pallas_call(
        functools.partial(input_back_kernel, len(parts)),
        out_shape=[shape((tokens, model), BF), shape((8, model), F32)],
        grid=(tokens // tile,),
        in_specs=[block, block, once((1, model), lambda i: (0, 0)), once((model, 3 * model), lambda i: (0, 0))] + [block] * len(parts),
        out_specs=[block, pl.BlockSpec((8, model), lambda i: (0, 0))],
        scratch_shapes=[pltpu.VMEM((tile, model), F32)],
        compiler_params=pltpu.CompilerParams(dimension_semantics=("arbitrary",), vmem_limit_bytes=LIMIT),
        cost_estimate=pl.CostEstimate(flops=6 * tokens * model * model, bytes_accessed=tokens * model * 14, transcendentals=tokens),
        name="input_back",
    )(x, resid_grad, gain, proj_in, *parts)


def turn(a, b):
    return lax.dot_general(a, b, (((0,), (0,)), ((), ())), preferred_element_type=F32).astype(BF)


def after(value, earlier):
    return lax.optimization_barrier((value, earlier))[0]


def exchange_sum_kernel(rows, seq, x_ref, out_ref, slots, total, send_sem, recv_sem):
    r, s = lax.axis_index("rows"), lax.axis_index("seq")
    partners = []
    bit = 1
    while bit < rows:
        partners.append((r + bit - 2 * bit * (lax.rem(r // bit, 2)), s))
        bit *= 2
    bit = 1
    while bit < seq:
        partners.append((r, s + bit - 2 * bit * (lax.rem(s // bit, 2))))
        bit *= 2
    barrier = pltpu.get_barrier_semaphore()
    for partner in partners:
        pl.semaphore_signal(barrier, inc=1, device_id=partner, device_id_type=pl.DeviceIdType.MESH)
    pl.semaphore_wait(barrier, len(partners))
    total[0] = x_ref[...]
    for step, partner in enumerate(partners):
        copy = pltpu.make_async_remote_copy(
            src_ref=total.at[step], dst_ref=slots.at[step], send_sem=send_sem.at[step], recv_sem=recv_sem.at[step],
            device_id=partner, device_id_type=pl.DeviceIdType.MESH,
        )
        copy.start()
        copy.wait()
        total[step + 1] = total[step] + slots[step]
    out_ref[...] = total[len(partners)]


def power_of_two(n):
    return n & (n - 1) == 0


def exchange_sum(value):
    rows, seq = lax.axis_size("rows"), lax.axis_size("seq")
    if not (power_of_two(rows) and power_of_two(seq)):
        return lax.psum(value, ("rows", "seq"))
    steps = (rows.bit_length() - 1) + (seq.bit_length() - 1)
    return pl.pallas_call(
        functools.partial(exchange_sum_kernel, rows, seq),
        out_shape=jax.ShapeDtypeStruct(value.shape, value.dtype),
        in_specs=[pl.BlockSpec(memory_space=pltpu.VMEM)],
        out_specs=pl.BlockSpec(memory_space=pltpu.VMEM),
        scratch_shapes=[
            pltpu.VMEM((steps, *value.shape), value.dtype),
            pltpu.VMEM((steps + 1, *value.shape), value.dtype),
            pltpu.SemaphoreType.DMA((steps,)),
            pltpu.SemaphoreType.DMA((steps,)),
        ],
        compiler_params=pltpu.CompilerParams(collective_id=7, has_side_effects=True),
        name="exchange_sum",
    )(value)


def swapped(value):
    count = lax.axis_size("seq")
    return lax.ppermute(value, "seq", [(i, (i + 1) % count) for i in range(count)])


def gather_rows(value):
    if lax.axis_size("seq") != 2:
        return lax.all_to_all(value, "seq", split_axis=0, concat_axis=1, tiled=True)
    s = lax.axis_index("seq")
    own = value.shape[0] // 2
    mine = lax.dynamic_slice_in_dim(value, s * own, own)
    other = swapped(lax.dynamic_slice_in_dim(value, (1 - s) * own, own))
    return jnp.concatenate([jnp.where(s == 0, mine, other), jnp.where(s == 0, other, mine)], axis=1)


def scatter_rows(value):
    if lax.axis_size("seq") != 2:
        return lax.all_to_all(value, "seq", split_axis=1, concat_axis=0, tiled=True)
    s = lax.axis_index("seq")
    part = value.shape[1] // 2
    mine = lax.dynamic_slice_in_dim(value, s * part, part, axis=1)
    other = swapped(lax.dynamic_slice_in_dim(value, (1 - s) * part, part, axis=1))
    return jnp.concatenate([jnp.where(s == 0, mine, other), jnp.where(s == 0, other, mine)], axis=0)


def seq_sum(value):
    if lax.axis_size("seq") != 2:
        return lax.psum(value, "seq").astype(F32)
    return value.astype(F32) + swapped(value).astype(F32)


def per_device_rows(inputs, split_point, keep_mask, norm_gain, proj_in, short_filter, cond_filter, spec_slope, spec_shift, skip_gain, proj_out, ffn_gain, ffn_in, ffn_out, out_grad):
    local_rows, local_len, model = inputs.shape
    count = lax.axis_size("seq")
    own = local_rows // count
    length = local_len * count
    tokens = own * length
    width = 256
    first_row = lax.axis_index("seq") * own
    flat = lambda a: a.reshape(tokens, model)
    shaped = lambda a: a.reshape(own, length, model)
    lift = lambda a: a.reshape(1, -1)

    x = gather_rows(inputs)
    kept = jnp.sum(keep_mask, axis=1)
    kept = kept + swapped(kept) if count == 2 else lax.psum(kept, "seq")
    keep = lax.dynamic_slice_in_dim(kept, first_row, own)
    split = lax.dynamic_slice_in_dim(split_point, first_row, own)
    whole_grad = flat(gather_rows(after(out_grad, x)))
    tables = spectral_tables(length, lax.axis_index("seq") * (2 * length))
    slope, shift, skip = lift(spec_slope), lift(spec_shift), lift(skip_gain)

    first, q, k, v, mixed, gated, resid, second = mixer_forward(
        x, split, keep, lift(norm_gain), proj_in, short_filter, cond_filter, slope, shift, skip, proj_out, lift(ffn_gain), tables
    )
    second = flat(second)
    second_turned, grad_turned = second.T, whole_grad.T
    pieces = 2
    totals, backs, ffn_shares = [], [], []
    chain = None
    for piece in range(pieces):
        total, back, grads = ffn_both(second, whole_grad, second_turned, grad_turned, ffn_in, ffn_out, piece, pieces)
        totals.append(total)
        backs.append(back)
        if chain is not None:
            grads = after(grads, chain)
        chain = lax.psum_scatter(grads, "rows", scatter_dimension=1, tiled=True)
        ffn_shares.append(seq_sum(chain))
    output, resid_grad, branch_low, ffn_gain_part = norm_back(flat(resid), totals, backs, whole_grad, lift(ffn_gain))
    output = scatter_rows(shaped(output))
    branch_low = shaped(branch_low)
    parts, mix_shares, chans = [], [], []
    for block in range(model // width):
        if block == 2:
            branch_low = after(branch_low, output)
        part, chan = mixer_backward(branch_low, split, keep, q, k, v, mixed, proj_out, short_filter, cond_filter, slope, shift, skip, tables, block)
        parts.append(flat(part))
        chans.append(chan)
        grads = turn(flat(first), parts[-1])
        if block == 0:
            grads = jnp.concatenate([turn(flat(gated), flat(branch_low)), grads], axis=1)
        grads = after(grads, chain)
        chain = lax.psum_scatter(grads, "rows", scatter_dimension=0, tiled=True)
        mix_shares.append(seq_sum(chain))
    input_grad, norm_gain_part = input_back(flat(x), resid_grad, lift(norm_gain), proj_in, parts)
    input_grad = scatter_rows(shaped(input_grad)).astype(F32)
    small = jnp.sum(jnp.concatenate([ffn_gain_part[None], norm_gain_part[None], jnp.concatenate(chans, axis=2)], 0), axis=1)
    small = exchange_sum(small)
    scale = 1.0 / length
    out_share, mix_shares[0] = mix_shares[0][:, :model], mix_shares[0][:, model:]
    return (
        output,
        input_grad,
        small[1],
        jnp.concatenate([share[:, k * width : (k + 1) * width] for k in range(3) for share in mix_shares], axis=1),
        jnp.concatenate([small[5:8], small[8:11]], axis=1),
        small[11:14],
        small[2] * scale,
        small[3] * scale,
        small[4],
        out_share,
        small[0],
        jnp.concatenate([share[k] for k in range(2) for share in ffn_shares], axis=1),
        jnp.concatenate([share[2] for share in ffn_shares], axis=1).T,
    )


PRECISE = lax.Precision.HIGH


def passed_along(value, axis, steps):
    count = lax.axis_size(axis)
    leading, last = (max(0, -steps), min(count, count - steps))
    return lax.ppermute(value, axis, [(source, source + steps) for source in range(leading, last)])


def layer_norm(values, scaling):
    center = values - jnp.mean(values, axis=-1, keepdims=True)
    spread = jnp.mean(center * center, axis=-1, keepdims=True)
    return center * lax.rsqrt(spread + EPSILON) * scaling


def conv_three(extended, weights, same_one, same_two):
    length = extended.shape[1] - 2
    return (
        weights[0] * extended[:, 2:]
        + weights[1] * extended[:, 1 : length + 1] * same_one
        + weights[2] * extended[:, :length] * same_two
    )


def dft_tables(seq_length):
    table_shape = (seq_length + 1, seq_length)
    product = lax.broadcasted_iota(jnp.int32, table_shape, 0) * lax.broadcasted_iota(
        jnp.int32, table_shape, 1
    )
    angles = (product % (2 * seq_length)).astype(jnp.float32) * (math.pi / seq_length)
    freq = lax.broadcasted_iota(jnp.int32, (seq_length + 1, 1), 0)
    edge = jnp.logical_or(freq == 0, freq == seq_length)
    weights = jnp.where(edge, 1.0, 2.0).astype(jnp.float32) / (2.0 * seq_length)
    return (jnp.cos(angles), jnp.sin(angles), weights)


def analyze(values, conds, cos_table, sin_table):
    value_real = jnp.einsum("ft,ktd->kfd", cos_table, values, precision=PRECISE)
    value_imag = -jnp.einsum("ft,ktd->kfd", sin_table, values, precision=PRECISE)
    cond_real = jnp.einsum("ft,ktd->kfd", cos_table, conds, precision=PRECISE)
    cond_imag = -jnp.einsum("ft,ktd->kfd", sin_table, conds, precision=PRECISE)
    return (value_real, value_imag, cond_real, cond_imag)


def synth(
    value_real,
    value_imag,
    cond_real,
    cond_imag,
    values,
    slopes,
    shifts,
    skip_gains,
    cos_table,
    sin_table,
    freq_weights,
):
    factor = jax.nn.sigmoid(slopes * (cond_real * cond_real + cond_imag * cond_imag) + shifts)
    filter_real = cond_real * factor
    filter_imag = cond_imag * factor
    prod_real = (value_real * filter_real - value_imag * filter_imag) * freq_weights
    prod_imag = (value_real * filter_imag + value_imag * filter_real) * freq_weights
    mixed_out = jnp.einsum("ft,kfd->ktd", cos_table, prod_real, precision=PRECISE) - jnp.einsum(
        "ft,kfd->ktd", sin_table, prod_imag, precision=PRECISE
    )
    return mixed_out + skip_gains * values


def times_transpose(left, right):
    return lax.dot_general(
        left, right, (((1,), (1,)), ((), ())), preferred_element_type=jnp.float32
    )


def transpose_times(left, right):
    return lax.dot_general(
        left, right, (((0,), (0,)), ((), ())), preferred_element_type=jnp.float32
    )


def per_device(
    inputs,
    split_point,
    keep_mask,
    norm_gain,
    proj_in,
    short_filter,
    cond_filter,
    spec_slope,
    spec_shift,
    skip_gain,
    proj_out,
    ffn_gain,
    ffn_in,
    ffn_out,
    out_grad,
):
    local_rows, local_len, model_width = inputs.shape
    hidden_width = ffn_out.shape[0]
    seq_count = lax.axis_size("seq")
    seq_index = lax.axis_index("seq")
    full_len = local_len * seq_count
    chan_width = model_width // seq_count
    token_count = local_rows * local_len
    positions = seq_index * local_len + lax.broadcasted_iota(jnp.int32, (local_rows, local_len), 1)
    splits = split_point[:, None]
    segment = positions >= splits
    same_one = (segment == (positions - 1 >= splits)).astype(jnp.float32)[:, :, None]
    same_two = (segment == (positions - 2 >= splits)).astype(jnp.float32)[:, :, None]
    keep_float = keep_mask.astype(jnp.float32)[:, :, None]
    flat_in = inputs.reshape(token_count, model_width).astype(jnp.float32)
    normed_one, norm_one_back = jax.vjp(layer_norm, flat_in, norm_gain)
    first_act = normed_one.astype(jnp.bfloat16)
    projected = jnp.dot(first_act, proj_in, preferred_element_type=jnp.float32).astype(jnp.bfloat16)
    proj_rows = projected.reshape(local_rows, local_len, 3 * model_width)
    edge_values = passed_along(proj_rows[:, local_len - 2 :, :], "seq", 1)
    extended = jnp.concatenate([edge_values, proj_rows], axis=1).astype(jnp.float32)

    def mixer_local(ext_values, short_weights, cond_weights):
        query_value = jnp.concatenate(
            [ext_values[:, :, :model_width], ext_values[:, :, 2 * model_width :]], axis=2
        )
        conv_both = conv_three(query_value, short_weights, same_one, same_two)
        cond_conv = conv_three(
            ext_values[:, :, model_width : 2 * model_width], cond_weights, same_one, same_two
        )
        return (
            conv_both[:, :, :model_width],
            conv_both[:, :, model_width:] * keep_float,
            cond_conv * keep_float,
        )

    (query_conv, value_masked, cond_masked), mixer_back = jax.vjp(
        mixer_local, extended, short_filter, cond_filter
    )
    value_low = value_masked.astype(jnp.bfloat16)
    cond_low = cond_masked.astype(jnp.bfloat16)
    slope_part = lax.dynamic_slice_in_dim(spec_slope, seq_index * chan_width, chan_width)
    shift_part = lax.dynamic_slice_in_dim(spec_shift, seq_index * chan_width, chan_width)
    skip_part = lax.dynamic_slice_in_dim(skip_gain, seq_index * chan_width, chan_width)
    cos_table, sin_table, freq_weights = dft_tables(full_len)

    def synth_local(
        value_real, value_imag, cond_real, cond_imag, values, slopes, shifts, skip_gains
    ):
        return synth(
            value_real,
            value_imag,
            cond_real,
            cond_imag,
            values,
            slopes,
            shifts,
            skip_gains,
            cos_table,
            sin_table,
            freq_weights,
        )

    value_chan = lax.all_to_all(value_low, "seq", split_axis=2, concat_axis=1, tiled=True)
    cond_chan = lax.all_to_all(cond_low, "seq", split_axis=2, concat_axis=1, tiled=True)
    value_float = value_chan.astype(jnp.float32)
    spectra = analyze(value_float, cond_chan.astype(jnp.float32), cos_table, sin_table)
    mixed_chan = synth_local(
        spectra[0],
        spectra[1],
        spectra[2],
        spectra[3],
        value_float,
        slope_part,
        shift_part,
        skip_part,
    ).astype(jnp.bfloat16)
    mixed_home = lax.all_to_all(mixed_chan, "seq", split_axis=1, concat_axis=2, tiled=True)
    mixed_float = mixed_home.astype(jnp.float32)
    gated = (query_conv * mixed_float).astype(jnp.bfloat16).reshape(token_count, model_width)
    branch = jnp.dot(gated, proj_out, preferred_element_type=jnp.float32)
    resid = flat_in + branch
    normed_two, norm_two_back = jax.vjp(layer_norm, resid, ffn_gain)
    second_act = normed_two.astype(jnp.bfloat16)
    gate_up = jnp.dot(second_act, ffn_in, preferred_element_type=jnp.float32)

    def glu_local(both_parts):
        return (
            jax.nn.gelu(both_parts[:, :hidden_width], approximate=False)
            * both_parts[:, hidden_width:]
        )

    hidden, glu_back = jax.vjp(glu_local, gate_up)
    hidden_low = hidden.astype(jnp.bfloat16)
    result = resid + jnp.dot(hidden_low, ffn_out, preferred_element_type=jnp.float32)
    output = result.astype(jnp.bfloat16).reshape(local_rows, local_len, model_width)
    flat_grad = out_grad.reshape(token_count, model_width)
    hidden_grad = times_transpose(flat_grad, ffn_out)
    (gate_up_grad,) = glu_back(hidden_grad)
    gate_up_low = gate_up_grad.astype(jnp.bfloat16)
    second_grad = times_transpose(gate_up_low, ffn_in)
    resid_part, ffn_gain_part = norm_two_back(second_grad)
    resid_grad = flat_grad.astype(jnp.float32) + resid_part
    branch_low = resid_grad.astype(jnp.bfloat16)
    gated_grad = times_transpose(branch_low, proj_out).reshape(local_rows, local_len, model_width)
    query_grad = gated_grad * mixed_float
    mixed_grad = (gated_grad * query_conv).astype(jnp.bfloat16)
    grad_chan = lax.all_to_all(mixed_grad, "seq", split_axis=2, concat_axis=1, tiled=True)
    grad_float = grad_chan.astype(jnp.float32)
    item_count = grad_chan.shape[0]
    slope_items = jnp.broadcast_to(slope_part, (item_count, 1, chan_width))
    shift_items = jnp.broadcast_to(shift_part, (item_count, 1, chan_width))
    skip_items = jnp.broadcast_to(skip_part, (item_count, 1, chan_width))
    value_float = value_chan.astype(jnp.float32)

    def spectral(values, conds, slopes, shifts, skip_gains):
        spectra = analyze(values, conds, cos_table, sin_table)
        return synth_local(
            spectra[0], spectra[1], spectra[2], spectra[3], values, slopes, shifts, skip_gains
        )

    unused, pull = jax.vjp(
        spectral, value_float, cond_chan.astype(jnp.float32), slope_items, shift_items, skip_items
    )
    value_back, cond_back, slope_rows, shift_rows, skip_rows = pull(grad_float)
    value_grad, cond_grad = (
        lax.all_to_all(
            value_back.astype(jnp.bfloat16), "seq", split_axis=1, concat_axis=2, tiled=True
        ),
        lax.all_to_all(
            cond_back.astype(jnp.bfloat16), "seq", split_axis=1, concat_axis=2, tiled=True
        ),
    )
    start_chan = (seq_index * chan_width,)
    empty_width = jnp.zeros((model_width,), jnp.float32)
    slope_full = lax.dynamic_update_slice(empty_width, jnp.sum(slope_rows, axis=(0, 1)), start_chan)
    shift_full = lax.dynamic_update_slice(empty_width, jnp.sum(shift_rows, axis=(0, 1)), start_chan)
    skip_full = lax.dynamic_update_slice(empty_width, jnp.sum(skip_rows, axis=(0, 1)), start_chan)
    ext_grad, short_grad, cond_weight_grad = mixer_back(
        (query_grad, value_grad.astype(jnp.float32), cond_grad.astype(jnp.float32))
    )
    incoming = passed_along(ext_grad[:, :2, :].astype(jnp.bfloat16), "seq", -1).astype(jnp.float32)
    proj_grad = ext_grad[:, 2:, :] + jnp.pad(incoming, ((0, 0), (local_len - 2, 0), (0, 0)))
    proj_low = proj_grad.astype(jnp.bfloat16).reshape(token_count, 3 * model_width)
    first_grad = times_transpose(proj_low, proj_in)
    input_part, norm_gain_part = norm_one_back(first_grad)
    input_grad = (resid_grad + input_part).reshape(local_rows, local_len, model_width)
    share = lax.psum_scatter(
        jnp.concatenate(
            [
                transpose_times(first_act, proj_low),
                transpose_times(gated, branch_low),
                transpose_times(second_act, gate_up_low),
                transpose_times(flat_grad, hidden_low),
            ],
            axis=1,
        ).astype(jnp.bfloat16),
        "rows",
        scatter_dimension=0,
        tiled=True,
    )
    summed = lax.psum(share, "seq").astype(jnp.float32)
    small_sums = lax.psum(
        (
            norm_gain_part,
            short_grad,
            cond_weight_grad,
            slope_full,
            shift_full,
            skip_full,
            ffn_gain_part,
        ),
        ("rows", "seq"),
    )
    proj_in_grad = summed[:, : 3 * model_width]
    proj_out_grad = summed[:, 3 * model_width : 4 * model_width]
    ffn_in_grad = summed[:, 4 * model_width : 4 * model_width + 2 * hidden_width]
    ffn_out_grad = jnp.transpose(summed[:, 4 * model_width + 2 * hidden_width :])
    return (
        output,
        input_grad,
        small_sums[0],
        proj_in_grad,
        small_sums[1],
        small_sums[2],
        small_sums[3],
        small_sums[4],
        small_sums[5],
        proj_out_grad,
        small_sums[6],
        ffn_in_grad,
        ffn_out_grad,
    )


def per_device_any(*args):
    rows, width = args[0].shape[0], args[0].shape[2]
    even = rows % lax.axis_size("seq") == 0 and width % 256 == 0
    return (per_device_rows if even else per_device)(*args)


def solution(mesh):
    in_specs = (
        P("rows", "seq", None),
        P("rows"),
        P("rows", "seq"),
        P(),
        P(),
        P(),
        P(),
        P(),
        P(),
        P(),
        P(),
        P(),
        P(),
        P(),
        P("rows", "seq", None),
    )
    out_specs = (
        P("rows", "seq", None),
        P("rows", "seq", None),
        P(),
        P("rows", None),
        P(),
        P(),
        P(),
        P(),
        P(),
        P("rows", None),
        P(),
        P("rows", None),
        P(None, "rows"),
    )
    return jax.shard_map(
        per_device_any, mesh=mesh, in_specs=in_specs, out_specs=out_specs, check_vma=False
    )
```

```python
import functools
import math

import jax
import jax.numpy as jnp
from jax import lax
from jax.experimental import pallas as pl
from jax.experimental.pallas import tpu as pltpu
from jax.sharding import PartitionSpec as P

EPSILON = 1e-05
BF = jnp.bfloat16
F32 = jnp.float32
ROOT_HALF = math.sqrt(0.5)
LIMIT = 67043328


def mm(a, b):
    return lax.dot_general(a, b, (((1,), (0,)), ((), ())), preferred_element_type=F32)


def mm_t(a, b):
    return lax.dot_general(a, b, (((1,), (1,)), ((), ())), preferred_element_type=F32)


def spectral_tables(length, offset):
    quarter = length // 4
    two_n = 2 * length
    m = lax.broadcasted_iota(jnp.int32, (quarter, quarter), 0)
    s = lax.broadcasted_iota(jnp.int32, (quarter, quarter), 1)

    def cos_sin(freq):
        angle = ((freq * s + offset) % two_n).astype(F32) * (2.0 * math.pi / two_n)
        return jnp.cos(angle), jnp.sin(angle)

    half = quarter // 2
    forward, inverse = [], []
    for r in (1, 2, 3):
        c, sn = cos_sin(8 * m + r)
        forward.append(jnp.concatenate([jnp.concatenate([c, sn], 1), jnp.concatenate([-sn, c], 1)], 0))
        inverse.append(forward[-1].T * (2.0 / two_n))
    row = m % half
    low = m < half
    c, sn = cos_sin(8 * jnp.where(m == half, half, row))
    zero = jnp.where(low | (m == half), c, -sn)
    c4, sn4 = cos_sin(8 * row + 4)
    four = jnp.where(low, c4, -sn4)
    edge = jnp.where((m == 0) | (m == half), 1.0, 2.0) / two_n
    fwd_real = jnp.concatenate([zero, four], 0)
    inv_real = jnp.concatenate([(zero * edge).T, four.T * (2.0 / two_n)], 0)
    return (
        fwd_real.astype(BF),
        jnp.concatenate(forward, 0).astype(BF),
        inv_real.astype(BF),
        jnp.concatenate(inverse, 0).astype(BF),
    )


def loop(count, body):
    lax.fori_loop(0, count, lambda i, c: (body(i), c)[1], 0)


def rows_of(i, size):
    return pl.ds(pl.multiple_of(i * size, size), size)


def norm_stats(v):
    center = v - jnp.mean(v, axis=-1, keepdims=True)
    scale = lax.rsqrt(jnp.mean(center * center, axis=-1, keepdims=True) + EPSILON)
    return center * scale, scale


def same_masks(position, split):
    same_one = position != split
    return same_one, same_one & (position != split + 1)


def butterfly(x_ref, y_ref, lane, width, quarter):
    tile = 32
    lanes = slice(lane, lane + width)

    def body(i):
        x0, x1, x2, x3 = [
            x_ref[pl.ds(pl.multiple_of(q * quarter + i * tile, tile), tile), :].astype(F32) for q in range(4)
        ]
        a, b, c, d = x0 + x2, x1 + x3, x0 - x2, x1 - x3
        sd, sb = d * ROOT_HALF, b * ROOT_HALF
        out = (a + b, a - b, x0 + sd, -x2 - sb, c, -d, x0 - sd, x2 - sb)
        for k, value in enumerate(out):
            y_ref[pl.ds(pl.multiple_of(k * quarter + i * tile, tile), tile), lanes] = value.astype(BF)

    loop(quarter // tile, body)


def blockwise(y_ref, spec_ref, fwd_real_ref, fwd_ref, quarter):
    q = quarter
    for k in range(2):
        spec_ref[k * q : (k + 1) * q, :] = mm(fwd_real_ref[k * q : (k + 1) * q, :], y_ref[k * q : (k + 1) * q, :])
    for k in range(3):
        spec_ref[2 * q + 2 * k * q : 2 * q + 2 * (k + 1) * q, :] = mm(
            fwd_ref[2 * k * q : 2 * (k + 1) * q, :], y_ref[2 * q + 2 * k * q : 2 * q + 2 * (k + 1) * q, :]
        )


def resynth(u_ref, out_ref, inv_real_ref, inv_ref, quarter):
    blockwise(u_ref, out_ref, inv_real_ref, inv_ref, quarter)


def each_bin(quarter, body, tile=16):
    half = quarter // 2
    body(0, half, True)

    def run(base, span, skip):
        def step(i):
            start = base + (i + skip) * tile
            body(start, start + span, False)

        loop(span // tile - skip, step)

    run(0, half, 1)
    run(quarter, half, 0)
    for k in range(3):
        run(2 * quarter + 2 * k * quarter, quarter, 0)


def recombine(o_ref, lanes, i, tile, quarter):
    def part(k):
        return o_ref[pl.ds(pl.multiple_of(k * quarter + i * tile, tile), tile), lanes]

    u0, u4, a1, b1, a2, b2, a3, b3 = [part(k) for k in range(8)]
    even, odd = u0 + u4, u0 - u4
    return (
        even + a1 + a2 + a3,
        odd + (a1 - b1 - a3 - b3) * ROOT_HALF - b2,
        even - b1 - a2 + b3,
        odd + (a3 - b3 - a1 - b1) * ROOT_HALF + b2,
    )


def conv_back(ref, t, tile, weights, split):
    block = ref[pl.ds(pl.multiple_of(t, tile), tile + 8), :]
    width = block.shape[1]
    position = t + lax.broadcasted_iota(jnp.int32, (tile, width), 0)
    one, two = same_masks(position, split)
    return (
        weights[0:1, :] * block[8 : tile + 8]
        + jnp.where(one, weights[1:2, :] * block[7 : tile + 7], 0.0)
        + jnp.where(two, weights[2:3, :] * block[6 : tile + 6], 0.0)
    )


def mixer_forward_kernel(
    split_ref, keep_ref, x_ref, norm_gain_ref, wq_ref, wk_ref, wv_ref, fq_ref, fv_ref, fk_ref, slope_ref, shift_ref,
    skip_ref, wo_ref, ffn_gain_ref, fwd_real_ref, fwd_ref, inv_real_ref, inv_ref,
    first_ref, q_ref, k_ref, v_ref, mixed_ref, gated_ref, resid_ref, second_ref,
    qs, ks, vs, xv, xc, y_s, spec_s, u_s, o_s, qc,
):
    r, j = pl.program_id(0), pl.program_id(1)
    length, width = q_ref.shape
    quarter = length // 4
    split, keep = split_ref[r], keep_ref[r]
    tile = 64

    @pl.when(j == 0)
    def _():
        def body(i):
            rows = rows_of(i, tile)
            v = x_ref[rows, :].astype(F32)
            n, _ = norm_stats(v)
            first_ref[rows, :] = (n * norm_gain_ref[...]).astype(BF)
            resid_ref[rows, :] = v

        loop(length // tile, body)
        for ref in (qs, ks, vs):
            ref[0:8, :] = jnp.zeros((8, width), F32)

    for w_ref, out_ref, ref in ((wq_ref, q_ref, qs), (wk_ref, k_ref, ks), (wv_ref, v_ref, vs)):
        value = mm(first_ref[...], w_ref[...]).astype(BF)
        out_ref[...] = value
        ref[8 : 8 + length, :] = value.astype(F32)

    def conv(i):
        t = i * tile
        rows = rows_of(i, tile)
        kept = t + lax.broadcasted_iota(jnp.int32, (tile, width), 0) < keep
        qc[rows, :] = conv_back(qs, t, tile, fq_ref, split)
        xv[rows, :] = jnp.where(kept, conv_back(vs, t, tile, fv_ref, split), 0.0).astype(BF)
        xc[rows, :] = jnp.where(kept, conv_back(ks, t, tile, fk_ref, split), 0.0).astype(BF)

    loop(length // tile, conv)
    butterfly(xv, y_s, 0, width, quarter)
    butterfly(xc, y_s, width, width, quarter)
    blockwise(y_s, spec_s, fwd_real_ref, fwd_ref, quarter)

    def bins(re, im, first):
        n = 16
        re, im = pl.ds(pl.multiple_of(re, n), n), pl.ds(pl.multiple_of(im, n), n)
        vr, vi = spec_s[re, 0:width], spec_s[im, 0:width]
        cr, ci = spec_s[re, width : 2 * width], spec_s[im, width : 2 * width]
        slope, shift = slope_ref[...], shift_ref[...]
        rr, ii = cr * cr, ci * ci
        if first:
            edge = lax.broadcasted_iota(jnp.int32, (n, width), 0) == 0
            hr = cr * jax.nn.sigmoid(slope * jnp.where(edge, rr, rr + ii) + shift)
            hi = ci * jax.nn.sigmoid(slope * jnp.where(edge, ii, rr + ii) + shift)
            ur = vr * hr - jnp.where(edge, 0.0, vi * hi)
            ui = jnp.where(edge, vi * hi, vr * hi + vi * hr)
        else:
            gain = jax.nn.sigmoid(slope * (rr + ii) + shift)
            hr, hi = cr * gain, ci * gain
            ur, ui = vr * hr - vi * hi, vr * hi + vi * hr
        u_s[re, :] = ur.astype(BF)
        u_s[im, :] = ui.astype(BF)

    each_bin(quarter, bins)
    resynth(u_s, o_s, inv_real_ref, inv_ref, quarter)

    def finish(i):
        n = 32
        parts = recombine(o_s, slice(0, width), i, n, quarter)
        for k, part in enumerate(parts):
            rows = pl.ds(pl.multiple_of(k * quarter + i * n, n), n)
            mixed = (part + skip_ref[...] * xv[rows, :].astype(F32)).astype(BF)
            mixed_ref[rows, :] = mixed
            gated_ref[rows, :] = (qc[rows, :] * mixed.astype(F32)).astype(BF)

    loop(quarter // 32, finish)
    resid_ref[...] += mm(gated_ref[...], wo_ref[...])

    @pl.when(j == pl.num_programs(1) - 1)
    def _():
        def body(i):
            rows = rows_of(i, tile)
            n, _ = norm_stats(resid_ref[rows, :])
            second_ref[rows, :] = (n * ffn_gain_ref[...]).astype(BF)

        loop(length // tile, body)


def once(shape, index):
    return pl.BlockSpec(shape, index, pipeline_mode=pl.Buffered(1))


def mixer_specs(length, model, width):
    blocks = model // width
    row = pl.BlockSpec((None, length, model), lambda r, j, *_: (r, 0, 0))
    part = pl.BlockSpec((None, length, width), lambda r, j, *_: (r, 0, j))

    def columns(rows, offset):
        return pl.BlockSpec((rows, width), lambda r, j, *_: (0, j + offset * blocks))

    out_rows = pl.BlockSpec((width, model), lambda r, j, *_: (j, 0))
    gain = once((1, model), lambda r, j, *_: (0, 0))
    q = length // 4
    tables = [once((2 * q, q), lambda r, j, *_: (0, 0)), once((6 * q, 2 * q), lambda r, j, *_: (0, 0))]
    return blocks, row, part, columns, out_rows, gain, tables + tables


def mixer_forward(x, split, keep, norm_gain, proj_in, short_filter, cond_filter, slope, shift, skip, proj_out, ffn_gain, tables, width=256):
    rows, length, model = x.shape
    blocks, row, part, columns, out_rows, gain, table_specs = mixer_specs(length, model, width)
    one = columns(1, 0)
    shape = jax.ShapeDtypeStruct
    low, full = shape((rows, length, model), BF), shape((rows, length, model), F32)
    pad = pltpu.VMEM((length + 8, width), F32)
    flops = rows * (2 * length * model * (3 * model + model) + 2 * 3 * model * (2 * length) * length // 2)
    return pl.pallas_call(
        mixer_forward_kernel,
        out_shape=[low, low, low, low, low, low, full, low],
        grid_spec=pltpu.PrefetchScalarGridSpec(
            num_scalar_prefetch=2,
            grid=(rows, blocks),
            in_specs=[row, gain, columns(model, 0), columns(model, 1), columns(model, 2), columns(3, 0), columns(3, 1), columns(3, 0), one, one, one, out_rows, gain] + table_specs,
            out_specs=[row, part, part, part, part, part, row, row],
            scratch_shapes=[pad, pad, pad] + [pltpu.VMEM((length, width), BF)] * 2 + [
                pltpu.VMEM((2 * length, 2 * width), BF),
                pltpu.VMEM((2 * length, 2 * width), F32),
                pltpu.VMEM((2 * length, width), BF),
                pltpu.VMEM((2 * length, width), F32),
                pltpu.VMEM((length, width), F32),
            ],
        ),
        compiler_params=pltpu.CompilerParams(dimension_semantics=("arbitrary", "arbitrary"), vmem_limit_bytes=LIMIT),
        cost_estimate=pl.CostEstimate(flops=flops, bytes_accessed=rows * length * model * 20, transcendentals=rows * length * model),
        name="mixer_forward",
    )(split, keep, x, norm_gain, proj_in, proj_in, proj_in, short_filter, short_filter, cond_filter, slope, shift, skip, proj_out, ffn_gain, *tables)


def normal_cdf_pdf(x):
    z = jnp.abs(x) * ROOT_HALF
    t = 1.0 / (1.0 + 0.3275911 * z)
    e = jnp.exp(-z * z)
    poly = t * (0.127414796 + t * (-0.142248368 + t * (0.7107068705 + t * (-0.7265760135 + t * 0.5307027145))))
    tail = poly * e
    return jnp.where(x >= 0, 1.0 - tail, tail), x * e * (1.0 / math.sqrt(2.0 * math.pi))


def ffn_kernel(
    sa_ref, og_ref, sat_ref, ogt_ref, wg_ref, wu_ref, wo_ref, out_ref, back_ref, grads_ref, gs, us, ds, hid, gg, ug
):
    j = pl.program_id(0)
    tokens, model = sa_ref.shape
    tile = gs.shape[0]
    chunk = 32

    @pl.when(j == 0)
    def _():
        def body(i):
            out_ref[rows_of(i, tile), :] = jnp.zeros((tile, model), F32)
            back_ref[rows_of(i, tile), :] = jnp.zeros((tile, model), F32)

        loop(tokens // tile, body)

    def body(i):
        rows = rows_of(i, tile)
        sa = sa_ref[rows, :]
        gs[...] = mm(sa, wg_ref[...])
        us[...] = mm(sa, wu_ref[...])
        ds[...] = mm_t(og_ref[rows, :], wo_ref[...])
        for c in range(tile // chunk):
            part = slice(c * chunk, (c + 1) * chunk)
            gate, up, dh = gs[part, :], us[part, :], ds[part, :]
            cdf, xpdf = normal_cdf_pdf(gate)
            act = gate * cdf
            target = pl.ds(pl.multiple_of(i * tile + c * chunk, chunk), chunk)
            hid[target, :] = (act * up).astype(BF)
            gg[target, :] = (dh * up * (cdf + xpdf)).astype(BF)
            ug[target, :] = (dh * act).astype(BF)
        out_ref[rows, :] += mm(hid[rows, :], wo_ref[...])
        back_ref[rows, :] += mm_t(gg[rows, :], wg_ref[...]) + mm_t(ug[rows, :], wu_ref[...])

    loop(tokens // tile, body)
    grads_ref[0] = mm(sat_ref[...], gg[...]).astype(BF)
    grads_ref[1] = mm(sat_ref[...], ug[...]).astype(BF)
    grads_ref[2] = mm(ogt_ref[...], hid[...]).astype(BF)


def ffn_both(second_act, out_grad, second_turned, grad_turned, ffn_in, ffn_out, piece, pieces, width=512, tile=256):
    tokens, model = second_act.shape
    total_blocks = ffn_out.shape[0] // width
    blocks = total_blocks // pieces
    first = piece * blocks
    hidden = blocks * width
    shape = jax.ShapeDtypeStruct
    whole = once((tokens, model), lambda j: (0, 0))
    turned = once((model, tokens), lambda j: (0, 0))
    return pl.pallas_call(
        ffn_kernel,
        out_shape=[shape((tokens, model), F32), shape((tokens, model), F32), shape((3, model, hidden), BF)],
        grid=(blocks,),
        in_specs=[
            whole, whole, turned, turned,
            pl.BlockSpec((model, width), lambda j: (0, j + first)),
            pl.BlockSpec((model, width), lambda j: (0, j + first + total_blocks)),
            pl.BlockSpec((width, model), lambda j: (j + first, 0)),
        ],
        out_specs=[whole, whole, pl.BlockSpec((3, model, width), lambda j: (0, 0, j))],
        scratch_shapes=[pltpu.VMEM((tile, width), F32)] * 3 + [pltpu.VMEM((tokens, width), BF)] * 3,
        compiler_params=pltpu.CompilerParams(dimension_semantics=("arbitrary",), vmem_limit_bytes=LIMIT),
        cost_estimate=pl.CostEstimate(flops=18 * tokens * model * hidden, bytes_accessed=tokens * model * 24 + model * hidden * 12, transcendentals=tokens * hidden),
        name="ffn_both",
    )(second_act, out_grad, second_turned, grad_turned, ffn_in, ffn_in, ffn_out)


def norm_back_kernel(pieces, resid_ref, *refs):
    sum_refs, back_refs = refs[:pieces], refs[pieces : 2 * pieces]
    og_ref, gain_ref, out_ref, grad_ref, low_ref, gain_grad_ref = refs[2 * pieces :]

    @pl.when(pl.program_id(0) == 0)
    def _():
        gain_grad_ref[...] = jnp.zeros_like(gain_grad_ref)

    tile = 64

    def body(i):
        rows = rows_of(i, tile)
        resid = resid_ref[rows, :]
        n, scale = norm_stats(resid)
        u = sum(ref[rows, :] for ref in back_refs)
        ug = u * gain_ref[...]
        un = u * n
        part = ug - jnp.mean(ug, axis=-1, keepdims=True) - n * jnp.mean(ug * n, axis=-1, keepdims=True)
        grad = og_ref[rows, :].astype(F32) + scale * part
        out_ref[rows, :] = (resid + sum(ref[rows, :] for ref in sum_refs)).astype(BF)
        grad_ref[rows, :] = grad
        low_ref[rows, :] = grad.astype(BF)
        gain_grad_ref[...] += jnp.sum(un.reshape(tile // 8, 8, un.shape[1]), axis=0)

    loop(resid_ref.shape[0] // tile, body)


def norm_back(resid, totals, backs, out_grad, gain, tile=512):
    tokens, model = resid.shape
    pieces = len(totals)
    shape = jax.ShapeDtypeStruct
    block = pl.BlockSpec((tile, model), lambda i: (i, 0))
    fixed = pl.BlockSpec((8, model), lambda i: (0, 0))
    return pl.pallas_call(
        functools.partial(norm_back_kernel, pieces),
        out_shape=[shape((tokens, model), BF), shape((tokens, model), F32), shape((tokens, model), BF), shape((8, model), F32)],
        grid=(tokens // tile,),
        in_specs=[block] * (2 * pieces + 2) + [pl.BlockSpec((1, model), lambda i: (0, 0))],
        out_specs=[block, block, block, fixed],
        compiler_params=pltpu.CompilerParams(dimension_semantics=("arbitrary",), vmem_limit_bytes=LIMIT),
        cost_estimate=pl.CostEstimate(flops=20 * tokens * model, bytes_accessed=tokens * model * 22, transcendentals=tokens),
        name="norm_back",
    )(resid, *totals, *backs, out_grad, gain)


def eight_sum(v):
    return jnp.sum(v.reshape(v.shape[0] // 8, 8, v.shape[1]), axis=0)


def mixer_backward_kernel(
    split_ref, keep_ref, low_ref, q_ref, k_ref, v_ref, mixed_ref, wo_ref,
    fq_ref, fv_ref, fk_ref, slope_ref, shift_ref, skip_ref, fwd_real_ref, fwd_ref, inv_real_ref, inv_ref,
    p_ref, chan_ref,
    qs, ks, vs, xv, xc, xy, y_s, spec_s, u_s, o_s,
):
    r = pl.program_id(1)
    length, width = q_ref.shape
    quarter = length // 4
    split, keep = split_ref[r], keep_ref[r]
    tile = 64

    @pl.when(r == 0)
    def _():
        chan_ref[...] = jnp.zeros_like(chan_ref)

    for ref, source in ((qs, q_ref), (ks, k_ref), (vs, v_ref)):
        ref[0:8, :] = jnp.zeros((8, width), F32)

        def widen(i, ref=ref, source=source):
            ref[pl.ds(pl.multiple_of(8 + i * tile, 8), tile), :] = source[rows_of(i, tile), :].astype(F32)

        loop(length // tile, widen)

    o_s[0:length, 0:width] = mm_t(low_ref[...], wo_ref[...])

    def conv(i):
        t = i * tile
        rows = rows_of(i, tile)
        kept = t + lax.broadcasted_iota(jnp.int32, (tile, width), 0) < keep
        gated_grad = o_s[rows, 0:width]
        low = (gated_grad * conv_back(qs, t, tile, fq_ref, split)).astype(BF)
        xy[rows, :] = low
        value = jnp.where(kept, conv_back(vs, t, tile, fv_ref, split), 0.0).astype(BF)
        xv[rows, :] = value
        xc[rows, :] = jnp.where(kept, conv_back(ks, t, tile, fk_ref, split), 0.0).astype(BF)
        chan_ref[2, :, :] += eight_sum(low.astype(F32) * value.astype(F32))

    loop(length // tile, conv)
    butterfly(xv, y_s, 0, width, quarter)
    butterfly(xc, y_s, width, width, quarter)
    butterfly(xy, y_s, 2 * width, width, quarter)

    def query(i):
        rows = rows_of(i, tile)
        qs[rows, :] = o_s[rows, 0:width] * mixed_ref[rows, :].astype(F32)

    loop(length // tile, query)
    blockwise(y_s, spec_s, fwd_real_ref, fwd_ref, quarter)

    def bins(re, im, first):
        n = 16
        re, im = pl.ds(pl.multiple_of(re, n), n), pl.ds(pl.multiple_of(im, n), n)
        vr, vi = spec_s[re, 0:width], spec_s[im, 0:width]
        cr, ci = spec_s[re, width : 2 * width], spec_s[im, width : 2 * width]
        yr, yi = spec_s[re, 2 * width : 3 * width], spec_s[im, 2 * width : 3 * width]
        slope, shift = slope_ref[...], shift_ref[...]
        rr, ii = cr * cr, ci * ci
        if first:
            edge = lax.broadcasted_iota(jnp.int32, (n, width), 0) == 0
            pr, pi = jnp.where(edge, rr, rr + ii), jnp.where(edge, ii, rr + ii)
            gr, gi = jax.nn.sigmoid(slope * pr + shift), jax.nn.sigmoid(slope * pi + shift)
            ar = vr * yr + jnp.where(edge, 0.0, vi * yi)
            ai = jnp.where(edge, -vi * yi, vi * yr - vr * yi)
            br = ar * cr - jnp.where(edge, 0.0, ai * ci)
            bi = jnp.where(edge, -ai * ci, br)
            wr, wi = br * gr * (1.0 - gr), bi * gi * (1.0 - gi)
            ws = jnp.where(edge, 0.5 * (wr + wi), wr)
            wp = jnp.where(edge, 0.5 * (wr * pr + wi * pi), wr * pr)
            hr, hi = gr * cr, gi * ci
            er = hr * yr + jnp.where(edge, 0.0, hi * yi)
            ei = jnp.where(edge, hi * yi, hr * yi - hi * yr)
            dr = gr * ar + 2.0 * slope * wr * cr
            di = 2.0 * slope * wi * ci - gi * ai
        else:
            p = rr + ii
            g = jax.nn.sigmoid(slope * p + shift)
            ar, ai = vr * yr + vi * yi, vi * yr - vr * yi
            ws = (ar * cr - ai * ci) * (g * (1.0 - g))
            wp = ws * p
            hr, hi = g * cr, g * ci
            er, ei = hr * yr + hi * yi, hr * yi - hi * yr
            k = 2.0 * slope * ws
            dr, di = g * ar + k * cr, k * ci - g * ai
        chan_ref[0, :, :] += eight_sum(wp)
        chan_ref[1, :, :] += eight_sum(ws)
        u_s[re, 0:width] = er.astype(BF)
        u_s[im, 0:width] = ei.astype(BF)
        u_s[re, width : 2 * width] = dr.astype(BF)
        u_s[im, width : 2 * width] = di.astype(BF)

    each_bin(quarter, bins)
    resynth(u_s, o_s, inv_real_ref, inv_ref, quarter)

    def finish(i):
        n = 32
        value = recombine(o_s, slice(0, width), i, n, quarter)
        cond = recombine(o_s, slice(width, 2 * width), i, n, quarter)
        for k in range(4):
            rows = pl.ds(pl.multiple_of(k * quarter + i * n, n), n)
            kept = k * quarter + i * n + lax.broadcasted_iota(jnp.int32, (n, width), 0) < keep
            grad = (value[k] + skip_ref[...] * xy[rows, :].astype(F32)).astype(BF).astype(F32)
            vs[rows, :] = jnp.where(kept, grad, 0.0)
            ks[rows, :] = jnp.where(kept, cond[k].astype(BF).astype(F32), 0.0)

    loop(quarter // 32, finish)
    for ref in (qs, ks, vs):
        ref[length : length + 8, :] = jnp.zeros((8, width), F32)

    for slot, (ref, source, f_ref) in enumerate(((qs, q_ref, fq_ref), (vs, v_ref, fv_ref), (ks, k_ref, fk_ref))):

        def adjoint(i, slot=slot, ref=ref, source=source, f_ref=f_ref):
            t = i * tile
            rows = rows_of(i, tile)
            block = ref[pl.ds(pl.multiple_of(t, tile), tile + 8), :]
            position = t + lax.broadcasted_iota(jnp.int32, (tile, width), 0)
            g0 = block[0:tile]
            g1 = jnp.where(position + 1 != split, block[1 : tile + 1], 0.0)
            g2 = jnp.where((position + 2 != split) & (position + 1 != split), block[2 : tile + 2], 0.0)
            s = source[rows, :].astype(F32)
            place = slice((0, 2, 1)[slot] * width, ((0, 2, 1)[slot] + 1) * width)
            p_ref[rows, place] = (f_ref[0:1, :] * g0 + f_ref[1:2, :] * g1 + f_ref[2:3, :] * g2).astype(BF)
            for k, g in enumerate((g0, g1, g2)):
                chan_ref[3 + 3 * slot + k, :, :] += eight_sum(g * s)

        loop(length // tile, adjoint)


def mixer_backward(branch_low, split, keep, q, k, v, mixed, proj_out, short_filter, cond_filter, slope, shift, skip, tables, width=256):
    rows, length, model = q.shape
    blocks = model // width
    shape = jax.ShapeDtypeStruct
    pad = pltpu.VMEM((length + 8, width), F32)
    quarter = length // 4
    row = pl.BlockSpec((None, length, model), lambda j, r, *_: (r, 0, 0))
    part = pl.BlockSpec((None, length, width), lambda j, r, *_: (r, 0, j))

    def columns(size, offset):
        return pl.BlockSpec((size, width), lambda j, r, *_: (0, j + offset * blocks))

    fixed = lambda j, r, *_: (0, 0)
    table_specs = [once((2 * quarter, quarter), fixed), once((6 * quarter, 2 * quarter), fixed)] * 2
    one = columns(1, 0)
    flops = rows * (2 * length * model * model + 2 * 5 * model * (2 * length) * length // 2)
    return pl.pallas_call(
        mixer_backward_kernel,
        out_shape=[shape((rows, length, 3 * model), BF), shape((12, 8, model), F32)],
        grid_spec=pltpu.PrefetchScalarGridSpec(
            num_scalar_prefetch=2,
            grid=(blocks, rows),
            in_specs=[row, part, part, part, part, pl.BlockSpec((width, model), lambda j, r, *_: (j, 0)), columns(3, 0), columns(3, 1), columns(3, 0), one, one, one] + table_specs,
            out_specs=[pl.BlockSpec((None, length, 3 * width), lambda j, r, *_: (r, 0, j)), pl.BlockSpec((12, 8, width), lambda j, r, *_: (0, 0, j))],
            scratch_shapes=[pad, pad, pad] + [pltpu.VMEM((length, width), BF)] * 3 + [
                pltpu.VMEM((2 * length, 3 * width), BF),
                pltpu.VMEM((2 * length, 3 * width), F32),
                pltpu.VMEM((2 * length, 2 * width), BF),
                pltpu.VMEM((2 * length, 2 * width), F32),
            ],
        ),
        compiler_params=pltpu.CompilerParams(dimension_semantics=("arbitrary", "arbitrary"), vmem_limit_bytes=LIMIT),
        cost_estimate=pl.CostEstimate(flops=flops, bytes_accessed=rows * length * (model * 2 * blocks + model * 14), transcendentals=rows * length * model),
        name="mixer_backward",
    )(split, keep, branch_low, q, k, v, mixed, proj_out, short_filter, short_filter, cond_filter, slope, shift, skip, *tables)


def input_back_kernel(width, x_ref, grad_ref, gain_ref, w_ref, p_ref, in_grad_ref, gain_grad_ref, acc):
    model = x_ref.shape[1]
    tile = 64

    @pl.when(pl.program_id(0) == 0)
    def _():
        gain_grad_ref[...] = jnp.zeros_like(gain_grad_ref)

    total = None
    for b in range(model // width):
        for k in range(3):
            place = (3 * b + k) * width
            term = mm_t(p_ref[:, place : place + width], w_ref[:, k * model + b * width : k * model + (b + 1) * width])
            total = term if total is None else total + term
    acc[...] = total

    def body(i):
        rows = rows_of(i, tile)
        n, scale = norm_stats(x_ref[rows, :].astype(F32))
        u = acc[rows, :]
        ug = u * gain_ref[...]
        part = ug - jnp.mean(ug, axis=-1, keepdims=True) - n * jnp.mean(ug * n, axis=-1, keepdims=True)
        in_grad_ref[rows, :] = (grad_ref[rows, :] + scale * part).astype(in_grad_ref.dtype)
        gain_grad_ref[...] += eight_sum(u * n)

    loop(x_ref.shape[0] // tile, body)


def input_back(x, resid_grad, gain, proj_in, proj_grad, width, tile=512):
    tokens, model = x.shape
    shape = jax.ShapeDtypeStruct
    block = pl.BlockSpec((tile, model), lambda i: (i, 0))
    return pl.pallas_call(
        functools.partial(input_back_kernel, width),
        out_shape=[shape((tokens, model), BF), shape((8, model), F32)],
        grid=(tokens // tile,),
        in_specs=[block, block, once((1, model), lambda i: (0, 0)), once((model, 3 * model), lambda i: (0, 0)), pl.BlockSpec((tile, 3 * model), lambda i: (i, 0))],
        out_specs=[block, pl.BlockSpec((8, model), lambda i: (0, 0))],
        scratch_shapes=[pltpu.VMEM((tile, model), F32)],
        compiler_params=pltpu.CompilerParams(dimension_semantics=("arbitrary",), vmem_limit_bytes=LIMIT),
        cost_estimate=pl.CostEstimate(flops=6 * tokens * model * model, bytes_accessed=tokens * model * 14, transcendentals=tokens),
        name="input_back",
    )(x, resid_grad, gain, proj_in, proj_grad)


def turn(a, b):
    return lax.dot_general(a, b, (((0,), (0,)), ((), ())), preferred_element_type=F32).astype(BF)


def after(value, earlier):
    return lax.optimization_barrier((value, earlier))[0]


def exchange_sum_kernel(rows, seq, x_ref, out_ref, slots, total, send_sem, recv_sem):
    r, s = lax.axis_index("rows"), lax.axis_index("seq")
    partners = []
    bit = 1
    while bit < rows:
        partners.append((r + bit - 2 * bit * (lax.rem(r // bit, 2)), s))
        bit *= 2
    bit = 1
    while bit < seq:
        partners.append((r, s + bit - 2 * bit * (lax.rem(s // bit, 2))))
        bit *= 2
    barrier = pltpu.get_barrier_semaphore()
    for partner in partners:
        pl.semaphore_signal(barrier, inc=1, device_id=partner, device_id_type=pl.DeviceIdType.MESH)
    pl.semaphore_wait(barrier, len(partners))
    total[0] = x_ref[...]
    for step, partner in enumerate(partners):
        copy = pltpu.make_async_remote_copy(
            src_ref=total.at[step], dst_ref=slots.at[step], send_sem=send_sem.at[step], recv_sem=recv_sem.at[step],
            device_id=partner, device_id_type=pl.DeviceIdType.MESH,
        )
        copy.start()
        copy.wait()
        total[step + 1] = total[step] + slots[step]
    out_ref[...] = total[len(partners)]


def power_of_two(n):
    return n & (n - 1) == 0


def exchange_sum(value):
    rows, seq = lax.axis_size("rows"), lax.axis_size("seq")
    if not (power_of_two(rows) and power_of_two(seq)):
        return lax.psum(value, ("rows", "seq"))
    steps = (rows.bit_length() - 1) + (seq.bit_length() - 1)
    return pl.pallas_call(
        functools.partial(exchange_sum_kernel, rows, seq),
        out_shape=jax.ShapeDtypeStruct(value.shape, value.dtype),
        in_specs=[pl.BlockSpec(memory_space=pltpu.VMEM)],
        out_specs=pl.BlockSpec(memory_space=pltpu.VMEM),
        scratch_shapes=[
            pltpu.VMEM((steps, *value.shape), value.dtype),
            pltpu.VMEM((steps + 1, *value.shape), value.dtype),
            pltpu.SemaphoreType.DMA((steps,)),
            pltpu.SemaphoreType.DMA((steps,)),
        ],
        compiler_params=pltpu.CompilerParams(collective_id=7, has_side_effects=True),
        name="exchange_sum",
    )(value)


def swapped(value):
    count = lax.axis_size("seq")
    return lax.ppermute(value, "seq", [(i, (i + 1) % count) for i in range(count)])


def gather_rows(value):
    if lax.axis_size("seq") != 2:
        return lax.all_to_all(value, "seq", split_axis=0, concat_axis=1, tiled=True)
    s = lax.axis_index("seq")
    own = value.shape[0] // 2
    mine = lax.dynamic_slice_in_dim(value, s * own, own)
    other = swapped(lax.dynamic_slice_in_dim(value, (1 - s) * own, own))
    return jnp.concatenate([jnp.where(s == 0, mine, other), jnp.where(s == 0, other, mine)], axis=1)


def scatter_rows(value):
    if lax.axis_size("seq") != 2:
        return lax.all_to_all(value, "seq", split_axis=1, concat_axis=0, tiled=True)
    s = lax.axis_index("seq")
    part = value.shape[1] // 2
    mine = lax.dynamic_slice_in_dim(value, s * part, part, axis=1)
    other = swapped(lax.dynamic_slice_in_dim(value, (1 - s) * part, part, axis=1))
    return jnp.concatenate([jnp.where(s == 0, mine, other), jnp.where(s == 0, other, mine)], axis=0)


def seq_sum(value):
    if lax.axis_size("seq") != 2:
        return lax.psum(value, "seq").astype(F32)
    return value.astype(F32) + swapped(value).astype(F32)


def per_device_rows(inputs, split_point, keep_mask, norm_gain, proj_in, short_filter, cond_filter, spec_slope, spec_shift, skip_gain, proj_out, ffn_gain, ffn_in, ffn_out, out_grad):
    local_rows, local_len, model = inputs.shape
    count = lax.axis_size("seq")
    own = local_rows // count
    length = local_len * count
    tokens = own * length
    width = 256
    first_row = lax.axis_index("seq") * own
    flat = lambda a: a.reshape(tokens, model)
    flat_wide = lambda a: a.reshape(tokens, 3 * model)
    shaped = lambda a: a.reshape(own, length, model)
    lift = lambda a: a.reshape(1, -1)

    x = gather_rows(inputs)
    kept = jnp.sum(keep_mask, axis=1)
    kept = kept + swapped(kept) if count == 2 else lax.psum(kept, "seq")
    keep = lax.dynamic_slice_in_dim(kept, first_row, own)
    split = lax.dynamic_slice_in_dim(split_point, first_row, own)
    whole_grad = flat(gather_rows(after(out_grad, x)))
    tables = spectral_tables(length, lax.axis_index("seq") * (2 * length))
    slope, shift, skip = lift(spec_slope), lift(spec_shift), lift(skip_gain)

    first, q, k, v, mixed, gated, resid, second = mixer_forward(
        x, split, keep, lift(norm_gain), proj_in, short_filter, cond_filter, slope, shift, skip, proj_out, lift(ffn_gain), tables
    )
    second = flat(second)
    second_turned, grad_turned = second.T, whole_grad.T
    pieces = 2
    totals, backs, grads = [], [], []
    for piece in range(pieces):
        total, back, grad = ffn_both(second, whole_grad, second_turned, grad_turned, ffn_in, ffn_out, piece, pieces)
        totals.append(total)
        backs.append(back)
        grads.append(grad)
    chain = lax.psum_scatter(grads[0], "rows", scatter_dimension=1, tiled=True)
    ffn_shares = [chain]
    output, resid_grad, branch_low, ffn_gain_part = norm_back(flat(resid), totals, backs, whole_grad, lift(ffn_gain))
    output = scatter_rows(shaped(output))
    out_part = turn(flat(gated), branch_low)
    for grad in grads[1:]:
        grad, chain, branch_low = lax.optimization_barrier((grad, chain, branch_low))
        chain = lax.psum_scatter(grad, "rows", scatter_dimension=1, tiled=True)
        ffn_shares.append(chain)
    proj_grad, chan = mixer_backward(shaped(branch_low), split, keep, q, k, v, mixed, proj_out, short_filter, cond_filter, slope, shift, skip, tables)
    proj_grad = flat_wide(proj_grad)
    mix_part = jnp.concatenate([out_part, turn(flat(first), proj_grad)], axis=1)
    mix_part, *ffn_shares = lax.optimization_barrier((mix_part, *ffn_shares))
    mix_share = lax.psum_scatter(mix_part, "rows", scatter_dimension=0, tiled=True)
    proj_grad = after(proj_grad, mix_part)
    input_grad, norm_gain_part = input_back(flat(x), resid_grad, lift(norm_gain), proj_in, proj_grad, width)
    input_grad = scatter_rows(shaped(input_grad)).astype(F32)
    ffn_shares = [seq_sum(share) for share in ffn_shares]
    small = jnp.sum(jnp.concatenate([ffn_gain_part[None], norm_gain_part[None], chan], 0), axis=1)
    small = exchange_sum(small)
    scale = 1.0 / length
    mix_share = seq_sum(mix_share)
    in_share = mix_share[:, model:].reshape(-1, model // width, 3, width).transpose(0, 2, 1, 3)
    return (
        output,
        input_grad,
        small[1],
        in_share.reshape(-1, 3 * model),
        jnp.concatenate([small[5:8], small[8:11]], axis=1),
        small[11:14],
        small[2] * scale,
        small[3] * scale,
        small[4],
        mix_share[:, :model],
        small[0],
        jnp.concatenate([share[k] for k in range(2) for share in ffn_shares], axis=1),
        jnp.concatenate([share[2] for share in ffn_shares], axis=1).T,
    )


PRECISE = lax.Precision.HIGH


def passed_along(value, axis, steps):
    count = lax.axis_size(axis)
    leading, last = (max(0, -steps), min(count, count - steps))
    return lax.ppermute(value, axis, [(source, source + steps) for source in range(leading, last)])


def layer_norm(values, scaling):
    center = values - jnp.mean(values, axis=-1, keepdims=True)
    spread = jnp.mean(center * center, axis=-1, keepdims=True)
    return center * lax.rsqrt(spread + EPSILON) * scaling


def conv_three(extended, weights, same_one, same_two):
    length = extended.shape[1] - 2
    return (
        weights[0] * extended[:, 2:]
        + weights[1] * extended[:, 1 : length + 1] * same_one
        + weights[2] * extended[:, :length] * same_two
    )


def dft_tables(seq_length):
    table_shape = (seq_length + 1, seq_length)
    product = lax.broadcasted_iota(jnp.int32, table_shape, 0) * lax.broadcasted_iota(
        jnp.int32, table_shape, 1
    )
    angles = (product % (2 * seq_length)).astype(jnp.float32) * (math.pi / seq_length)
    freq = lax.broadcasted_iota(jnp.int32, (seq_length + 1, 1), 0)
    edge = jnp.logical_or(freq == 0, freq == seq_length)
    weights = jnp.where(edge, 1.0, 2.0).astype(jnp.float32) / (2.0 * seq_length)
    return (jnp.cos(angles), jnp.sin(angles), weights)


def analyze(values, conds, cos_table, sin_table):
    value_real = jnp.einsum("ft,ktd->kfd", cos_table, values, precision=PRECISE)
    value_imag = -jnp.einsum("ft,ktd->kfd", sin_table, values, precision=PRECISE)
    cond_real = jnp.einsum("ft,ktd->kfd", cos_table, conds, precision=PRECISE)
    cond_imag = -jnp.einsum("ft,ktd->kfd", sin_table, conds, precision=PRECISE)
    return (value_real, value_imag, cond_real, cond_imag)


def synth(
    value_real,
    value_imag,
    cond_real,
    cond_imag,
    values,
    slopes,
    shifts,
    skip_gains,
    cos_table,
    sin_table,
    freq_weights,
):
    factor = jax.nn.sigmoid(slopes * (cond_real * cond_real + cond_imag * cond_imag) + shifts)
    filter_real = cond_real * factor
    filter_imag = cond_imag * factor
    prod_real = (value_real * filter_real - value_imag * filter_imag) * freq_weights
    prod_imag = (value_real * filter_imag + value_imag * filter_real) * freq_weights
    mixed_out = jnp.einsum("ft,kfd->ktd", cos_table, prod_real, precision=PRECISE) - jnp.einsum(
        "ft,kfd->ktd", sin_table, prod_imag, precision=PRECISE
    )
    return mixed_out + skip_gains * values


def times_transpose(left, right):
    return lax.dot_general(
        left, right, (((1,), (1,)), ((), ())), preferred_element_type=jnp.float32
    )


def transpose_times(left, right):
    return lax.dot_general(
        left, right, (((0,), (0,)), ((), ())), preferred_element_type=jnp.float32
    )


def per_device(
    inputs,
    split_point,
    keep_mask,
    norm_gain,
    proj_in,
    short_filter,
    cond_filter,
    spec_slope,
    spec_shift,
    skip_gain,
    proj_out,
    ffn_gain,
    ffn_in,
    ffn_out,
    out_grad,
):
    local_rows, local_len, model_width = inputs.shape
    hidden_width = ffn_out.shape[0]
    seq_count = lax.axis_size("seq")
    seq_index = lax.axis_index("seq")
    full_len = local_len * seq_count
    chan_width = model_width // seq_count
    token_count = local_rows * local_len
    positions = seq_index * local_len + lax.broadcasted_iota(jnp.int32, (local_rows, local_len), 1)
    splits = split_point[:, None]
    segment = positions >= splits
    same_one = (segment == (positions - 1 >= splits)).astype(jnp.float32)[:, :, None]
    same_two = (segment == (positions - 2 >= splits)).astype(jnp.float32)[:, :, None]
    keep_float = keep_mask.astype(jnp.float32)[:, :, None]
    flat_in = inputs.reshape(token_count, model_width).astype(jnp.float32)
    normed_one, norm_one_back = jax.vjp(layer_norm, flat_in, norm_gain)
    first_act = normed_one.astype(jnp.bfloat16)
    projected = jnp.dot(first_act, proj_in, preferred_element_type=jnp.float32).astype(jnp.bfloat16)
    proj_rows = projected.reshape(local_rows, local_len, 3 * model_width)
    edge_values = passed_along(proj_rows[:, local_len - 2 :, :], "seq", 1)
    extended = jnp.concatenate([edge_values, proj_rows], axis=1).astype(jnp.float32)

    def mixer_local(ext_values, short_weights, cond_weights):
        query_value = jnp.concatenate(
            [ext_values[:, :, :model_width], ext_values[:, :, 2 * model_width :]], axis=2
        )
        conv_both = conv_three(query_value, short_weights, same_one, same_two)
        cond_conv = conv_three(
            ext_values[:, :, model_width : 2 * model_width], cond_weights, same_one, same_two
        )
        return (
            conv_both[:, :, :model_width],
            conv_both[:, :, model_width:] * keep_float,
            cond_conv * keep_float,
        )

    (query_conv, value_masked, cond_masked), mixer_back = jax.vjp(
        mixer_local, extended, short_filter, cond_filter
    )
    value_low = value_masked.astype(jnp.bfloat16)
    cond_low = cond_masked.astype(jnp.bfloat16)
    slope_part = lax.dynamic_slice_in_dim(spec_slope, seq_index * chan_width, chan_width)
    shift_part = lax.dynamic_slice_in_dim(spec_shift, seq_index * chan_width, chan_width)
    skip_part = lax.dynamic_slice_in_dim(skip_gain, seq_index * chan_width, chan_width)
    cos_table, sin_table, freq_weights = dft_tables(full_len)

    def synth_local(
        value_real, value_imag, cond_real, cond_imag, values, slopes, shifts, skip_gains
    ):
        return synth(
            value_real,
            value_imag,
            cond_real,
            cond_imag,
            values,
            slopes,
            shifts,
            skip_gains,
            cos_table,
            sin_table,
            freq_weights,
        )

    value_chan = lax.all_to_all(value_low, "seq", split_axis=2, concat_axis=1, tiled=True)
    cond_chan = lax.all_to_all(cond_low, "seq", split_axis=2, concat_axis=1, tiled=True)
    value_float = value_chan.astype(jnp.float32)
    spectra = analyze(value_float, cond_chan.astype(jnp.float32), cos_table, sin_table)
    mixed_chan = synth_local(
        spectra[0],
        spectra[1],
        spectra[2],
        spectra[3],
        value_float,
        slope_part,
        shift_part,
        skip_part,
    ).astype(jnp.bfloat16)
    mixed_home = lax.all_to_all(mixed_chan, "seq", split_axis=1, concat_axis=2, tiled=True)
    mixed_float = mixed_home.astype(jnp.float32)
    gated = (query_conv * mixed_float).astype(jnp.bfloat16).reshape(token_count, model_width)
    branch = jnp.dot(gated, proj_out, preferred_element_type=jnp.float32)
    resid = flat_in + branch
    normed_two, norm_two_back = jax.vjp(layer_norm, resid, ffn_gain)
    second_act = normed_two.astype(jnp.bfloat16)
    gate_up = jnp.dot(second_act, ffn_in, preferred_element_type=jnp.float32)

    def glu_local(both_parts):
        return (
            jax.nn.gelu(both_parts[:, :hidden_width], approximate=False)
            * both_parts[:, hidden_width:]
        )

    hidden, glu_back = jax.vjp(glu_local, gate_up)
    hidden_low = hidden.astype(jnp.bfloat16)
    result = resid + jnp.dot(hidden_low, ffn_out, preferred_element_type=jnp.float32)
    output = result.astype(jnp.bfloat16).reshape(local_rows, local_len, model_width)
    flat_grad = out_grad.reshape(token_count, model_width)
    hidden_grad = times_transpose(flat_grad, ffn_out)
    (gate_up_grad,) = glu_back(hidden_grad)
    gate_up_low = gate_up_grad.astype(jnp.bfloat16)
    second_grad = times_transpose(gate_up_low, ffn_in)
    resid_part, ffn_gain_part = norm_two_back(second_grad)
    resid_grad = flat_grad.astype(jnp.float32) + resid_part
    branch_low = resid_grad.astype(jnp.bfloat16)
    gated_grad = times_transpose(branch_low, proj_out).reshape(local_rows, local_len, model_width)
    query_grad = gated_grad * mixed_float
    mixed_grad = (gated_grad * query_conv).astype(jnp.bfloat16)
    grad_chan = lax.all_to_all(mixed_grad, "seq", split_axis=2, concat_axis=1, tiled=True)
    grad_float = grad_chan.astype(jnp.float32)
    item_count = grad_chan.shape[0]
    slope_items = jnp.broadcast_to(slope_part, (item_count, 1, chan_width))
    shift_items = jnp.broadcast_to(shift_part, (item_count, 1, chan_width))
    skip_items = jnp.broadcast_to(skip_part, (item_count, 1, chan_width))
    value_float = value_chan.astype(jnp.float32)

    def spectral(values, conds, slopes, shifts, skip_gains):
        spectra = analyze(values, conds, cos_table, sin_table)
        return synth_local(
            spectra[0], spectra[1], spectra[2], spectra[3], values, slopes, shifts, skip_gains
        )

    unused, pull = jax.vjp(
        spectral, value_float, cond_chan.astype(jnp.float32), slope_items, shift_items, skip_items
    )
    value_back, cond_back, slope_rows, shift_rows, skip_rows = pull(grad_float)
    value_grad, cond_grad = (
        lax.all_to_all(
            value_back.astype(jnp.bfloat16), "seq", split_axis=1, concat_axis=2, tiled=True
        ),
        lax.all_to_all(
            cond_back.astype(jnp.bfloat16), "seq", split_axis=1, concat_axis=2, tiled=True
        ),
    )
    start_chan = (seq_index * chan_width,)
    empty_width = jnp.zeros((model_width,), jnp.float32)
    slope_full = lax.dynamic_update_slice(empty_width, jnp.sum(slope_rows, axis=(0, 1)), start_chan)
    shift_full = lax.dynamic_update_slice(empty_width, jnp.sum(shift_rows, axis=(0, 1)), start_chan)
    skip_full = lax.dynamic_update_slice(empty_width, jnp.sum(skip_rows, axis=(0, 1)), start_chan)
    ext_grad, short_grad, cond_weight_grad = mixer_back(
        (query_grad, value_grad.astype(jnp.float32), cond_grad.astype(jnp.float32))
    )
    incoming = passed_along(ext_grad[:, :2, :].astype(jnp.bfloat16), "seq", -1).astype(jnp.float32)
    proj_grad = ext_grad[:, 2:, :] + jnp.pad(incoming, ((0, 0), (local_len - 2, 0), (0, 0)))
    proj_low = proj_grad.astype(jnp.bfloat16).reshape(token_count, 3 * model_width)
    first_grad = times_transpose(proj_low, proj_in)
    input_part, norm_gain_part = norm_one_back(first_grad)
    input_grad = (resid_grad + input_part).reshape(local_rows, local_len, model_width)
    share = lax.psum_scatter(
        jnp.concatenate(
            [
                transpose_times(first_act, proj_low),
                transpose_times(gated, branch_low),
                transpose_times(second_act, gate_up_low),
                transpose_times(flat_grad, hidden_low),
            ],
            axis=1,
        ).astype(jnp.bfloat16),
        "rows",
        scatter_dimension=0,
        tiled=True,
    )
    summed = lax.psum(share, "seq").astype(jnp.float32)
    small_sums = lax.psum(
        (
            norm_gain_part,
            short_grad,
            cond_weight_grad,
            slope_full,
            shift_full,
            skip_full,
            ffn_gain_part,
        ),
        ("rows", "seq"),
    )
    proj_in_grad = summed[:, : 3 * model_width]
    proj_out_grad = summed[:, 3 * model_width : 4 * model_width]
    ffn_in_grad = summed[:, 4 * model_width : 4 * model_width + 2 * hidden_width]
    ffn_out_grad = jnp.transpose(summed[:, 4 * model_width + 2 * hidden_width :])
    return (
        output,
        input_grad,
        small_sums[0],
        proj_in_grad,
        small_sums[1],
        small_sums[2],
        small_sums[3],
        small_sums[4],
        small_sums[5],
        proj_out_grad,
        small_sums[6],
        ffn_in_grad,
        ffn_out_grad,
    )


def per_device_any(*args):
    rows, width = args[0].shape[0], args[0].shape[2]
    even = rows % lax.axis_size("seq") == 0 and width % 256 == 0
    return (per_device_rows if even else per_device)(*args)


def solution(mesh):
    in_specs = (
        P("rows", "seq", None),
        P("rows"),
        P("rows", "seq"),
        P(),
        P(),
        P(),
        P(),
        P(),
        P(),
        P(),
        P(),
        P(),
        P(),
        P(),
        P("rows", "seq", None),
    )
    out_specs = (
        P("rows", "seq", None),
        P("rows", "seq", None),
        P(),
        P("rows", None),
        P(),
        P(),
        P(),
        P(),
        P(),
        P("rows", None),
        P(),
        P("rows", None),
        P(None, "rows"),
    )
    return jax.shard_map(
        per_device_any, mesh=mesh, in_specs=in_specs, out_specs=out_specs, check_vma=False
    )
```

```python
import functools
import math

import jax
import jax.numpy as jnp
from jax import lax
from jax.experimental import pallas as pl
from jax.experimental.pallas import tpu as pltpu
from jax.sharding import PartitionSpec as P

EPSILON = 1e-05
BF = jnp.bfloat16
F32 = jnp.float32
ROOT_HALF = math.sqrt(0.5)
LIMIT = 67043328


def mm(a, b):
    return lax.dot_general(a, b, (((1,), (0,)), ((), ())), preferred_element_type=F32)


def mm_t(a, b):
    return lax.dot_general(a, b, (((1,), (1,)), ((), ())), preferred_element_type=F32)


def spectral_tables(length, offset):
    quarter = length // 4
    two_n = 2 * length
    m = lax.broadcasted_iota(jnp.int32, (quarter, quarter), 0)
    s = lax.broadcasted_iota(jnp.int32, (quarter, quarter), 1)

    def cos_sin(freq):
        angle = ((freq * s + offset) % two_n).astype(F32) * (2.0 * math.pi / two_n)
        return jnp.cos(angle), jnp.sin(angle)

    half = quarter // 2
    forward, inverse = [], []
    for r in (1, 2, 3):
        c, sn = cos_sin(8 * m + r)
        forward.append(jnp.concatenate([jnp.concatenate([c, sn], 1), jnp.concatenate([-sn, c], 1)], 0))
        inverse.append(forward[-1].T * (2.0 / two_n))
    row = m % half
    low = m < half
    c, sn = cos_sin(8 * jnp.where(m == half, half, row))
    zero = jnp.where(low | (m == half), c, -sn)
    c4, sn4 = cos_sin(8 * row + 4)
    four = jnp.where(low, c4, -sn4)
    edge = jnp.where((m == 0) | (m == half), 1.0, 2.0) / two_n
    fwd_real = jnp.concatenate([zero, four], 0)
    inv_real = jnp.concatenate([(zero * edge).T, four.T * (2.0 / two_n)], 0)
    return (
        fwd_real.astype(BF),
        jnp.concatenate(forward, 0).astype(BF),
        inv_real.astype(BF),
        jnp.concatenate(inverse, 0).astype(BF),
    )


def loop(count, body):
    lax.fori_loop(0, count, lambda i, c: (body(i), c)[1], 0)


def rows_of(i, size):
    return pl.ds(pl.multiple_of(i * size, size), size)


def norm_stats(v):
    center = v - jnp.mean(v, axis=-1, keepdims=True)
    scale = lax.rsqrt(jnp.mean(center * center, axis=-1, keepdims=True) + EPSILON)
    return center * scale, scale


def same_masks(position, split):
    same_one = position != split
    return same_one, same_one & (position != split + 1)


def butterfly(x_ref, y_ref, lane, width, quarter):
    tile = 32
    lanes = slice(lane, lane + width)

    def body(i):
        x0, x1, x2, x3 = [
            x_ref[pl.ds(pl.multiple_of(q * quarter + i * tile, tile), tile), :].astype(F32) for q in range(4)
        ]
        a, b, c, d = x0 + x2, x1 + x3, x0 - x2, x1 - x3
        sd, sb = d * ROOT_HALF, b * ROOT_HALF
        out = (a + b, a - b, x0 + sd, -x2 - sb, c, -d, x0 - sd, x2 - sb)
        for k, value in enumerate(out):
            y_ref[pl.ds(pl.multiple_of(k * quarter + i * tile, tile), tile), lanes] = value.astype(BF)

    loop(quarter // tile, body)


def blockwise(y_ref, spec_ref, fwd_real_ref, fwd_ref, quarter):
    q = quarter
    for k in range(2):
        spec_ref[k * q : (k + 1) * q, :] = mm(fwd_real_ref[k * q : (k + 1) * q, :], y_ref[k * q : (k + 1) * q, :])
    for k in range(3):
        spec_ref[2 * q + 2 * k * q : 2 * q + 2 * (k + 1) * q, :] = mm(
            fwd_ref[2 * k * q : 2 * (k + 1) * q, :], y_ref[2 * q + 2 * k * q : 2 * q + 2 * (k + 1) * q, :]
        )


def resynth(u_ref, out_ref, inv_real_ref, inv_ref, quarter):
    blockwise(u_ref, out_ref, inv_real_ref, inv_ref, quarter)


def each_bin(quarter, body, tile=16):
    half = quarter // 2
    body(0, half, True)

    def run(base, span, skip):
        def step(i):
            start = base + (i + skip) * tile
            body(start, start + span, False)

        loop(span // tile - skip, step)

    run(0, half, 1)
    run(quarter, half, 0)
    for k in range(3):
        run(2 * quarter + 2 * k * quarter, quarter, 0)


def recombine(o_ref, lanes, i, tile, quarter):
    def part(k):
        return o_ref[pl.ds(pl.multiple_of(k * quarter + i * tile, tile), tile), lanes]

    u0, u4, a1, b1, a2, b2, a3, b3 = [part(k) for k in range(8)]
    even, odd = u0 + u4, u0 - u4
    return (
        even + a1 + a2 + a3,
        odd + (a1 - b1 - a3 - b3) * ROOT_HALF - b2,
        even - b1 - a2 + b3,
        odd + (a3 - b3 - a1 - b1) * ROOT_HALF + b2,
    )


def conv_back(ref, t, tile, weights, split):
    block = ref[pl.ds(pl.multiple_of(t, tile), tile + 8), :]
    width = block.shape[1]
    position = t + lax.broadcasted_iota(jnp.int32, (tile, width), 0)
    one, two = same_masks(position, split)
    return (
        weights[0:1, :] * block[8 : tile + 8]
        + jnp.where(one, weights[1:2, :] * block[7 : tile + 7], 0.0)
        + jnp.where(two, weights[2:3, :] * block[6 : tile + 6], 0.0)
    )


def mixer_forward_kernel(
    first_row, earlier, split_ref, keep_ref, x_ref, norm_gain_ref, wq_ref, wk_ref, wv_ref, fq_ref, fv_ref, fk_ref, slope_ref, shift_ref,
    skip_ref, wo_ref, ffn_gain_ref, fwd_real_ref, fwd_ref, inv_real_ref, inv_ref,
    *refs,
):
    first_ref, q_ref, k_ref, v_ref, mixed_ref, gated_ref, resid_ref, second_ref = refs[earlier : earlier + 8]
    qs, ks, vs, xv, xc, y_s, spec_s, u_s, o_s, qc = refs[earlier + 8 :]
    r, j = first_row + pl.program_id(0), pl.program_id(1)
    length, width = q_ref.shape
    quarter = length // 4
    split, keep = split_ref[r], keep_ref[r]
    tile = 64

    @pl.when(j == 0)
    def _():
        def body(i):
            rows = rows_of(i, tile)
            v = x_ref[rows, :].astype(F32)
            n, _ = norm_stats(v)
            first_ref[rows, :] = (n * norm_gain_ref[...]).astype(BF)
            resid_ref[rows, :] = v

        loop(length // tile, body)
        for ref in (qs, ks, vs):
            ref[0:8, :] = jnp.zeros((8, width), F32)

    for w_ref, out_ref, ref in ((wq_ref, q_ref, qs), (wk_ref, k_ref, ks), (wv_ref, v_ref, vs)):
        value = mm(first_ref[...], w_ref[...]).astype(BF)
        out_ref[...] = value
        ref[8 : 8 + length, :] = value.astype(F32)

    def conv(i):
        t = i * tile
        rows = rows_of(i, tile)
        kept = t + lax.broadcasted_iota(jnp.int32, (tile, width), 0) < keep
        qc[rows, :] = conv_back(qs, t, tile, fq_ref, split)
        xv[rows, :] = jnp.where(kept, conv_back(vs, t, tile, fv_ref, split), 0.0).astype(BF)
        xc[rows, :] = jnp.where(kept, conv_back(ks, t, tile, fk_ref, split), 0.0).astype(BF)

    loop(length // tile, conv)
    butterfly(xv, y_s, 0, width, quarter)
    butterfly(xc, y_s, width, width, quarter)
    blockwise(y_s, spec_s, fwd_real_ref, fwd_ref, quarter)

    def bins(re, im, first):
        n = 16
        re, im = pl.ds(pl.multiple_of(re, n), n), pl.ds(pl.multiple_of(im, n), n)
        vr, vi = spec_s[re, 0:width], spec_s[im, 0:width]
        cr, ci = spec_s[re, width : 2 * width], spec_s[im, width : 2 * width]
        slope, shift = slope_ref[...], shift_ref[...]
        rr, ii = cr * cr, ci * ci
        if first:
            edge = lax.broadcasted_iota(jnp.int32, (n, width), 0) == 0
            hr = cr * jax.nn.sigmoid(slope * jnp.where(edge, rr, rr + ii) + shift)
            hi = ci * jax.nn.sigmoid(slope * jnp.where(edge, ii, rr + ii) + shift)
            ur = vr * hr - jnp.where(edge, 0.0, vi * hi)
            ui = jnp.where(edge, vi * hi, vr * hi + vi * hr)
        else:
            gain = jax.nn.sigmoid(slope * (rr + ii) + shift)
            hr, hi = cr * gain, ci * gain
            ur, ui = vr * hr - vi * hi, vr * hi + vi * hr
        u_s[re, :] = ur.astype(BF)
        u_s[im, :] = ui.astype(BF)

    each_bin(quarter, bins)
    resynth(u_s, o_s, inv_real_ref, inv_ref, quarter)

    def finish(i):
        n = 32
        parts = recombine(o_s, slice(0, width), i, n, quarter)
        for k, part in enumerate(parts):
            rows = pl.ds(pl.multiple_of(k * quarter + i * n, n), n)
            mixed = (part + skip_ref[...] * xv[rows, :].astype(F32)).astype(BF)
            mixed_ref[rows, :] = mixed
            gated_ref[rows, :] = (qc[rows, :] * mixed.astype(F32)).astype(BF)

    loop(quarter // 32, finish)
    resid_ref[...] += mm(gated_ref[...], wo_ref[...])

    @pl.when(j == pl.num_programs(1) - 1)
    def _():
        def body(i):
            rows = rows_of(i, tile)
            n, _ = norm_stats(resid_ref[rows, :])
            second_ref[rows, :] = (n * ffn_gain_ref[...]).astype(BF)

        loop(length // tile, body)


def once(shape, index):
    return pl.BlockSpec(shape, index, pipeline_mode=pl.Buffered(1))


def mixer_specs(length, model, width, first_row):
    blocks = model // width
    row = pl.BlockSpec((None, length, model), lambda r, j, *_: (r + first_row, 0, 0))
    part = pl.BlockSpec((None, length, width), lambda r, j, *_: (r + first_row, 0, j))

    def columns(rows, offset):
        return pl.BlockSpec((rows, width), lambda r, j, *_: (0, j + offset * blocks))

    out_rows = pl.BlockSpec((width, model), lambda r, j, *_: (j, 0))
    gain = once((1, model), lambda r, j, *_: (0, 0))
    q = length // 4
    tables = [once((2 * q, q), lambda r, j, *_: (0, 0)), once((6 * q, 2 * q), lambda r, j, *_: (0, 0))]
    return blocks, row, part, columns, out_rows, gain, tables + tables


def mixer_forward(x, split, keep, norm_gain, proj_in, short_filter, cond_filter, slope, shift, skip, proj_out, ffn_gain, tables, first_row, total_rows, earlier, width=256):
    rows, length, model = x.shape
    blocks, row, part, columns, out_rows, gain, table_specs = mixer_specs(length, model, width, first_row)
    x_row = pl.BlockSpec((None, length, model), lambda r, j, *_: (r, 0, 0))
    one = columns(1, 0)
    shape = jax.ShapeDtypeStruct
    low, full = shape((total_rows, length, model), BF), shape((total_rows, length, model), F32)
    pad = pltpu.VMEM((length + 8, width), F32)
    flops = rows * (2 * length * model * (3 * model + model) + 2 * 3 * model * (2 * length) * length // 2)
    operands = (split, keep, x, norm_gain, proj_in, proj_in, proj_in, short_filter, short_filter, cond_filter, slope, shift, skip, proj_out, ffn_gain, *tables)
    return pl.pallas_call(
        functools.partial(mixer_forward_kernel, first_row, len(earlier)),
        out_shape=[low, low, low, low, low, low, full, low],
        grid_spec=pltpu.PrefetchScalarGridSpec(
            num_scalar_prefetch=2,
            grid=(rows, blocks),
            in_specs=[x_row, gain, columns(model, 0), columns(model, 1), columns(model, 2), columns(3, 0), columns(3, 1), columns(3, 0), one, one, one, out_rows, gain] + table_specs + [pl.BlockSpec(memory_space=pl.ANY)] * len(earlier),
            out_specs=[row, part, part, part, part, part, row, row],
            scratch_shapes=[pad, pad, pad] + [pltpu.VMEM((length, width), BF)] * 2 + [
                pltpu.VMEM((2 * length, 2 * width), BF),
                pltpu.VMEM((2 * length, 2 * width), F32),
                pltpu.VMEM((2 * length, width), BF),
                pltpu.VMEM((2 * length, width), F32),
                pltpu.VMEM((length, width), F32),
            ],
        ),
        compiler_params=pltpu.CompilerParams(dimension_semantics=("arbitrary", "arbitrary"), vmem_limit_bytes=LIMIT),
        cost_estimate=pl.CostEstimate(flops=flops, bytes_accessed=rows * length * model * 20, transcendentals=rows * length * model),
        input_output_aliases={len(operands) + k: k for k in range(len(earlier))},
        name="mixer_forward",
    )(*operands, *earlier)


def normal_cdf_pdf(x):
    z = jnp.abs(x) * ROOT_HALF
    t = 1.0 / (1.0 + 0.3275911 * z)
    e = jnp.exp(-z * z)
    poly = t * (0.127414796 + t * (-0.142248368 + t * (0.7107068705 + t * (-0.7265760135 + t * 0.5307027145))))
    tail = poly * e
    return jnp.where(x >= 0, 1.0 - tail, tail), x * e * (1.0 / math.sqrt(2.0 * math.pi))


def ffn_kernel(
    sa_ref, og_ref, sat_ref, ogt_ref, wg_ref, wu_ref, wo_ref, out_ref, back_ref, grads_ref, *scratch
):
    j = pl.program_id(0)
    tokens, model = sa_ref.shape
    streams = [scratch[6 * n : 6 * n + 6] for n in range(2)]
    tile = streams[0][0].shape[0]
    half = tokens // 2
    steps = half // tile
    chunk = 32

    @pl.when(j == 0)
    def _():
        def body(i):
            out_ref[rows_of(i, tile), :] = jnp.zeros((tile, model), F32)
            back_ref[rows_of(i, tile), :] = jnp.zeros((tile, model), F32)

        loop(tokens // tile, body)

    def place(n, i, size=tile, offset=0):
        return pl.ds(pl.multiple_of(n * half + i * tile + offset, size), size)

    def products(n, i):
        gs, us, ds = streams[n][:3]
        rows = place(n, i)
        sa = sa_ref[rows, :]
        gs[...] = mm(sa, wg_ref[...])
        us[...] = mm(sa, wu_ref[...])
        ds[...] = mm_t(og_ref[rows, :], wo_ref[...])

    def elementwise(n, i):
        gs, us, ds, hid, gg, ug = streams[n]
        for c in range(tile // chunk):
            part = slice(c * chunk, (c + 1) * chunk)
            gate, up, dh = gs[part, :], us[part, :], ds[part, :]
            cdf, xpdf = normal_cdf_pdf(gate)
            act = gate * cdf
            target = place(0, i, chunk, c * chunk)
            hid[target, :] = (act * up).astype(BF)
            gg[target, :] = (dh * up * (cdf + xpdf)).astype(BF)
            ug[target, :] = (dh * act).astype(BF)

    def sums(n, i):
        hid, gg, ug = streams[n][3:]
        rows, source = place(n, i), place(0, i)
        out_ref[rows, :] += mm(hid[source, :], wo_ref[...])
        back_ref[rows, :] += mm_t(gg[source, :], wg_ref[...]) + mm_t(ug[source, :], wu_ref[...])

    products(0, 0)
    products(1, 0)
    elementwise(0, 0)

    def body(i):
        products(0, i + 1)
        sums(0, i)
        elementwise(1, i)
        products(1, i + 1)
        sums(1, i)
        elementwise(0, i + 1)

    loop(steps - 1, body)
    last = steps - 1
    sums(0, last)
    elementwise(1, last)
    sums(1, last)
    (hid0, gg0, ug0), (hid1, gg1, ug1) = streams[0][3:], streams[1][3:]
    for k, (ref, first, second) in enumerate(((sat_ref, gg0, gg1), (sat_ref, ug0, ug1), (ogt_ref, hid0, hid1))):
        grads_ref[k] = (mm(ref[:, 0:half], first[...]) + mm(ref[:, half:tokens], second[...])).astype(BF)


def ffn_both(second_act, out_grad, second_turned, grad_turned, ffn_in, ffn_out, piece, pieces, width=512, tile=512):
    tokens, model = second_act.shape
    total_blocks = ffn_out.shape[0] // width
    blocks = total_blocks // pieces
    first = piece * blocks
    hidden = blocks * width
    shape = jax.ShapeDtypeStruct
    whole = once((tokens, model), lambda j: (0, 0))
    turned = once((model, tokens), lambda j: (0, 0))
    return pl.pallas_call(
        ffn_kernel,
        out_shape=[shape((tokens, model), F32), shape((tokens, model), F32), shape((3, model, hidden), BF)],
        grid=(blocks,),
        in_specs=[
            whole, whole, turned, turned,
            pl.BlockSpec((model, width), lambda j: (0, j + first)),
            pl.BlockSpec((model, width), lambda j: (0, j + first + total_blocks)),
            pl.BlockSpec((width, model), lambda j: (j + first, 0)),
        ],
        out_specs=[whole, whole, pl.BlockSpec((3, model, width), lambda j: (0, 0, j))],
        scratch_shapes=([pltpu.VMEM((tile, width), F32)] * 3 + [pltpu.VMEM((tokens // 2, width), BF)] * 3) * 2,
        compiler_params=pltpu.CompilerParams(dimension_semantics=("arbitrary",), vmem_limit_bytes=LIMIT),
        cost_estimate=pl.CostEstimate(flops=18 * tokens * model * hidden, bytes_accessed=tokens * model * 24 + model * hidden * 12, transcendentals=tokens * hidden),
        name="ffn_both",
    )(second_act, out_grad, second_turned, grad_turned, ffn_in, ffn_in, ffn_out)


def norm_back_kernel(pieces, resid_ref, *refs):
    sum_refs, back_refs = refs[:pieces], refs[pieces : 2 * pieces]
    og_ref, gain_ref, out_ref, grad_ref, low_ref, gain_grad_ref = refs[2 * pieces :]

    @pl.when(pl.program_id(0) == 0)
    def _():
        gain_grad_ref[...] = jnp.zeros_like(gain_grad_ref)

    tile = 64

    def body(i):
        rows = rows_of(i, tile)
        resid = resid_ref[rows, :]
        n, scale = norm_stats(resid)
        u = sum(ref[rows, :] for ref in back_refs)
        ug = u * gain_ref[...]
        un = u * n
        part = ug - jnp.mean(ug, axis=-1, keepdims=True) - n * jnp.mean(ug * n, axis=-1, keepdims=True)
        grad = og_ref[rows, :].astype(F32) + scale * part
        out_ref[rows, :] = (resid + sum(ref[rows, :] for ref in sum_refs)).astype(BF)
        grad_ref[rows, :] = grad
        low_ref[rows, :] = grad.astype(BF)
        gain_grad_ref[...] += jnp.sum(un.reshape(tile // 8, 8, un.shape[1]), axis=0)

    loop(resid_ref.shape[0] // tile, body)


def norm_back(resid, totals, backs, out_grad, gain, tile=512):
    tokens, model = resid.shape
    pieces = len(totals)
    shape = jax.ShapeDtypeStruct
    block = pl.BlockSpec((tile, model), lambda i: (i, 0))
    fixed = pl.BlockSpec((8, model), lambda i: (0, 0))
    return pl.pallas_call(
        functools.partial(norm_back_kernel, pieces),
        out_shape=[shape((tokens, model), BF), shape((tokens, model), F32), shape((tokens, model), BF), shape((8, model), F32)],
        grid=(tokens // tile,),
        in_specs=[block] * (2 * pieces + 2) + [pl.BlockSpec((1, model), lambda i: (0, 0))],
        out_specs=[block, block, block, fixed],
        compiler_params=pltpu.CompilerParams(dimension_semantics=("arbitrary",), vmem_limit_bytes=LIMIT),
        cost_estimate=pl.CostEstimate(flops=20 * tokens * model, bytes_accessed=tokens * model * 22, transcendentals=tokens),
        name="norm_back",
    )(resid, *totals, *backs, out_grad, gain)


def eight_sum(v):
    return jnp.sum(v.reshape(v.shape[0] // 8, 8, v.shape[1]), axis=0)


def mixer_backward_kernel(
    split_ref, keep_ref, low_ref, q_ref, k_ref, v_ref, mixed_ref, wo_ref,
    fq_ref, fv_ref, fk_ref, slope_ref, shift_ref, skip_ref, fwd_real_ref, fwd_ref, inv_real_ref, inv_ref,
    p_ref, chan_ref,
    qs, ks, vs, xv, xc, xy, y_s, spec_s, u_s, o_s,
):
    r = pl.program_id(1)
    length, width = q_ref.shape
    quarter = length // 4
    split, keep = split_ref[r], keep_ref[r]
    tile = 64

    @pl.when(r == 0)
    def _():
        chan_ref[...] = jnp.zeros_like(chan_ref)

    for ref, source in ((qs, q_ref), (ks, k_ref), (vs, v_ref)):
        ref[0:8, :] = jnp.zeros((8, width), F32)

        def widen(i, ref=ref, source=source):
            ref[pl.ds(pl.multiple_of(8 + i * tile, 8), tile), :] = source[rows_of(i, tile), :].astype(F32)

        loop(length // tile, widen)

    o_s[0:length, 0:width] = mm_t(low_ref[...], wo_ref[...])

    def conv(i):
        t = i * tile
        rows = rows_of(i, tile)
        kept = t + lax.broadcasted_iota(jnp.int32, (tile, width), 0) < keep
        gated_grad = o_s[rows, 0:width]
        low = (gated_grad * conv_back(qs, t, tile, fq_ref, split)).astype(BF)
        xy[rows, :] = low
        value = jnp.where(kept, conv_back(vs, t, tile, fv_ref, split), 0.0).astype(BF)
        xv[rows, :] = value
        xc[rows, :] = jnp.where(kept, conv_back(ks, t, tile, fk_ref, split), 0.0).astype(BF)
        chan_ref[2, :, :] += eight_sum(low.astype(F32) * value.astype(F32))

    loop(length // tile, conv)
    butterfly(xv, y_s, 0, width, quarter)
    butterfly(xc, y_s, width, width, quarter)
    butterfly(xy, y_s, 2 * width, width, quarter)

    def query(i):
        rows = rows_of(i, tile)
        qs[rows, :] = o_s[rows, 0:width] * mixed_ref[rows, :].astype(F32)

    loop(length // tile, query)
    blockwise(y_s, spec_s, fwd_real_ref, fwd_ref, quarter)

    def bins(re, im, first):
        n = 16
        re, im = pl.ds(pl.multiple_of(re, n), n), pl.ds(pl.multiple_of(im, n), n)
        vr, vi = spec_s[re, 0:width], spec_s[im, 0:width]
        cr, ci = spec_s[re, width : 2 * width], spec_s[im, width : 2 * width]
        yr, yi = spec_s[re, 2 * width : 3 * width], spec_s[im, 2 * width : 3 * width]
        slope, shift = slope_ref[...], shift_ref[...]
        rr, ii = cr * cr, ci * ci
        if first:
            edge = lax.broadcasted_iota(jnp.int32, (n, width), 0) == 0
            pr, pi = jnp.where(edge, rr, rr + ii), jnp.where(edge, ii, rr + ii)
            gr, gi = jax.nn.sigmoid(slope * pr + shift), jax.nn.sigmoid(slope * pi + shift)
            ar = vr * yr + jnp.where(edge, 0.0, vi * yi)
            ai = jnp.where(edge, -vi * yi, vi * yr - vr * yi)
            br = ar * cr - jnp.where(edge, 0.0, ai * ci)
            bi = jnp.where(edge, -ai * ci, br)
            wr, wi = br * gr * (1.0 - gr), bi * gi * (1.0 - gi)
            ws = jnp.where(edge, 0.5 * (wr + wi), wr)
            wp = jnp.where(edge, 0.5 * (wr * pr + wi * pi), wr * pr)
            hr, hi = gr * cr, gi * ci
            er = hr * yr + jnp.where(edge, 0.0, hi * yi)
            ei = jnp.where(edge, hi * yi, hr * yi - hi * yr)
            dr = gr * ar + 2.0 * slope * wr * cr
            di = 2.0 * slope * wi * ci - gi * ai
        else:
            p = rr + ii
            g = jax.nn.sigmoid(slope * p + shift)
            ar, ai = vr * yr + vi * yi, vi * yr - vr * yi
            ws = (ar * cr - ai * ci) * (g * (1.0 - g))
            wp = ws * p
            hr, hi = g * cr, g * ci
            er, ei = hr * yr + hi * yi, hr * yi - hi * yr
            k = 2.0 * slope * ws
            dr, di = g * ar + k * cr, k * ci - g * ai
        chan_ref[0, :, :] += eight_sum(wp)
        chan_ref[1, :, :] += eight_sum(ws)
        u_s[re, 0:width] = er.astype(BF)
        u_s[im, 0:width] = ei.astype(BF)
        u_s[re, width : 2 * width] = dr.astype(BF)
        u_s[im, width : 2 * width] = di.astype(BF)

    each_bin(quarter, bins)
    resynth(u_s, o_s, inv_real_ref, inv_ref, quarter)

    def finish(i):
        n = 32
        value = recombine(o_s, slice(0, width), i, n, quarter)
        cond = recombine(o_s, slice(width, 2 * width), i, n, quarter)
        for k in range(4):
            rows = pl.ds(pl.multiple_of(k * quarter + i * n, n), n)
            kept = k * quarter + i * n + lax.broadcasted_iota(jnp.int32, (n, width), 0) < keep
            grad = (value[k] + skip_ref[...] * xy[rows, :].astype(F32)).astype(BF).astype(F32)
            vs[rows, :] = jnp.where(kept, grad, 0.0)
            ks[rows, :] = jnp.where(kept, cond[k].astype(BF).astype(F32), 0.0)

    loop(quarter // 32, finish)
    for ref in (qs, ks, vs):
        ref[length : length + 8, :] = jnp.zeros((8, width), F32)

    for slot, (ref, source, f_ref) in enumerate(((qs, q_ref, fq_ref), (vs, v_ref, fv_ref), (ks, k_ref, fk_ref))):

        def adjoint(i, slot=slot, ref=ref, source=source, f_ref=f_ref):
            t = i * tile
            rows = rows_of(i, tile)
            block = ref[pl.ds(pl.multiple_of(t, tile), tile + 8), :]
            position = t + lax.broadcasted_iota(jnp.int32, (tile, width), 0)
            g0 = block[0:tile]
            g1 = jnp.where(position + 1 != split, block[1 : tile + 1], 0.0)
            g2 = jnp.where((position + 2 != split) & (position + 1 != split), block[2 : tile + 2], 0.0)
            s = source[rows, :].astype(F32)
            place = slice((0, 2, 1)[slot] * width, ((0, 2, 1)[slot] + 1) * width)
            p_ref[rows, place] = (f_ref[0:1, :] * g0 + f_ref[1:2, :] * g1 + f_ref[2:3, :] * g2).astype(BF)
            for k, g in enumerate((g0, g1, g2)):
                chan_ref[3 + 3 * slot + k, :, :] += eight_sum(g * s)

        loop(length // tile, adjoint)


def mixer_backward(branch_low, split, keep, q, k, v, mixed, proj_out, short_filter, cond_filter, slope, shift, skip, tables, width=256):
    rows, length, model = q.shape
    blocks = model // width
    shape = jax.ShapeDtypeStruct
    pad = pltpu.VMEM((length + 8, width), F32)
    quarter = length // 4
    row = pl.BlockSpec((None, length, model), lambda j, r, *_: (r, 0, 0))
    part = pl.BlockSpec((None, length, width), lambda j, r, *_: (r, 0, j))

    def columns(size, offset):
        return pl.BlockSpec((size, width), lambda j, r, *_: (0, j + offset * blocks))

    fixed = lambda j, r, *_: (0, 0)
    table_specs = [once((2 * quarter, quarter), fixed), once((6 * quarter, 2 * quarter), fixed)] * 2
    one = columns(1, 0)
    flops = rows * (2 * length * model * model + 2 * 5 * model * (2 * length) * length // 2)
    return pl.pallas_call(
        mixer_backward_kernel,
        out_shape=[shape((rows, length, 3 * model), BF), shape((12, 8, model), F32)],
        grid_spec=pltpu.PrefetchScalarGridSpec(
            num_scalar_prefetch=2,
            grid=(blocks, rows),
            in_specs=[row, part, part, part, part, pl.BlockSpec((width, model), lambda j, r, *_: (j, 0)), columns(3, 0), columns(3, 1), columns(3, 0), one, one, one] + table_specs,
            out_specs=[pl.BlockSpec((None, length, 3 * width), lambda j, r, *_: (r, 0, j)), pl.BlockSpec((12, 8, width), lambda j, r, *_: (0, 0, j))],
            scratch_shapes=[pad, pad, pad] + [pltpu.VMEM((length, width), BF)] * 3 + [
                pltpu.VMEM((2 * length, 3 * width), BF),
                pltpu.VMEM((2 * length, 3 * width), F32),
                pltpu.VMEM((2 * length, 2 * width), BF),
                pltpu.VMEM((2 * length, 2 * width), F32),
            ],
        ),
        compiler_params=pltpu.CompilerParams(dimension_semantics=("arbitrary", "arbitrary"), vmem_limit_bytes=LIMIT),
        cost_estimate=pl.CostEstimate(flops=flops, bytes_accessed=rows * length * (model * 2 * blocks + model * 14), transcendentals=rows * length * model),
        name="mixer_backward",
    )(split, keep, branch_low, q, k, v, mixed, proj_out, short_filter, short_filter, cond_filter, slope, shift, skip, *tables)


def input_back_kernel(width, x_ref, grad_ref, gain_ref, w_ref, p_ref, in_grad_ref, gain_grad_ref, acc):
    model = x_ref.shape[1]
    tile = 64

    @pl.when(pl.program_id(0) == 0)
    def _():
        gain_grad_ref[...] = jnp.zeros_like(gain_grad_ref)

    total = None
    for b in range(model // width):
        for k in range(3):
            place = (3 * b + k) * width
            term = mm_t(p_ref[:, place : place + width], w_ref[:, k * model + b * width : k * model + (b + 1) * width])
            total = term if total is None else total + term
    acc[...] = total

    def body(i):
        rows = rows_of(i, tile)
        n, scale = norm_stats(x_ref[rows, :].astype(F32))
        u = acc[rows, :]
        ug = u * gain_ref[...]
        part = ug - jnp.mean(ug, axis=-1, keepdims=True) - n * jnp.mean(ug * n, axis=-1, keepdims=True)
        in_grad_ref[rows, :] = (grad_ref[rows, :] + scale * part).astype(in_grad_ref.dtype)
        gain_grad_ref[...] += eight_sum(u * n)

    loop(x_ref.shape[0] // tile, body)


def input_back(x, resid_grad, gain, proj_in, proj_grad, width, tile=512):
    tokens, model = x.shape
    shape = jax.ShapeDtypeStruct
    block = pl.BlockSpec((tile, model), lambda i: (i, 0))
    return pl.pallas_call(
        functools.partial(input_back_kernel, width),
        out_shape=[shape((tokens, model), BF), shape((8, model), F32)],
        grid=(tokens // tile,),
        in_specs=[block, block, once((1, model), lambda i: (0, 0)), once((model, 3 * model), lambda i: (0, 0)), pl.BlockSpec((tile, 3 * model), lambda i: (i, 0))],
        out_specs=[block, pl.BlockSpec((8, model), lambda i: (0, 0))],
        scratch_shapes=[pltpu.VMEM((tile, model), F32)],
        compiler_params=pltpu.CompilerParams(dimension_semantics=("arbitrary",), vmem_limit_bytes=LIMIT),
        cost_estimate=pl.CostEstimate(flops=6 * tokens * model * model, bytes_accessed=tokens * model * 14, transcendentals=tokens),
        name="input_back",
    )(x, resid_grad, gain, proj_in, proj_grad)


def turn(a, b):
    return lax.dot_general(a, b, (((0,), (0,)), ((), ())), preferred_element_type=F32).astype(BF)


def after(value, earlier):
    return lax.optimization_barrier((value, earlier))[0]


def exchange_sum_kernel(rows, seq, x_ref, out_ref, slots, total, send_sem, recv_sem):
    r, s = lax.axis_index("rows"), lax.axis_index("seq")
    partners = []
    bit = 1
    while bit < rows:
        partners.append((r + bit - 2 * bit * (lax.rem(r // bit, 2)), s))
        bit *= 2
    bit = 1
    while bit < seq:
        partners.append((r, s + bit - 2 * bit * (lax.rem(s // bit, 2))))
        bit *= 2
    barrier = pltpu.get_barrier_semaphore()
    for partner in partners:
        pl.semaphore_signal(barrier, inc=1, device_id=partner, device_id_type=pl.DeviceIdType.MESH)
    pl.semaphore_wait(barrier, len(partners))
    total[0] = x_ref[...]
    for step, partner in enumerate(partners):
        copy = pltpu.make_async_remote_copy(
            src_ref=total.at[step], dst_ref=slots.at[step], send_sem=send_sem.at[step], recv_sem=recv_sem.at[step],
            device_id=partner, device_id_type=pl.DeviceIdType.MESH,
        )
        copy.start()
        copy.wait()
        total[step + 1] = total[step] + slots[step]
    out_ref[...] = total[len(partners)]


def power_of_two(n):
    return n & (n - 1) == 0


def exchange_sum(value):
    rows, seq = lax.axis_size("rows"), lax.axis_size("seq")
    if not (power_of_two(rows) and power_of_two(seq)):
        return lax.psum(value, ("rows", "seq"))
    steps = (rows.bit_length() - 1) + (seq.bit_length() - 1)
    return pl.pallas_call(
        functools.partial(exchange_sum_kernel, rows, seq),
        out_shape=jax.ShapeDtypeStruct(value.shape, value.dtype),
        in_specs=[pl.BlockSpec(memory_space=pltpu.VMEM)],
        out_specs=pl.BlockSpec(memory_space=pltpu.VMEM),
        scratch_shapes=[
            pltpu.VMEM((steps, *value.shape), value.dtype),
            pltpu.VMEM((steps + 1, *value.shape), value.dtype),
            pltpu.SemaphoreType.DMA((steps,)),
            pltpu.SemaphoreType.DMA((steps,)),
        ],
        compiler_params=pltpu.CompilerParams(collective_id=7, has_side_effects=True),
        cost_estimate=pl.CostEstimate(flops=20_000_000_000, bytes_accessed=0, transcendentals=0),
        name="exchange_sum",
    )(value)


def swapped(value):
    count = lax.axis_size("seq")
    return lax.ppermute(value, "seq", [(i, (i + 1) % count) for i in range(count)])


def gather_rows(value, first=0, count=None):
    own = value.shape[0] // lax.axis_size("seq")
    count = own if count is None else count
    if lax.axis_size("seq") != 2:
        whole = lax.all_to_all(value, "seq", split_axis=0, concat_axis=1, tiled=True)
        return whole[first : first + count]
    s = lax.axis_index("seq")
    mine = lax.dynamic_slice_in_dim(value, s * own + first, count)
    other = swapped(lax.dynamic_slice_in_dim(value, (1 - s) * own + first, count))
    return jnp.concatenate([jnp.where(s == 0, mine, other), jnp.where(s == 0, other, mine)], axis=1)


def scatter_rows(value):
    if lax.axis_size("seq") != 2:
        return lax.all_to_all(value, "seq", split_axis=1, concat_axis=0, tiled=True)
    s = lax.axis_index("seq")
    part = value.shape[1] // 2
    mine = lax.dynamic_slice_in_dim(value, s * part, part, axis=1)
    other = swapped(lax.dynamic_slice_in_dim(value, (1 - s) * part, part, axis=1))
    return jnp.concatenate([jnp.where(s == 0, mine, other), jnp.where(s == 0, other, mine)], axis=0)


def seq_sum(value):
    if lax.axis_size("seq") != 2:
        return lax.psum(value, "seq").astype(F32)
    return value.astype(F32) + swapped(value).astype(F32)


def per_device_rows(inputs, split_point, keep_mask, norm_gain, proj_in, short_filter, cond_filter, spec_slope, spec_shift, skip_gain, proj_out, ffn_gain, ffn_in, ffn_out, out_grad):
    local_rows, local_len, model = inputs.shape
    count = lax.axis_size("seq")
    own = local_rows // count
    length = local_len * count
    tokens = own * length
    width = 256
    first_row = lax.axis_index("seq") * own
    flat = lambda a: a.reshape(tokens, model)
    flat_wide = lambda a: a.reshape(tokens, 3 * model)
    shaped = lambda a: a.reshape(own, length, model)
    lift = lambda a: a.reshape(1, -1)

    pieces = [(0, 1), (1, own - 1)] if own > 1 else [(0, own)]
    xs = []
    for start, size in pieces:
        xs.append(gather_rows(after(inputs, xs) if xs else inputs, start, size))
    kept = jnp.sum(keep_mask, axis=1)
    kept = kept + swapped(kept) if count == 2 else lax.psum(kept, "seq")
    keep = lax.dynamic_slice_in_dim(kept, first_row, own)
    split = lax.dynamic_slice_in_dim(split_point, first_row, own)
    tables = spectral_tables(length, lax.axis_index("seq") * (2 * length))
    slope, shift, skip = lift(spec_slope), lift(spec_shift), lift(skip_gain)

    held = ()
    for x, (start, size) in zip(xs, pieces):
        held = mixer_forward(
            x, split, keep, lift(norm_gain), proj_in, short_filter, cond_filter, slope, shift, skip, proj_out, lift(ffn_gain), tables, start, own, held
        )
        if start == 0:
            whole_grad = flat(gather_rows(after(out_grad, (xs[-1], held[-1]))))
    first, q, k, v, mixed, gated, resid, second = held
    x = jnp.concatenate(xs, axis=0)
    second = flat(second)
    second_turned, grad_turned = second.T, whole_grad.T
    pieces = 2
    totals, backs, grads = [], [], []
    for piece in range(pieces):
        total, back, grad = ffn_both(second, whole_grad, second_turned, grad_turned, ffn_in, ffn_out, piece, pieces)
        totals.append(total)
        backs.append(back)
        grads.append(grad)
    chain = lax.psum_scatter(grads[0], "rows", scatter_dimension=1, tiled=True)
    ffn_shares = [chain]
    output, resid_grad, branch_low, ffn_gain_part = norm_back(flat(resid), totals, backs, whole_grad, lift(ffn_gain))
    output = scatter_rows(shaped(output))
    out_part = turn(flat(gated), branch_low)
    for grad in grads[1:]:
        grad, chain, branch_low = lax.optimization_barrier((grad, chain, branch_low))
        chain = lax.psum_scatter(grad, "rows", scatter_dimension=1, tiled=True)
        ffn_shares.append(chain)
    proj_grad, chan = mixer_backward(shaped(branch_low), split, keep, q, k, v, mixed, proj_out, short_filter, cond_filter, slope, shift, skip, tables)
    proj_grad = flat_wide(proj_grad)
    mix_part = jnp.concatenate([out_part, turn(flat(first), proj_grad)], axis=1)
    mix_part, *ffn_shares = lax.optimization_barrier((mix_part, *ffn_shares))
    mix_share = lax.psum_scatter(mix_part, "rows", scatter_dimension=0, tiled=True)
    proj_grad = after(proj_grad, mix_part)
    input_grad, norm_gain_part = input_back(flat(x), resid_grad, lift(norm_gain), proj_in, proj_grad, width)
    input_grad = scatter_rows(shaped(input_grad)).astype(F32)
    ffn_shares = [seq_sum(share) for share in ffn_shares]
    small = jnp.sum(jnp.concatenate([ffn_gain_part[None], norm_gain_part[None], chan], 0), axis=1)
    small = exchange_sum(small)
    scale = 1.0 / length
    mix_share = seq_sum(mix_share)
    in_share = mix_share[:, model:].reshape(-1, model // width, 3, width).transpose(0, 2, 1, 3)
    return (
        output,
        input_grad,
        small[1],
        in_share.reshape(-1, 3 * model),
        jnp.concatenate([small[5:8], small[8:11]], axis=1),
        small[11:14],
        small[2] * scale,
        small[3] * scale,
        small[4],
        mix_share[:, :model],
        small[0],
        jnp.concatenate([share[k] for k in range(2) for share in ffn_shares], axis=1),
        jnp.concatenate([share[2] for share in ffn_shares], axis=1).T,
    )


PRECISE = lax.Precision.HIGH


def passed_along(value, axis, steps):
    count = lax.axis_size(axis)
    leading, last = (max(0, -steps), min(count, count - steps))
    return lax.ppermute(value, axis, [(source, source + steps) for source in range(leading, last)])


def layer_norm(values, scaling):
    center = values - jnp.mean(values, axis=-1, keepdims=True)
    spread = jnp.mean(center * center, axis=-1, keepdims=True)
    return center * lax.rsqrt(spread + EPSILON) * scaling


def conv_three(extended, weights, same_one, same_two):
    length = extended.shape[1] - 2
    return (
        weights[0] * extended[:, 2:]
        + weights[1] * extended[:, 1 : length + 1] * same_one
        + weights[2] * extended[:, :length] * same_two
    )


def dft_tables(seq_length):
    table_shape = (seq_length + 1, seq_length)
    product = lax.broadcasted_iota(jnp.int32, table_shape, 0) * lax.broadcasted_iota(
        jnp.int32, table_shape, 1
    )
    angles = (product % (2 * seq_length)).astype(jnp.float32) * (math.pi / seq_length)
    freq = lax.broadcasted_iota(jnp.int32, (seq_length + 1, 1), 0)
    edge = jnp.logical_or(freq == 0, freq == seq_length)
    weights = jnp.where(edge, 1.0, 2.0).astype(jnp.float32) / (2.0 * seq_length)
    return (jnp.cos(angles), jnp.sin(angles), weights)


def analyze(values, conds, cos_table, sin_table):
    value_real = jnp.einsum("ft,ktd->kfd", cos_table, values, precision=PRECISE)
    value_imag = -jnp.einsum("ft,ktd->kfd", sin_table, values, precision=PRECISE)
    cond_real = jnp.einsum("ft,ktd->kfd", cos_table, conds, precision=PRECISE)
    cond_imag = -jnp.einsum("ft,ktd->kfd", sin_table, conds, precision=PRECISE)
    return (value_real, value_imag, cond_real, cond_imag)


def synth(
    value_real,
    value_imag,
    cond_real,
    cond_imag,
    values,
    slopes,
    shifts,
    skip_gains,
    cos_table,
    sin_table,
    freq_weights,
):
    factor = jax.nn.sigmoid(slopes * (cond_real * cond_real + cond_imag * cond_imag) + shifts)
    filter_real = cond_real * factor
    filter_imag = cond_imag * factor
    prod_real = (value_real * filter_real - value_imag * filter_imag) * freq_weights
    prod_imag = (value_real * filter_imag + value_imag * filter_real) * freq_weights
    mixed_out = jnp.einsum("ft,kfd->ktd", cos_table, prod_real, precision=PRECISE) - jnp.einsum(
        "ft,kfd->ktd", sin_table, prod_imag, precision=PRECISE
    )
    return mixed_out + skip_gains * values


def times_transpose(left, right):
    return lax.dot_general(
        left, right, (((1,), (1,)), ((), ())), preferred_element_type=jnp.float32
    )


def transpose_times(left, right):
    return lax.dot_general(
        left, right, (((0,), (0,)), ((), ())), preferred_element_type=jnp.float32
    )


def per_device(
    inputs,
    split_point,
    keep_mask,
    norm_gain,
    proj_in,
    short_filter,
    cond_filter,
    spec_slope,
    spec_shift,
    skip_gain,
    proj_out,
    ffn_gain,
    ffn_in,
    ffn_out,
    out_grad,
):
    local_rows, local_len, model_width = inputs.shape
    hidden_width = ffn_out.shape[0]
    seq_count = lax.axis_size("seq")
    seq_index = lax.axis_index("seq")
    full_len = local_len * seq_count
    chan_width = model_width // seq_count
    token_count = local_rows * local_len
    positions = seq_index * local_len + lax.broadcasted_iota(jnp.int32, (local_rows, local_len), 1)
    splits = split_point[:, None]
    segment = positions >= splits
    same_one = (segment == (positions - 1 >= splits)).astype(jnp.float32)[:, :, None]
    same_two = (segment == (positions - 2 >= splits)).astype(jnp.float32)[:, :, None]
    keep_float = keep_mask.astype(jnp.float32)[:, :, None]
    flat_in = inputs.reshape(token_count, model_width).astype(jnp.float32)
    normed_one, norm_one_back = jax.vjp(layer_norm, flat_in, norm_gain)
    first_act = normed_one.astype(jnp.bfloat16)
    projected = jnp.dot(first_act, proj_in, preferred_element_type=jnp.float32).astype(jnp.bfloat16)
    proj_rows = projected.reshape(local_rows, local_len, 3 * model_width)
    edge_values = passed_along(proj_rows[:, local_len - 2 :, :], "seq", 1)
    extended = jnp.concatenate([edge_values, proj_rows], axis=1).astype(jnp.float32)

    def mixer_local(ext_values, short_weights, cond_weights):
        query_value = jnp.concatenate(
            [ext_values[:, :, :model_width], ext_values[:, :, 2 * model_width :]], axis=2
        )
        conv_both = conv_three(query_value, short_weights, same_one, same_two)
        cond_conv = conv_three(
            ext_values[:, :, model_width : 2 * model_width], cond_weights, same_one, same_two
        )
        return (
            conv_both[:, :, :model_width],
            conv_both[:, :, model_width:] * keep_float,
            cond_conv * keep_float,
        )

    (query_conv, value_masked, cond_masked), mixer_back = jax.vjp(
        mixer_local, extended, short_filter, cond_filter
    )
    value_low = value_masked.astype(jnp.bfloat16)
    cond_low = cond_masked.astype(jnp.bfloat16)
    slope_part = lax.dynamic_slice_in_dim(spec_slope, seq_index * chan_width, chan_width)
    shift_part = lax.dynamic_slice_in_dim(spec_shift, seq_index * chan_width, chan_width)
    skip_part = lax.dynamic_slice_in_dim(skip_gain, seq_index * chan_width, chan_width)
    cos_table, sin_table, freq_weights = dft_tables(full_len)

    def synth_local(
        value_real, value_imag, cond_real, cond_imag, values, slopes, shifts, skip_gains
    ):
        return synth(
            value_real,
            value_imag,
            cond_real,
            cond_imag,
            values,
            slopes,
            shifts,
            skip_gains,
            cos_table,
            sin_table,
            freq_weights,
        )

    value_chan = lax.all_to_all(value_low, "seq", split_axis=2, concat_axis=1, tiled=True)
    cond_chan = lax.all_to_all(cond_low, "seq", split_axis=2, concat_axis=1, tiled=True)
    value_float = value_chan.astype(jnp.float32)
    spectra = analyze(value_float, cond_chan.astype(jnp.float32), cos_table, sin_table)
    mixed_chan = synth_local(
        spectra[0],
        spectra[1],
        spectra[2],
        spectra[3],
        value_float,
        slope_part,
        shift_part,
        skip_part,
    ).astype(jnp.bfloat16)
    mixed_home = lax.all_to_all(mixed_chan, "seq", split_axis=1, concat_axis=2, tiled=True)
    mixed_float = mixed_home.astype(jnp.float32)
    gated = (query_conv * mixed_float).astype(jnp.bfloat16).reshape(token_count, model_width)
    branch = jnp.dot(gated, proj_out, preferred_element_type=jnp.float32)
    resid = flat_in + branch
    normed_two, norm_two_back = jax.vjp(layer_norm, resid, ffn_gain)
    second_act = normed_two.astype(jnp.bfloat16)
    gate_up = jnp.dot(second_act, ffn_in, preferred_element_type=jnp.float32)

    def glu_local(both_parts):
        return (
            jax.nn.gelu(both_parts[:, :hidden_width], approximate=False)
            * both_parts[:, hidden_width:]
        )

    hidden, glu_back = jax.vjp(glu_local, gate_up)
    hidden_low = hidden.astype(jnp.bfloat16)
    result = resid + jnp.dot(hidden_low, ffn_out, preferred_element_type=jnp.float32)
    output = result.astype(jnp.bfloat16).reshape(local_rows, local_len, model_width)
    flat_grad = out_grad.reshape(token_count, model_width)
    hidden_grad = times_transpose(flat_grad, ffn_out)
    (gate_up_grad,) = glu_back(hidden_grad)
    gate_up_low = gate_up_grad.astype(jnp.bfloat16)
    second_grad = times_transpose(gate_up_low, ffn_in)
    resid_part, ffn_gain_part = norm_two_back(second_grad)
    resid_grad = flat_grad.astype(jnp.float32) + resid_part
    branch_low = resid_grad.astype(jnp.bfloat16)
    gated_grad = times_transpose(branch_low, proj_out).reshape(local_rows, local_len, model_width)
    query_grad = gated_grad * mixed_float
    mixed_grad = (gated_grad * query_conv).astype(jnp.bfloat16)
    grad_chan = lax.all_to_all(mixed_grad, "seq", split_axis=2, concat_axis=1, tiled=True)
    grad_float = grad_chan.astype(jnp.float32)
    item_count = grad_chan.shape[0]
    slope_items = jnp.broadcast_to(slope_part, (item_count, 1, chan_width))
    shift_items = jnp.broadcast_to(shift_part, (item_count, 1, chan_width))
    skip_items = jnp.broadcast_to(skip_part, (item_count, 1, chan_width))
    value_float = value_chan.astype(jnp.float32)

    def spectral(values, conds, slopes, shifts, skip_gains):
        spectra = analyze(values, conds, cos_table, sin_table)
        return synth_local(
            spectra[0], spectra[1], spectra[2], spectra[3], values, slopes, shifts, skip_gains
        )

    unused, pull = jax.vjp(
        spectral, value_float, cond_chan.astype(jnp.float32), slope_items, shift_items, skip_items
    )
    value_back, cond_back, slope_rows, shift_rows, skip_rows = pull(grad_float)
    value_grad, cond_grad = (
        lax.all_to_all(
            value_back.astype(jnp.bfloat16), "seq", split_axis=1, concat_axis=2, tiled=True
        ),
        lax.all_to_all(
            cond_back.astype(jnp.bfloat16), "seq", split_axis=1, concat_axis=2, tiled=True
        ),
    )
    start_chan = (seq_index * chan_width,)
    empty_width = jnp.zeros((model_width,), jnp.float32)
    slope_full = lax.dynamic_update_slice(empty_width, jnp.sum(slope_rows, axis=(0, 1)), start_chan)
    shift_full = lax.dynamic_update_slice(empty_width, jnp.sum(shift_rows, axis=(0, 1)), start_chan)
    skip_full = lax.dynamic_update_slice(empty_width, jnp.sum(skip_rows, axis=(0, 1)), start_chan)
    ext_grad, short_grad, cond_weight_grad = mixer_back(
        (query_grad, value_grad.astype(jnp.float32), cond_grad.astype(jnp.float32))
    )
    incoming = passed_along(ext_grad[:, :2, :].astype(jnp.bfloat16), "seq", -1).astype(jnp.float32)
    proj_grad = ext_grad[:, 2:, :] + jnp.pad(incoming, ((0, 0), (local_len - 2, 0), (0, 0)))
    proj_low = proj_grad.astype(jnp.bfloat16).reshape(token_count, 3 * model_width)
    first_grad = times_transpose(proj_low, proj_in)
    input_part, norm_gain_part = norm_one_back(first_grad)
    input_grad = (resid_grad + input_part).reshape(local_rows, local_len, model_width)
    share = lax.psum_scatter(
        jnp.concatenate(
            [
                transpose_times(first_act, proj_low),
                transpose_times(gated, branch_low),
                transpose_times(second_act, gate_up_low),
                transpose_times(flat_grad, hidden_low),
            ],
            axis=1,
        ).astype(jnp.bfloat16),
        "rows",
        scatter_dimension=0,
        tiled=True,
    )
    summed = lax.psum(share, "seq").astype(jnp.float32)
    small_sums = lax.psum(
        (
            norm_gain_part,
            short_grad,
            cond_weight_grad,
            slope_full,
            shift_full,
            skip_full,
            ffn_gain_part,
        ),
        ("rows", "seq"),
    )
    proj_in_grad = summed[:, : 3 * model_width]
    proj_out_grad = summed[:, 3 * model_width : 4 * model_width]
    ffn_in_grad = summed[:, 4 * model_width : 4 * model_width + 2 * hidden_width]
    ffn_out_grad = jnp.transpose(summed[:, 4 * model_width + 2 * hidden_width :])
    return (
        output,
        input_grad,
        small_sums[0],
        proj_in_grad,
        small_sums[1],
        small_sums[2],
        small_sums[3],
        small_sums[4],
        small_sums[5],
        proj_out_grad,
        small_sums[6],
        ffn_in_grad,
        ffn_out_grad,
    )


def per_device_any(*args):
    rows, width = args[0].shape[0], args[0].shape[2]
    even = rows % lax.axis_size("seq") == 0 and width % 256 == 0
    return (per_device_rows if even else per_device)(*args)


def solution(mesh):
    in_specs = (
        P("rows", "seq", None),
        P("rows"),
        P("rows", "seq"),
        P(),
        P(),
        P(),
        P(),
        P(),
        P(),
        P(),
        P(),
        P(),
        P(),
        P(),
        P("rows", "seq", None),
    )
    out_specs = (
        P("rows", "seq", None),
        P("rows", "seq", None),
        P(),
        P("rows", None),
        P(),
        P(),
        P(),
        P(),
        P(),
        P("rows", None),
        P(),
        P("rows", None),
        P(None, "rows"),
    )
    return jax.shard_map(
        per_device_any, mesh=mesh, in_specs=in_specs, out_specs=out_specs, check_vma=False
    )
```

```python
import functools
import math

import jax
import jax.numpy as jnp
from jax import lax
from jax.experimental import pallas as pl
from jax.experimental.pallas import tpu as pltpu
from jax.sharding import PartitionSpec as P

EPSILON = 1e-05
BF = jnp.bfloat16
F32 = jnp.float32
ROOT_HALF = math.sqrt(0.5)
LIMIT = 67043328


def mm(a, b):
    return lax.dot_general(a, b, (((1,), (0,)), ((), ())), preferred_element_type=F32)


def mm_t(a, b):
    return lax.dot_general(a, b, (((1,), (1,)), ((), ())), preferred_element_type=F32)


def spectral_tables(length, offset):
    quarter = length // 4
    two_n = 2 * length
    m = lax.broadcasted_iota(jnp.int32, (quarter, quarter), 0)
    s = lax.broadcasted_iota(jnp.int32, (quarter, quarter), 1)

    def cos_sin(freq):
        angle = ((freq * s + offset) % two_n).astype(F32) * (2.0 * math.pi / two_n)
        return jnp.cos(angle), jnp.sin(angle)

    half = quarter // 2
    forward, inverse = [], []
    for r in (1, 2, 3):
        c, sn = cos_sin(8 * m + r)
        forward.append(jnp.concatenate([jnp.concatenate([c, sn], 1), jnp.concatenate([-sn, c], 1)], 0))
        inverse.append(forward[-1].T * (2.0 / two_n))
    row = m % half
    low = m < half
    c, sn = cos_sin(8 * jnp.where(m == half, half, row))
    zero = jnp.where(low | (m == half), c, -sn)
    c4, sn4 = cos_sin(8 * row + 4)
    four = jnp.where(low, c4, -sn4)
    edge = jnp.where((m == 0) | (m == half), 1.0, 2.0) / two_n
    fwd_real = jnp.concatenate([zero, four], 0)
    inv_real = jnp.concatenate([(zero * edge).T, four.T * (2.0 / two_n)], 0)
    return (
        fwd_real.astype(BF),
        jnp.concatenate(forward, 0).astype(BF),
        inv_real.astype(BF),
        jnp.concatenate(inverse, 0).astype(BF),
    )


def loop(count, body):
    lax.fori_loop(0, count, lambda i, c: (body(i), c)[1], 0)


def rows_of(i, size):
    return pl.ds(pl.multiple_of(i * size, size), size)


def norm_stats(v):
    center = v - jnp.mean(v, axis=-1, keepdims=True)
    scale = lax.rsqrt(jnp.mean(center * center, axis=-1, keepdims=True) + EPSILON)
    return center * scale, scale


def same_masks(position, split):
    same_one = position != split
    return same_one, same_one & (position != split + 1)


def butterfly(x_ref, y_ref, lane, width, quarter):
    tile = 32
    lanes = slice(lane, lane + width)

    def body(i):
        x0, x1, x2, x3 = [
            x_ref[pl.ds(pl.multiple_of(q * quarter + i * tile, tile), tile), :].astype(F32) for q in range(4)
        ]
        a, b, c, d = x0 + x2, x1 + x3, x0 - x2, x1 - x3
        sd, sb = d * ROOT_HALF, b * ROOT_HALF
        out = (a + b, a - b, x0 + sd, -x2 - sb, c, -d, x0 - sd, x2 - sb)
        for k, value in enumerate(out):
            y_ref[pl.ds(pl.multiple_of(k * quarter + i * tile, tile), tile), lanes] = value.astype(BF)

    loop(quarter // tile, body)


def blockwise(y_ref, spec_ref, fwd_real_ref, fwd_ref, quarter):
    q = quarter
    for k in range(2):
        spec_ref[k * q : (k + 1) * q, :] = mm(fwd_real_ref[k * q : (k + 1) * q, :], y_ref[k * q : (k + 1) * q, :])
    for k in range(3):
        spec_ref[2 * q + 2 * k * q : 2 * q + 2 * (k + 1) * q, :] = mm(
            fwd_ref[2 * k * q : 2 * (k + 1) * q, :], y_ref[2 * q + 2 * k * q : 2 * q + 2 * (k + 1) * q, :]
        )


def resynth(u_ref, out_ref, inv_real_ref, inv_ref, quarter):
    blockwise(u_ref, out_ref, inv_real_ref, inv_ref, quarter)


def each_bin(quarter, body, tile=16):
    half = quarter // 2
    body(0, half, True)

    def run(base, span, skip):
        def step(i):
            start = base + (i + skip) * tile
            body(start, start + span, False)

        loop(span // tile - skip, step)

    run(0, half, 1)
    run(quarter, half, 0)
    for k in range(3):
        run(2 * quarter + 2 * k * quarter, quarter, 0)


def recombine(o_ref, lanes, i, tile, quarter):
    def part(k):
        return o_ref[pl.ds(pl.multiple_of(k * quarter + i * tile, tile), tile), lanes]

    u0, u4, a1, b1, a2, b2, a3, b3 = [part(k) for k in range(8)]
    even, odd = u0 + u4, u0 - u4
    return (
        even + a1 + a2 + a3,
        odd + (a1 - b1 - a3 - b3) * ROOT_HALF - b2,
        even - b1 - a2 + b3,
        odd + (a3 - b3 - a1 - b1) * ROOT_HALF + b2,
    )


def conv_back(ref, t, tile, weights, split):
    block = ref[pl.ds(pl.multiple_of(t, tile), tile + 8), :]
    width = block.shape[1]
    position = t + lax.broadcasted_iota(jnp.int32, (tile, width), 0)
    one, two = same_masks(position, split)
    return (
        weights[0:1, :] * block[8 : tile + 8]
        + jnp.where(one, weights[1:2, :] * block[7 : tile + 7], 0.0)
        + jnp.where(two, weights[2:3, :] * block[6 : tile + 6], 0.0)
    )


def mixer_forward_kernel(
    first_row, earlier, split_ref, keep_ref, x_ref, norm_gain_ref, wq_ref, wk_ref, wv_ref, fq_ref, fv_ref, fk_ref, slope_ref, shift_ref,
    skip_ref, wo_ref, ffn_gain_ref, fwd_real_ref, fwd_ref, inv_real_ref, inv_ref,
    *refs,
):
    first_ref, q_ref, k_ref, v_ref, mixed_ref, gated_ref, resid_ref, second_ref = refs[earlier : earlier + 8]
    qs, ks, vs, xv, xc, y_s, spec_s, u_s, o_s, qc = refs[earlier + 8 :]
    r, j = first_row + pl.program_id(0), pl.program_id(1)
    length, width = q_ref.shape
    quarter = length // 4
    split, keep = split_ref[r], keep_ref[r]
    tile = 64

    @pl.when(j == 0)
    def _():
        def body(i):
            rows = rows_of(i, tile)
            v = x_ref[rows, :].astype(F32)
            n, _ = norm_stats(v)
            first_ref[rows, :] = (n * norm_gain_ref[...]).astype(BF)
            resid_ref[rows, :] = v

        loop(length // tile, body)
        for ref in (qs, ks, vs):
            ref[0:8, :] = jnp.zeros((8, width), F32)

    for w_ref, out_ref, ref in ((wq_ref, q_ref, qs), (wk_ref, k_ref, ks), (wv_ref, v_ref, vs)):
        value = mm(first_ref[...], w_ref[...]).astype(BF)
        out_ref[...] = value
        ref[8 : 8 + length, :] = value.astype(F32)

    def conv(i):
        t = i * tile
        rows = rows_of(i, tile)
        kept = t + lax.broadcasted_iota(jnp.int32, (tile, width), 0) < keep
        qc[rows, :] = conv_back(qs, t, tile, fq_ref, split)
        xv[rows, :] = jnp.where(kept, conv_back(vs, t, tile, fv_ref, split), 0.0).astype(BF)
        xc[rows, :] = jnp.where(kept, conv_back(ks, t, tile, fk_ref, split), 0.0).astype(BF)

    loop(length // tile, conv)
    butterfly(xv, y_s, 0, width, quarter)
    butterfly(xc, y_s, width, width, quarter)
    blockwise(y_s, spec_s, fwd_real_ref, fwd_ref, quarter)

    def bins(re, im, first):
        n = 16
        re, im = pl.ds(pl.multiple_of(re, n), n), pl.ds(pl.multiple_of(im, n), n)
        vr, vi = spec_s[re, 0:width], spec_s[im, 0:width]
        cr, ci = spec_s[re, width : 2 * width], spec_s[im, width : 2 * width]
        slope, shift = slope_ref[...], shift_ref[...]
        rr, ii = cr * cr, ci * ci
        if first:
            edge = lax.broadcasted_iota(jnp.int32, (n, width), 0) == 0
            hr = cr * jax.nn.sigmoid(slope * jnp.where(edge, rr, rr + ii) + shift)
            hi = ci * jax.nn.sigmoid(slope * jnp.where(edge, ii, rr + ii) + shift)
            ur = vr * hr - jnp.where(edge, 0.0, vi * hi)
            ui = jnp.where(edge, vi * hi, vr * hi + vi * hr)
        else:
            gain = jax.nn.sigmoid(slope * (rr + ii) + shift)
            hr, hi = cr * gain, ci * gain
            ur, ui = vr * hr - vi * hi, vr * hi + vi * hr
        u_s[re, :] = ur.astype(BF)
        u_s[im, :] = ui.astype(BF)

    each_bin(quarter, bins)
    resynth(u_s, o_s, inv_real_ref, inv_ref, quarter)

    def finish(i):
        n = 32
        parts = recombine(o_s, slice(0, width), i, n, quarter)
        for k, part in enumerate(parts):
            rows = pl.ds(pl.multiple_of(k * quarter + i * n, n), n)
            mixed = (part + skip_ref[...] * xv[rows, :].astype(F32)).astype(BF)
            mixed_ref[rows, :] = mixed
            gated_ref[rows, :] = (qc[rows, :] * mixed.astype(F32)).astype(BF)

    loop(quarter // 32, finish)
    resid_ref[...] += mm(gated_ref[...], wo_ref[...])

    @pl.when(j == pl.num_programs(1) - 1)
    def _():
        def body(i):
            rows = rows_of(i, tile)
            n, _ = norm_stats(resid_ref[rows, :])
            second_ref[rows, :] = (n * ffn_gain_ref[...]).astype(BF)

        loop(length // tile, body)


def once(shape, index):
    return pl.BlockSpec(shape, index, pipeline_mode=pl.Buffered(1))


def mixer_specs(length, model, width, first_row):
    blocks = model // width
    row = pl.BlockSpec((None, length, model), lambda r, j, *_: (r + first_row, 0, 0))
    part = pl.BlockSpec((None, length, width), lambda r, j, *_: (r + first_row, 0, j))

    def columns(rows, offset):
        return pl.BlockSpec((rows, width), lambda r, j, *_: (0, j + offset * blocks))

    out_rows = pl.BlockSpec((width, model), lambda r, j, *_: (j, 0))
    gain = once((1, model), lambda r, j, *_: (0, 0))
    q = length // 4
    tables = [once((2 * q, q), lambda r, j, *_: (0, 0)), once((6 * q, 2 * q), lambda r, j, *_: (0, 0))]
    return blocks, row, part, columns, out_rows, gain, tables + tables


def mixer_forward(x, split, keep, norm_gain, proj_in, short_filter, cond_filter, slope, shift, skip, proj_out, ffn_gain, tables, first_row, total_rows, earlier, width=256):
    rows, length, model = x.shape
    blocks, row, part, columns, out_rows, gain, table_specs = mixer_specs(length, model, width, first_row)
    x_row = pl.BlockSpec((None, length, model), lambda r, j, *_: (r, 0, 0))
    one = columns(1, 0)
    shape = jax.ShapeDtypeStruct
    low, full = shape((total_rows, length, model), BF), shape((total_rows, length, model), F32)
    pad = pltpu.VMEM((length + 8, width), F32)
    flops = rows * (2 * length * model * (3 * model + model) + 2 * 3 * model * (2 * length) * length // 2)
    operands = (split, keep, x, norm_gain, proj_in, proj_in, proj_in, short_filter, short_filter, cond_filter, slope, shift, skip, proj_out, ffn_gain, *tables)
    return pl.pallas_call(
        functools.partial(mixer_forward_kernel, first_row, len(earlier)),
        out_shape=[low, low, low, low, low, low, full, low],
        grid_spec=pltpu.PrefetchScalarGridSpec(
            num_scalar_prefetch=2,
            grid=(rows, blocks),
            in_specs=[x_row, gain, columns(model, 0), columns(model, 1), columns(model, 2), columns(3, 0), columns(3, 1), columns(3, 0), one, one, one, out_rows, gain] + table_specs + [pl.BlockSpec(memory_space=pl.ANY)] * len(earlier),
            out_specs=[row, part, part, part, part, part, row, row],
            scratch_shapes=[pad, pad, pad] + [pltpu.VMEM((length, width), BF)] * 2 + [
                pltpu.VMEM((2 * length, 2 * width), BF),
                pltpu.VMEM((2 * length, 2 * width), F32),
                pltpu.VMEM((2 * length, width), BF),
                pltpu.VMEM((2 * length, width), F32),
                pltpu.VMEM((length, width), F32),
            ],
        ),
        compiler_params=pltpu.CompilerParams(dimension_semantics=("arbitrary", "arbitrary"), vmem_limit_bytes=LIMIT),
        cost_estimate=pl.CostEstimate(flops=flops, bytes_accessed=rows * length * model * 20, transcendentals=rows * length * model),
        input_output_aliases={len(operands) + k: k for k in range(len(earlier))},
        name="mixer_forward",
    )(*operands, *earlier)


def normal_cdf_pdf(x):
    z = jnp.abs(x) * ROOT_HALF
    t = 1.0 / (1.0 + 0.3275911 * z)
    e = jnp.exp(-z * z)
    poly = t * (0.127414796 + t * (-0.142248368 + t * (0.7107068705 + t * (-0.7265760135 + t * 0.5307027145))))
    tail = poly * e
    return jnp.where(x >= 0, 1.0 - tail, tail), x * e * (1.0 / math.sqrt(2.0 * math.pi))


def ffn_kernel(
    sa_ref, og_ref, sat_ref, ogt_ref, wg_ref, wu_ref, wo_ref, out_ref, back_ref, grads_ref, *scratch
):
    j = pl.program_id(0)
    tokens, model = sa_ref.shape
    streams = [scratch[6 * n : 6 * n + 6] for n in range(2)]
    tile = streams[0][0].shape[0]
    half = tokens // 2
    steps = half // tile
    chunk = 32

    @pl.when(j == 0)
    def _():
        def body(i):
            out_ref[rows_of(i, tile), :] = jnp.zeros((tile, model), F32)
            back_ref[rows_of(i, tile), :] = jnp.zeros((tile, model), F32)

        loop(tokens // tile, body)

    def place(n, i, size=tile, offset=0):
        return pl.ds(pl.multiple_of(n * half + i * tile + offset, size), size)

    def products(n, i):
        gs, us, ds = streams[n][:3]
        rows = place(n, i)
        sa = sa_ref[rows, :]
        gs[...] = mm(sa, wg_ref[...])
        us[...] = mm(sa, wu_ref[...])
        ds[...] = mm_t(og_ref[rows, :], wo_ref[...])

    def elementwise(n, i):
        gs, us, ds, hid, gg, ug = streams[n]
        for c in range(tile // chunk):
            part = slice(c * chunk, (c + 1) * chunk)
            gate, up, dh = gs[part, :], us[part, :], ds[part, :]
            cdf, xpdf = normal_cdf_pdf(gate)
            act = gate * cdf
            target = place(0, i, chunk, c * chunk)
            hid[target, :] = (act * up).astype(BF)
            gg[target, :] = (dh * up * (cdf + xpdf)).astype(BF)
            ug[target, :] = (dh * act).astype(BF)

    def sums(n, i):
        hid, gg, ug = streams[n][3:]
        rows, source = place(n, i), place(0, i)
        out_ref[rows, :] += mm(hid[source, :], wo_ref[...])
        back_ref[rows, :] += mm_t(gg[source, :], wg_ref[...]) + mm_t(ug[source, :], wu_ref[...])

    products(0, 0)
    products(1, 0)
    elementwise(0, 0)

    def body(i):
        products(0, i + 1)
        sums(0, i)
        elementwise(1, i)
        products(1, i + 1)
        sums(1, i)
        elementwise(0, i + 1)

    loop(steps - 1, body)
    last = steps - 1
    sums(0, last)
    elementwise(1, last)
    sums(1, last)
    (hid0, gg0, ug0), (hid1, gg1, ug1) = streams[0][3:], streams[1][3:]
    for k, (ref, first, second) in enumerate(((sat_ref, gg0, gg1), (sat_ref, ug0, ug1), (ogt_ref, hid0, hid1))):
        grads_ref[k] = (mm(ref[:, 0:half], first[...]) + mm(ref[:, half:tokens], second[...])).astype(BF)


def ffn_both(second_act, out_grad, second_turned, grad_turned, ffn_in, ffn_out, share, width=512, tile=512):
    tokens, model = second_act.shape
    total_blocks = ffn_out.shape[0] // width
    first, last = (total_blocks * n // 3 for n in share)
    blocks = last - first
    hidden = blocks * width
    shape = jax.ShapeDtypeStruct
    whole = once((tokens, model), lambda j: (0, 0))
    turned = once((model, tokens), lambda j: (0, 0))
    return pl.pallas_call(
        ffn_kernel,
        out_shape=[shape((tokens, model), F32), shape((tokens, model), F32), shape((3, model, hidden), BF)],
        grid=(blocks,),
        in_specs=[
            whole, whole, turned, turned,
            pl.BlockSpec((model, width), lambda j: (0, j + first)),
            pl.BlockSpec((model, width), lambda j: (0, j + first + total_blocks)),
            pl.BlockSpec((width, model), lambda j: (j + first, 0)),
        ],
        out_specs=[whole, whole, pl.BlockSpec((3, model, width), lambda j: (0, 0, j))],
        scratch_shapes=([pltpu.VMEM((tile, width), F32)] * 3 + [pltpu.VMEM((tokens // 2, width), BF)] * 3) * 2,
        compiler_params=pltpu.CompilerParams(dimension_semantics=("arbitrary",), vmem_limit_bytes=LIMIT),
        cost_estimate=pl.CostEstimate(flops=18 * tokens * model * hidden, bytes_accessed=tokens * model * 24 + model * hidden * 12, transcendentals=tokens * hidden),
        name="ffn_both",
    )(second_act, out_grad, second_turned, grad_turned, ffn_in, ffn_in, ffn_out)


def norm_back_kernel(pieces, resid_ref, *refs):
    sum_refs, back_refs = refs[:pieces], refs[pieces : 2 * pieces]
    og_ref, gain_ref, out_ref, grad_ref, low_ref, gain_grad_ref = refs[2 * pieces :]

    @pl.when(pl.program_id(0) == 0)
    def _():
        gain_grad_ref[...] = jnp.zeros_like(gain_grad_ref)

    tile = 64

    def body(i):
        rows = rows_of(i, tile)
        resid = resid_ref[rows, :]
        n, scale = norm_stats(resid)
        u = sum(ref[rows, :] for ref in back_refs)
        ug = u * gain_ref[...]
        un = u * n
        part = ug - jnp.mean(ug, axis=-1, keepdims=True) - n * jnp.mean(ug * n, axis=-1, keepdims=True)
        grad = og_ref[rows, :].astype(F32) + scale * part
        out_ref[rows, :] = (resid + sum(ref[rows, :] for ref in sum_refs)).astype(BF)
        grad_ref[rows, :] = grad
        low_ref[rows, :] = grad.astype(BF)
        gain_grad_ref[...] += jnp.sum(un.reshape(tile // 8, 8, un.shape[1]), axis=0)

    loop(resid_ref.shape[0] // tile, body)


def norm_back(resid, totals, backs, out_grad, gain, tile=512):
    tokens, model = resid.shape
    pieces = len(totals)
    shape = jax.ShapeDtypeStruct
    block = pl.BlockSpec((tile, model), lambda i: (i, 0))
    fixed = pl.BlockSpec((8, model), lambda i: (0, 0))
    return pl.pallas_call(
        functools.partial(norm_back_kernel, pieces),
        out_shape=[shape((tokens, model), BF), shape((tokens, model), F32), shape((tokens, model), BF), shape((8, model), F32)],
        grid=(tokens // tile,),
        in_specs=[block] * (2 * pieces + 2) + [pl.BlockSpec((1, model), lambda i: (0, 0))],
        out_specs=[block, block, block, fixed],
        compiler_params=pltpu.CompilerParams(dimension_semantics=("arbitrary",), vmem_limit_bytes=LIMIT),
        cost_estimate=pl.CostEstimate(flops=20 * tokens * model, bytes_accessed=tokens * model * 22, transcendentals=tokens),
        name="norm_back",
    )(resid, *totals, *backs, out_grad, gain)


def eight_sum(v):
    return jnp.sum(v.reshape(v.shape[0] // 8, 8, v.shape[1]), axis=0)


def mixer_backward_kernel(
    split_ref, keep_ref, low_ref, q_ref, k_ref, v_ref, mixed_ref, wo_ref,
    fq_ref, fv_ref, fk_ref, slope_ref, shift_ref, skip_ref, fwd_real_ref, fwd_ref, inv_real_ref, inv_ref,
    p_ref, chan_ref,
    qs, ks, vs, xv, xc, xy, y_s, spec_s, u_s, o_s,
):
    r = pl.program_id(1)
    length, width = q_ref.shape
    quarter = length // 4
    split, keep = split_ref[r], keep_ref[r]
    tile = 64

    @pl.when(r == 0)
    def _():
        chan_ref[...] = jnp.zeros_like(chan_ref)

    for ref, source in ((qs, q_ref), (ks, k_ref), (vs, v_ref)):
        ref[0:8, :] = jnp.zeros((8, width), F32)

        def widen(i, ref=ref, source=source):
            ref[pl.ds(pl.multiple_of(8 + i * tile, 8), tile), :] = source[rows_of(i, tile), :].astype(F32)

        loop(length // tile, widen)

    o_s[0:length, 0:width] = mm_t(low_ref[...], wo_ref[...])

    def conv(i):
        t = i * tile
        rows = rows_of(i, tile)
        kept = t + lax.broadcasted_iota(jnp.int32, (tile, width), 0) < keep
        gated_grad = o_s[rows, 0:width]
        low = (gated_grad * conv_back(qs, t, tile, fq_ref, split)).astype(BF)
        xy[rows, :] = low
        value = jnp.where(kept, conv_back(vs, t, tile, fv_ref, split), 0.0).astype(BF)
        xv[rows, :] = value
        xc[rows, :] = jnp.where(kept, conv_back(ks, t, tile, fk_ref, split), 0.0).astype(BF)
        chan_ref[2, :, :] += eight_sum(low.astype(F32) * value.astype(F32))

    loop(length // tile, conv)
    butterfly(xv, y_s, 0, width, quarter)
    butterfly(xc, y_s, width, width, quarter)
    butterfly(xy, y_s, 2 * width, width, quarter)

    def query(i):
        rows = rows_of(i, tile)
        qs[rows, :] = o_s[rows, 0:width] * mixed_ref[rows, :].astype(F32)

    loop(length // tile, query)
    blockwise(y_s, spec_s, fwd_real_ref, fwd_ref, quarter)

    def bins(re, im, first):
        n = 16
        re, im = pl.ds(pl.multiple_of(re, n), n), pl.ds(pl.multiple_of(im, n), n)
        vr, vi = spec_s[re, 0:width], spec_s[im, 0:width]
        cr, ci = spec_s[re, width : 2 * width], spec_s[im, width : 2 * width]
        yr, yi = spec_s[re, 2 * width : 3 * width], spec_s[im, 2 * width : 3 * width]
        slope, shift = slope_ref[...], shift_ref[...]
        rr, ii = cr * cr, ci * ci
        if first:
            edge = lax.broadcasted_iota(jnp.int32, (n, width), 0) == 0
            pr, pi = jnp.where(edge, rr, rr + ii), jnp.where(edge, ii, rr + ii)
            gr, gi = jax.nn.sigmoid(slope * pr + shift), jax.nn.sigmoid(slope * pi + shift)
            ar = vr * yr + jnp.where(edge, 0.0, vi * yi)
            ai = jnp.where(edge, -vi * yi, vi * yr - vr * yi)
            br = ar * cr - jnp.where(edge, 0.0, ai * ci)
            bi = jnp.where(edge, -ai * ci, br)
            wr, wi = br * gr * (1.0 - gr), bi * gi * (1.0 - gi)
            ws = jnp.where(edge, 0.5 * (wr + wi), wr)
            wp = jnp.where(edge, 0.5 * (wr * pr + wi * pi), wr * pr)
            hr, hi = gr * cr, gi * ci
            er = hr * yr + jnp.where(edge, 0.0, hi * yi)
            ei = jnp.where(edge, hi * yi, hr * yi - hi * yr)
            dr = gr * ar + 2.0 * slope * wr * cr
            di = 2.0 * slope * wi * ci - gi * ai
        else:
            p = rr + ii
            g = jax.nn.sigmoid(slope * p + shift)
            ar, ai = vr * yr + vi * yi, vi * yr - vr * yi
            ws = (ar * cr - ai * ci) * (g * (1.0 - g))
            wp = ws * p
            hr, hi = g * cr, g * ci
            er, ei = hr * yr + hi * yi, hr * yi - hi * yr
            k = 2.0 * slope * ws
            dr, di = g * ar + k * cr, k * ci - g * ai
        chan_ref[0, :, :] += eight_sum(wp)
        chan_ref[1, :, :] += eight_sum(ws)
        u_s[re, 0:width] = er.astype(BF)
        u_s[im, 0:width] = ei.astype(BF)
        u_s[re, width : 2 * width] = dr.astype(BF)
        u_s[im, width : 2 * width] = di.astype(BF)

    each_bin(quarter, bins)
    resynth(u_s, o_s, inv_real_ref, inv_ref, quarter)

    def finish(i):
        n = 32
        value = recombine(o_s, slice(0, width), i, n, quarter)
        cond = recombine(o_s, slice(width, 2 * width), i, n, quarter)
        for k in range(4):
            rows = pl.ds(pl.multiple_of(k * quarter + i * n, n), n)
            kept = k * quarter + i * n + lax.broadcasted_iota(jnp.int32, (n, width), 0) < keep
            grad = (value[k] + skip_ref[...] * xy[rows, :].astype(F32)).astype(BF).astype(F32)
            vs[rows, :] = jnp.where(kept, grad, 0.0)
            ks[rows, :] = jnp.where(kept, cond[k].astype(BF).astype(F32), 0.0)

    loop(quarter // 32, finish)
    for ref in (qs, ks, vs):
        ref[length : length + 8, :] = jnp.zeros((8, width), F32)

    for slot, (ref, source, f_ref) in enumerate(((qs, q_ref, fq_ref), (vs, v_ref, fv_ref), (ks, k_ref, fk_ref))):

        def adjoint(i, slot=slot, ref=ref, source=source, f_ref=f_ref):
            t = i * tile
            rows = rows_of(i, tile)
            block = ref[pl.ds(pl.multiple_of(t, tile), tile + 8), :]
            position = t + lax.broadcasted_iota(jnp.int32, (tile, width), 0)
            g0 = block[0:tile]
            g1 = jnp.where(position + 1 != split, block[1 : tile + 1], 0.0)
            g2 = jnp.where((position + 2 != split) & (position + 1 != split), block[2 : tile + 2], 0.0)
            s = source[rows, :].astype(F32)
            place = slice((0, 2, 1)[slot] * width, ((0, 2, 1)[slot] + 1) * width)
            p_ref[rows, place] = (f_ref[0:1, :] * g0 + f_ref[1:2, :] * g1 + f_ref[2:3, :] * g2).astype(BF)
            for k, g in enumerate((g0, g1, g2)):
                chan_ref[3 + 3 * slot + k, :, :] += eight_sum(g * s)

        loop(length // tile, adjoint)


def mixer_backward(branch_low, split, keep, q, k, v, mixed, proj_out, short_filter, cond_filter, slope, shift, skip, tables, width=256):
    rows, length, model = q.shape
    blocks = model // width
    shape = jax.ShapeDtypeStruct
    pad = pltpu.VMEM((length + 8, width), F32)
    quarter = length // 4
    row = pl.BlockSpec((None, length, model), lambda j, r, *_: (r, 0, 0))
    part = pl.BlockSpec((None, length, width), lambda j, r, *_: (r, 0, j))

    def columns(size, offset):
        return pl.BlockSpec((size, width), lambda j, r, *_: (0, j + offset * blocks))

    fixed = lambda j, r, *_: (0, 0)
    table_specs = [once((2 * quarter, quarter), fixed), once((6 * quarter, 2 * quarter), fixed)] * 2
    one = columns(1, 0)
    flops = rows * (2 * length * model * model + 2 * 5 * model * (2 * length) * length // 2)
    return pl.pallas_call(
        mixer_backward_kernel,
        out_shape=[shape((rows, length, 3 * model), BF), shape((12, 8, model), F32)],
        grid_spec=pltpu.PrefetchScalarGridSpec(
            num_scalar_prefetch=2,
            grid=(blocks, rows),
            in_specs=[row, part, part, part, part, pl.BlockSpec((width, model), lambda j, r, *_: (j, 0)), columns(3, 0), columns(3, 1), columns(3, 0), one, one, one] + table_specs,
            out_specs=[pl.BlockSpec((None, length, 3 * width), lambda j, r, *_: (r, 0, j)), pl.BlockSpec((12, 8, width), lambda j, r, *_: (0, 0, j))],
            scratch_shapes=[pad, pad, pad] + [pltpu.VMEM((length, width), BF)] * 3 + [
                pltpu.VMEM((2 * length, 3 * width), BF),
                pltpu.VMEM((2 * length, 3 * width), F32),
                pltpu.VMEM((2 * length, 2 * width), BF),
                pltpu.VMEM((2 * length, 2 * width), F32),
            ],
        ),
        compiler_params=pltpu.CompilerParams(dimension_semantics=("arbitrary", "arbitrary"), vmem_limit_bytes=LIMIT),
        cost_estimate=pl.CostEstimate(flops=flops, bytes_accessed=rows * length * (model * 2 * blocks + model * 14), transcendentals=rows * length * model),
        name="mixer_backward",
    )(split, keep, branch_low, q, k, v, mixed, proj_out, short_filter, short_filter, cond_filter, slope, shift, skip, *tables)


def input_back_kernel(width, x_ref, grad_ref, gain_ref, w_ref, p_ref, in_grad_ref, gain_grad_ref, acc):
    model = x_ref.shape[1]
    tile = 64

    @pl.when(pl.program_id(0) == 0)
    def _():
        gain_grad_ref[...] = jnp.zeros_like(gain_grad_ref)

    total = None
    for b in range(model // width):
        for k in range(3):
            place = (3 * b + k) * width
            term = mm_t(p_ref[:, place : place + width], w_ref[:, k * model + b * width : k * model + (b + 1) * width])
            total = term if total is None else total + term
    acc[...] = total

    def body(i):
        rows = rows_of(i, tile)
        n, scale = norm_stats(x_ref[rows, :].astype(F32))
        u = acc[rows, :]
        ug = u * gain_ref[...]
        part = ug - jnp.mean(ug, axis=-1, keepdims=True) - n * jnp.mean(ug * n, axis=-1, keepdims=True)
        in_grad_ref[rows, :] = (grad_ref[rows, :] + scale * part).astype(in_grad_ref.dtype)
        gain_grad_ref[...] += eight_sum(u * n)

    loop(x_ref.shape[0] // tile, body)


def input_back(x, resid_grad, gain, proj_in, proj_grad, width, tile=512):
    tokens, model = x.shape
    shape = jax.ShapeDtypeStruct
    block = pl.BlockSpec((tile, model), lambda i: (i, 0))
    return pl.pallas_call(
        functools.partial(input_back_kernel, width),
        out_shape=[shape((tokens, model), BF), shape((8, model), F32)],
        grid=(tokens // tile,),
        in_specs=[block, block, once((1, model), lambda i: (0, 0)), once((model, 3 * model), lambda i: (0, 0)), pl.BlockSpec((tile, 3 * model), lambda i: (i, 0))],
        out_specs=[block, pl.BlockSpec((8, model), lambda i: (0, 0))],
        scratch_shapes=[pltpu.VMEM((tile, model), F32)],
        compiler_params=pltpu.CompilerParams(dimension_semantics=("arbitrary",), vmem_limit_bytes=LIMIT),
        cost_estimate=pl.CostEstimate(flops=6 * tokens * model * model, bytes_accessed=tokens * model * 14, transcendentals=tokens),
        name="input_back",
    )(x, resid_grad, gain, proj_in, proj_grad)


def turn(a, b):
    return lax.dot_general(a, b, (((0,), (0,)), ((), ())), preferred_element_type=F32).astype(BF)


def after(value, earlier):
    return lax.optimization_barrier((value, earlier))[0]


def exchange_sum_kernel(rows, seq, x_ref, send_ref, out_ref, other_ref, slots, total, send_sem, recv_sem, far_send_sem, far_recv_sem):
    r, s = lax.axis_index("rows"), lax.axis_index("seq")
    partners = []
    bit = 1
    while bit < rows:
        partners.append((r + bit - 2 * bit * (lax.rem(r // bit, 2)), s))
        bit *= 2
    bit = 1
    while bit < seq:
        partners.append((r, s + bit - 2 * bit * (lax.rem(s // bit, 2))))
        bit *= 2
    barrier = pltpu.get_barrier_semaphore()
    for partner in partners:
        pl.semaphore_signal(barrier, inc=1, device_id=partner, device_id_type=pl.DeviceIdType.MESH)
    pl.semaphore_wait(barrier, len(partners))
    part = other_ref.shape[1]
    far = pltpu.make_async_remote_copy(
        src_ref=send_ref.at[:, pl.ds(pl.multiple_of((1 - s) * part, part), part)], dst_ref=other_ref,
        send_sem=far_send_sem, recv_sem=far_recv_sem, device_id=(r, 1 - s), device_id_type=pl.DeviceIdType.MESH,
    )
    far.start()
    total[0] = x_ref[...]
    for step, partner in enumerate(partners):
        copy = pltpu.make_async_remote_copy(
            src_ref=total.at[step], dst_ref=slots.at[step], send_sem=send_sem.at[step], recv_sem=recv_sem.at[step],
            device_id=partner, device_id_type=pl.DeviceIdType.MESH,
        )
        copy.start()
        copy.wait()
        total[step + 1] = total[step] + slots[step]
    out_ref[...] = total[len(partners)]
    far.wait()


def power_of_two(n):
    return n & (n - 1) == 0


def exchange_sum(value, whole_rows):
    rows, seq = lax.axis_size("rows"), lax.axis_size("seq")
    if not (power_of_two(rows) and seq == 2):
        return lax.psum(value, ("rows", "seq")), scatter_rows(whole_rows).astype(F32)
    steps = rows.bit_length()
    own, length, model = whole_rows.shape
    part = length // 2
    shape = jax.ShapeDtypeStruct
    total, other = pl.pallas_call(
        functools.partial(exchange_sum_kernel, rows, seq),
        out_shape=[shape(value.shape, value.dtype), shape((own, part, model), whole_rows.dtype)],
        in_specs=[pl.BlockSpec(memory_space=pltpu.VMEM), pl.BlockSpec(memory_space=pl.ANY)],
        out_specs=[pl.BlockSpec(memory_space=pltpu.VMEM), pl.BlockSpec(memory_space=pl.ANY)],
        scratch_shapes=[
            pltpu.VMEM((steps, *value.shape), value.dtype),
            pltpu.VMEM((steps + 1, *value.shape), value.dtype),
            pltpu.SemaphoreType.DMA((steps,)),
            pltpu.SemaphoreType.DMA((steps,)),
            pltpu.SemaphoreType.DMA,
            pltpu.SemaphoreType.DMA,
        ],
        compiler_params=pltpu.CompilerParams(collective_id=7, has_side_effects=True),
        cost_estimate=pl.CostEstimate(flops=20_000_000_000, bytes_accessed=0, transcendentals=0),
        name="exchange_sum",
    )(value, whole_rows)
    return total, assemble(whole_rows, other)


def assemble_kernel(own, s_ref, mine_ref, other_ref, out_ref):
    out_ref[...] = jnp.where(pl.program_id(0) // own == s_ref[0], mine_ref[...], other_ref[...]).astype(F32)


def assemble(whole_rows, other):
    own, part, model = other.shape
    block = (None, part, model)
    return pl.pallas_call(
        functools.partial(assemble_kernel, own),
        out_shape=jax.ShapeDtypeStruct((2 * own, part, model), F32),
        grid_spec=pltpu.PrefetchScalarGridSpec(
            num_scalar_prefetch=1,
            grid=(2 * own,),
            in_specs=[pl.BlockSpec(block, lambda i, s: (i % own, s[0], 0)), pl.BlockSpec(block, lambda i, s: (i % own, 0, 0))],
            out_specs=pl.BlockSpec(block, lambda i, s: (i, 0, 0)),
        ),
        compiler_params=pltpu.CompilerParams(dimension_semantics=("arbitrary",), vmem_limit_bytes=LIMIT),
        name="assemble",
    )(lax.axis_index("seq").astype(jnp.int32)[None], whole_rows, other)


def swapped(value):
    count = lax.axis_size("seq")
    return lax.ppermute(value, "seq", [(i, (i + 1) % count) for i in range(count)])


def gather_rows(value, first=0, count=None):
    own = value.shape[0] // lax.axis_size("seq")
    count = own if count is None else count
    if lax.axis_size("seq") != 2:
        whole = lax.all_to_all(value, "seq", split_axis=0, concat_axis=1, tiled=True)
        return whole[first : first + count]
    s = lax.axis_index("seq")
    mine = lax.dynamic_slice_in_dim(value, s * own + first, count)
    other = swapped(lax.dynamic_slice_in_dim(value, (1 - s) * own + first, count))
    return jnp.concatenate([jnp.where(s == 0, mine, other), jnp.where(s == 0, other, mine)], axis=1)


def scatter_rows(value):
    if lax.axis_size("seq") != 2:
        return lax.all_to_all(value, "seq", split_axis=1, concat_axis=0, tiled=True)
    s = lax.axis_index("seq")
    part = value.shape[1] // 2
    mine = lax.dynamic_slice_in_dim(value, s * part, part, axis=1)
    other = swapped(lax.dynamic_slice_in_dim(value, (1 - s) * part, part, axis=1))
    return jnp.concatenate([jnp.where(s == 0, mine, other), jnp.where(s == 0, other, mine)], axis=0)


def seq_sum(value):
    if lax.axis_size("seq") != 2:
        return lax.psum(value, "seq").astype(F32)
    return value.astype(F32) + swapped(value).astype(F32)


def per_device_rows(inputs, split_point, keep_mask, norm_gain, proj_in, short_filter, cond_filter, spec_slope, spec_shift, skip_gain, proj_out, ffn_gain, ffn_in, ffn_out, out_grad):
    local_rows, local_len, model = inputs.shape
    count = lax.axis_size("seq")
    own = local_rows // count
    length = local_len * count
    tokens = own * length
    width = 256
    first_row = lax.axis_index("seq") * own
    flat = lambda a: a.reshape(tokens, model)
    flat_wide = lambda a: a.reshape(tokens, 3 * model)
    shaped = lambda a: a.reshape(own, length, model)
    lift = lambda a: a.reshape(1, -1)

    pieces = [(0, 1), (1, own - 1)] if own > 1 else [(0, own)]
    xs = []
    for start, size in pieces:
        xs.append(gather_rows(after(inputs, xs) if xs else inputs, start, size))
    kept = jnp.sum(keep_mask, axis=1)
    kept = kept + swapped(kept) if count == 2 else lax.psum(kept, "seq")
    keep = lax.dynamic_slice_in_dim(kept, first_row, own)
    split = lax.dynamic_slice_in_dim(split_point, first_row, own)
    tables = spectral_tables(length, lax.axis_index("seq") * (2 * length))
    slope, shift, skip = lift(spec_slope), lift(spec_shift), lift(skip_gain)

    held = ()
    for x, (start, size) in zip(xs, pieces):
        held = mixer_forward(
            x, split, keep, lift(norm_gain), proj_in, short_filter, cond_filter, slope, shift, skip, proj_out, lift(ffn_gain), tables, start, own, held
        )
        if start == 0:
            whole_grad = flat(gather_rows(after(out_grad, (xs[-1], held[-1]))))
    first, q, k, v, mixed, gated, resid, second = held
    x = jnp.concatenate(xs, axis=0)
    second = flat(second)
    second_turned, grad_turned = second.T, whole_grad.T
    totals, backs, grads = [], [], []
    for share in ((0, 1), (1, 3)):
        total, back, grad = ffn_both(second, whole_grad, second_turned, grad_turned, ffn_in, ffn_out, share)
        totals.append(total)
        backs.append(back)
        grads.append(grad)
    early_share = lax.psum_scatter(grads[0], "rows", scatter_dimension=1, tiled=True)
    output, resid_grad, branch_low, ffn_gain_part = norm_back(flat(resid), totals, backs, whole_grad, lift(ffn_gain))
    output = scatter_rows(shaped(output))
    out_part = turn(flat(gated), branch_low)
    grad, branch_low, early_share = lax.optimization_barrier((grads[1], branch_low, early_share))
    late_share = lax.psum_scatter(grad, "rows", scatter_dimension=1, tiled=True)
    proj_grad, chan = mixer_backward(shaped(branch_low), split, keep, q, k, v, mixed, proj_out, short_filter, cond_filter, slope, shift, skip, tables)
    proj_grad = flat_wide(proj_grad)
    mix_part = jnp.concatenate([out_part, turn(flat(first), proj_grad)], axis=1)
    mix_part, late_share = lax.optimization_barrier((mix_part, late_share))
    mix_share = lax.psum_scatter(mix_part, "rows", scatter_dimension=0, tiled=True)
    proj_grad = after(proj_grad, mix_part)
    input_grad, norm_gain_part = input_back(flat(x), resid_grad, lift(norm_gain), proj_in, proj_grad, width)
    ffn_shares = [seq_sum(early_share), seq_sum(late_share)]
    small = jnp.sum(jnp.concatenate([ffn_gain_part[None], norm_gain_part[None], chan], 0), axis=1)
    small, input_grad = exchange_sum(small, shaped(input_grad))
    scale = 1.0 / length
    mix_share = seq_sum(mix_share)
    in_share = mix_share[:, model:].reshape(-1, model // width, 3, width).transpose(0, 2, 1, 3)
    return (
        output,
        input_grad,
        small[1],
        in_share.reshape(-1, 3 * model),
        jnp.concatenate([small[5:8], small[8:11]], axis=1),
        small[11:14],
        small[2] * scale,
        small[3] * scale,
        small[4],
        mix_share[:, :model],
        small[0],
        jnp.concatenate([share[k] for k in range(2) for share in ffn_shares], axis=1),
        jnp.concatenate([share[2] for share in ffn_shares], axis=1).T,
    )


PRECISE = lax.Precision.HIGH


def passed_along(value, axis, steps):
    count = lax.axis_size(axis)
    leading, last = (max(0, -steps), min(count, count - steps))
    return lax.ppermute(value, axis, [(source, source + steps) for source in range(leading, last)])


def layer_norm(values, scaling):
    center = values - jnp.mean(values, axis=-1, keepdims=True)
    spread = jnp.mean(center * center, axis=-1, keepdims=True)
    return center * lax.rsqrt(spread + EPSILON) * scaling


def conv_three(extended, weights, same_one, same_two):
    length = extended.shape[1] - 2
    return (
        weights[0] * extended[:, 2:]
        + weights[1] * extended[:, 1 : length + 1] * same_one
        + weights[2] * extended[:, :length] * same_two
    )


def dft_tables(seq_length):
    table_shape = (seq_length + 1, seq_length)
    product = lax.broadcasted_iota(jnp.int32, table_shape, 0) * lax.broadcasted_iota(
        jnp.int32, table_shape, 1
    )
    angles = (product % (2 * seq_length)).astype(jnp.float32) * (math.pi / seq_length)
    freq = lax.broadcasted_iota(jnp.int32, (seq_length + 1, 1), 0)
    edge = jnp.logical_or(freq == 0, freq == seq_length)
    weights = jnp.where(edge, 1.0, 2.0).astype(jnp.float32) / (2.0 * seq_length)
    return (jnp.cos(angles), jnp.sin(angles), weights)


def analyze(values, conds, cos_table, sin_table):
    value_real = jnp.einsum("ft,ktd->kfd", cos_table, values, precision=PRECISE)
    value_imag = -jnp.einsum("ft,ktd->kfd", sin_table, values, precision=PRECISE)
    cond_real = jnp.einsum("ft,ktd->kfd", cos_table, conds, precision=PRECISE)
    cond_imag = -jnp.einsum("ft,ktd->kfd", sin_table, conds, precision=PRECISE)
    return (value_real, value_imag, cond_real, cond_imag)


def synth(
    value_real,
    value_imag,
    cond_real,
    cond_imag,
    values,
    slopes,
    shifts,
    skip_gains,
    cos_table,
    sin_table,
    freq_weights,
):
    factor = jax.nn.sigmoid(slopes * (cond_real * cond_real + cond_imag * cond_imag) + shifts)
    filter_real = cond_real * factor
    filter_imag = cond_imag * factor
    prod_real = (value_real * filter_real - value_imag * filter_imag) * freq_weights
    prod_imag = (value_real * filter_imag + value_imag * filter_real) * freq_weights
    mixed_out = jnp.einsum("ft,kfd->ktd", cos_table, prod_real, precision=PRECISE) - jnp.einsum(
        "ft,kfd->ktd", sin_table, prod_imag, precision=PRECISE
    )
    return mixed_out + skip_gains * values


def times_transpose(left, right):
    return lax.dot_general(
        left, right, (((1,), (1,)), ((), ())), preferred_element_type=jnp.float32
    )


def transpose_times(left, right):
    return lax.dot_general(
        left, right, (((0,), (0,)), ((), ())), preferred_element_type=jnp.float32
    )


def per_device(
    inputs,
    split_point,
    keep_mask,
    norm_gain,
    proj_in,
    short_filter,
    cond_filter,
    spec_slope,
    spec_shift,
    skip_gain,
    proj_out,
    ffn_gain,
    ffn_in,
    ffn_out,
    out_grad,
):
    local_rows, local_len, model_width = inputs.shape
    hidden_width = ffn_out.shape[0]
    seq_count = lax.axis_size("seq")
    seq_index = lax.axis_index("seq")
    full_len = local_len * seq_count
    chan_width = model_width // seq_count
    token_count = local_rows * local_len
    positions = seq_index * local_len + lax.broadcasted_iota(jnp.int32, (local_rows, local_len), 1)
    splits = split_point[:, None]
    segment = positions >= splits
    same_one = (segment == (positions - 1 >= splits)).astype(jnp.float32)[:, :, None]
    same_two = (segment == (positions - 2 >= splits)).astype(jnp.float32)[:, :, None]
    keep_float = keep_mask.astype(jnp.float32)[:, :, None]
    flat_in = inputs.reshape(token_count, model_width).astype(jnp.float32)
    normed_one, norm_one_back = jax.vjp(layer_norm, flat_in, norm_gain)
    first_act = normed_one.astype(jnp.bfloat16)
    projected = jnp.dot(first_act, proj_in, preferred_element_type=jnp.float32).astype(jnp.bfloat16)
    proj_rows = projected.reshape(local_rows, local_len, 3 * model_width)
    edge_values = passed_along(proj_rows[:, local_len - 2 :, :], "seq", 1)
    extended = jnp.concatenate([edge_values, proj_rows], axis=1).astype(jnp.float32)

    def mixer_local(ext_values, short_weights, cond_weights):
        query_value = jnp.concatenate(
            [ext_values[:, :, :model_width], ext_values[:, :, 2 * model_width :]], axis=2
        )
        conv_both = conv_three(query_value, short_weights, same_one, same_two)
        cond_conv = conv_three(
            ext_values[:, :, model_width : 2 * model_width], cond_weights, same_one, same_two
        )
        return (
            conv_both[:, :, :model_width],
            conv_both[:, :, model_width:] * keep_float,
            cond_conv * keep_float,
        )

    (query_conv, value_masked, cond_masked), mixer_back = jax.vjp(
        mixer_local, extended, short_filter, cond_filter
    )
    value_low = value_masked.astype(jnp.bfloat16)
    cond_low = cond_masked.astype(jnp.bfloat16)
    slope_part = lax.dynamic_slice_in_dim(spec_slope, seq_index * chan_width, chan_width)
    shift_part = lax.dynamic_slice_in_dim(spec_shift, seq_index * chan_width, chan_width)
    skip_part = lax.dynamic_slice_in_dim(skip_gain, seq_index * chan_width, chan_width)
    cos_table, sin_table, freq_weights = dft_tables(full_len)

    def synth_local(
        value_real, value_imag, cond_real, cond_imag, values, slopes, shifts, skip_gains
    ):
        return synth(
            value_real,
            value_imag,
            cond_real,
            cond_imag,
            values,
            slopes,
            shifts,
            skip_gains,
            cos_table,
            sin_table,
            freq_weights,
        )

    value_chan = lax.all_to_all(value_low, "seq", split_axis=2, concat_axis=1, tiled=True)
    cond_chan = lax.all_to_all(cond_low, "seq", split_axis=2, concat_axis=1, tiled=True)
    value_float = value_chan.astype(jnp.float32)
    spectra = analyze(value_float, cond_chan.astype(jnp.float32), cos_table, sin_table)
    mixed_chan = synth_local(
        spectra[0],
        spectra[1],
        spectra[2],
        spectra[3],
        value_float,
        slope_part,
        shift_part,
        skip_part,
    ).astype(jnp.bfloat16)
    mixed_home = lax.all_to_all(mixed_chan, "seq", split_axis=1, concat_axis=2, tiled=True)
    mixed_float = mixed_home.astype(jnp.float32)
    gated = (query_conv * mixed_float).astype(jnp.bfloat16).reshape(token_count, model_width)
    branch = jnp.dot(gated, proj_out, preferred_element_type=jnp.float32)
    resid = flat_in + branch
    normed_two, norm_two_back = jax.vjp(layer_norm, resid, ffn_gain)
    second_act = normed_two.astype(jnp.bfloat16)
    gate_up = jnp.dot(second_act, ffn_in, preferred_element_type=jnp.float32)

    def glu_local(both_parts):
        return (
            jax.nn.gelu(both_parts[:, :hidden_width], approximate=False)
            * both_parts[:, hidden_width:]
        )

    hidden, glu_back = jax.vjp(glu_local, gate_up)
    hidden_low = hidden.astype(jnp.bfloat16)
    result = resid + jnp.dot(hidden_low, ffn_out, preferred_element_type=jnp.float32)
    output = result.astype(jnp.bfloat16).reshape(local_rows, local_len, model_width)
    flat_grad = out_grad.reshape(token_count, model_width)
    hidden_grad = times_transpose(flat_grad, ffn_out)
    (gate_up_grad,) = glu_back(hidden_grad)
    gate_up_low = gate_up_grad.astype(jnp.bfloat16)
    second_grad = times_transpose(gate_up_low, ffn_in)
    resid_part, ffn_gain_part = norm_two_back(second_grad)
    resid_grad = flat_grad.astype(jnp.float32) + resid_part
    branch_low = resid_grad.astype(jnp.bfloat16)
    gated_grad = times_transpose(branch_low, proj_out).reshape(local_rows, local_len, model_width)
    query_grad = gated_grad * mixed_float
    mixed_grad = (gated_grad * query_conv).astype(jnp.bfloat16)
    grad_chan = lax.all_to_all(mixed_grad, "seq", split_axis=2, concat_axis=1, tiled=True)
    grad_float = grad_chan.astype(jnp.float32)
    item_count = grad_chan.shape[0]
    slope_items = jnp.broadcast_to(slope_part, (item_count, 1, chan_width))
    shift_items = jnp.broadcast_to(shift_part, (item_count, 1, chan_width))
    skip_items = jnp.broadcast_to(skip_part, (item_count, 1, chan_width))
    value_float = value_chan.astype(jnp.float32)

    def spectral(values, conds, slopes, shifts, skip_gains):
        spectra = analyze(values, conds, cos_table, sin_table)
        return synth_local(
            spectra[0], spectra[1], spectra[2], spectra[3], values, slopes, shifts, skip_gains
        )

    unused, pull = jax.vjp(
        spectral, value_float, cond_chan.astype(jnp.float32), slope_items, shift_items, skip_items
    )
    value_back, cond_back, slope_rows, shift_rows, skip_rows = pull(grad_float)
    value_grad, cond_grad = (
        lax.all_to_all(
            value_back.astype(jnp.bfloat16), "seq", split_axis=1, concat_axis=2, tiled=True
        ),
        lax.all_to_all(
            cond_back.astype(jnp.bfloat16), "seq", split_axis=1, concat_axis=2, tiled=True
        ),
    )
    start_chan = (seq_index * chan_width,)
    empty_width = jnp.zeros((model_width,), jnp.float32)
    slope_full = lax.dynamic_update_slice(empty_width, jnp.sum(slope_rows, axis=(0, 1)), start_chan)
    shift_full = lax.dynamic_update_slice(empty_width, jnp.sum(shift_rows, axis=(0, 1)), start_chan)
    skip_full = lax.dynamic_update_slice(empty_width, jnp.sum(skip_rows, axis=(0, 1)), start_chan)
    ext_grad, short_grad, cond_weight_grad = mixer_back(
        (query_grad, value_grad.astype(jnp.float32), cond_grad.astype(jnp.float32))
    )
    incoming = passed_along(ext_grad[:, :2, :].astype(jnp.bfloat16), "seq", -1).astype(jnp.float32)
    proj_grad = ext_grad[:, 2:, :] + jnp.pad(incoming, ((0, 0), (local_len - 2, 0), (0, 0)))
    proj_low = proj_grad.astype(jnp.bfloat16).reshape(token_count, 3 * model_width)
    first_grad = times_transpose(proj_low, proj_in)
    input_part, norm_gain_part = norm_one_back(first_grad)
    input_grad = (resid_grad + input_part).reshape(local_rows, local_len, model_width)
    share = lax.psum_scatter(
        jnp.concatenate(
            [
                transpose_times(first_act, proj_low),
                transpose_times(gated, branch_low),
                transpose_times(second_act, gate_up_low),
                transpose_times(flat_grad, hidden_low),
            ],
            axis=1,
        ).astype(jnp.bfloat16),
        "rows",
        scatter_dimension=0,
        tiled=True,
    )
    summed = lax.psum(share, "seq").astype(jnp.float32)
    small_sums = lax.psum(
        (
            norm_gain_part,
            short_grad,
            cond_weight_grad,
            slope_full,
            shift_full,
            skip_full,
            ffn_gain_part,
        ),
        ("rows", "seq"),
    )
    proj_in_grad = summed[:, : 3 * model_width]
    proj_out_grad = summed[:, 3 * model_width : 4 * model_width]
    ffn_in_grad = summed[:, 4 * model_width : 4 * model_width + 2 * hidden_width]
    ffn_out_grad = jnp.transpose(summed[:, 4 * model_width + 2 * hidden_width :])
    return (
        output,
        input_grad,
        small_sums[0],
        proj_in_grad,
        small_sums[1],
        small_sums[2],
        small_sums[3],
        small_sums[4],
        small_sums[5],
        proj_out_grad,
        small_sums[6],
        ffn_in_grad,
        ffn_out_grad,
    )


def per_device_any(*args):
    rows, width = args[0].shape[0], args[0].shape[2]
    even = rows % lax.axis_size("seq") == 0 and width % 256 == 0
    return (per_device_rows if even else per_device)(*args)


def solution(mesh):
    in_specs = (
        P("rows", "seq", None),
        P("rows"),
        P("rows", "seq"),
        P(),
        P(),
        P(),
        P(),
        P(),
        P(),
        P(),
        P(),
        P(),
        P(),
        P(),
        P("rows", "seq", None),
    )
    out_specs = (
        P("rows", "seq", None),
        P("rows", "seq", None),
        P(),
        P("rows", None),
        P(),
        P(),
        P(),
        P(),
        P(),
        P("rows", None),
        P(),
        P("rows", None),
        P(None, "rows"),
    )
    return jax.shard_map(
        per_device_any, mesh=mesh, in_specs=in_specs, out_specs=out_specs, check_vma=False
    )
```

```python
import functools
import math

import jax
import jax.numpy as jnp
from jax import lax
from jax.experimental import pallas as pl
from jax.experimental.pallas import tpu as pltpu
from jax.sharding import PartitionSpec as P

EPSILON = 1e-05
BF = jnp.bfloat16
F32 = jnp.float32
ROOT_HALF = math.sqrt(0.5)
LIMIT = 67043328


def mm(a, b):
    return lax.dot_general(a, b, (((1,), (0,)), ((), ())), preferred_element_type=F32)


def mm_t(a, b):
    return lax.dot_general(a, b, (((1,), (1,)), ((), ())), preferred_element_type=F32)


def spectral_tables(length, offset):
    quarter = length // 4
    two_n = 2 * length
    m = lax.broadcasted_iota(jnp.int32, (quarter, quarter), 0)
    s = lax.broadcasted_iota(jnp.int32, (quarter, quarter), 1)

    def cos_sin(freq):
        angle = ((freq * s + offset) % two_n).astype(F32) * (2.0 * math.pi / two_n)
        return jnp.cos(angle), jnp.sin(angle)

    half = quarter // 2
    forward, inverse = [], []
    for r in (1, 2, 3):
        c, sn = cos_sin(8 * m + r)
        forward.append(jnp.concatenate([jnp.concatenate([c, sn], 1), jnp.concatenate([-sn, c], 1)], 0))
        inverse.append(forward[-1].T * (2.0 / two_n))
    row = m % half
    low = m < half
    c, sn = cos_sin(8 * jnp.where(m == half, half, row))
    zero = jnp.where(low | (m == half), c, -sn)
    c4, sn4 = cos_sin(8 * row + 4)
    four = jnp.where(low, c4, -sn4)
    edge = jnp.where((m == 0) | (m == half), 1.0, 2.0) / two_n
    fwd_real = jnp.concatenate([zero, four], 0)
    inv_real = jnp.concatenate([(zero * edge).T, four.T * (2.0 / two_n)], 0)
    return (
        fwd_real.astype(BF),
        jnp.concatenate(forward, 0).astype(BF),
        inv_real.astype(BF),
        jnp.concatenate(inverse, 0).astype(BF),
    )


def loop(count, body, unroll=1):
    lax.fori_loop(0, count, lambda i, c: (body(i), c)[1], 0, unroll=unroll)


def rows_of(i, size):
    return pl.ds(pl.multiple_of(i * size, size), size)


def norm_stats(v):
    center = v - jnp.mean(v, axis=-1, keepdims=True)
    scale = lax.rsqrt(jnp.mean(center * center, axis=-1, keepdims=True) + EPSILON)
    return center * scale, scale


def same_masks(position, split):
    same_one = position != split
    return same_one, same_one & (position != split + 1)


def butterfly(x_ref, y_ref, lane, width, quarter):
    tile = 32
    lanes = slice(lane, lane + width)

    def body(i):
        x0, x1, x2, x3 = [
            x_ref[pl.ds(pl.multiple_of(q * quarter + i * tile, tile), tile), :].astype(F32) for q in range(4)
        ]
        a, b, c, d = x0 + x2, x1 + x3, x0 - x2, x1 - x3
        sd, sb = d * ROOT_HALF, b * ROOT_HALF
        out = (a + b, a - b, x0 + sd, -x2 - sb, c, -d, x0 - sd, x2 - sb)
        for k, value in enumerate(out):
            y_ref[pl.ds(pl.multiple_of(k * quarter + i * tile, tile), tile), lanes] = value.astype(BF)

    loop(quarter // tile, body)


def blockwise(y_ref, spec_ref, fwd_real_ref, fwd_ref, quarter):
    q = quarter
    for k in range(2):
        spec_ref[k * q : (k + 1) * q, :] = mm(fwd_real_ref[k * q : (k + 1) * q, :], y_ref[k * q : (k + 1) * q, :])
    for k in range(3):
        spec_ref[2 * q + 2 * k * q : 2 * q + 2 * (k + 1) * q, :] = mm(
            fwd_ref[2 * k * q : 2 * (k + 1) * q, :], y_ref[2 * q + 2 * k * q : 2 * q + 2 * (k + 1) * q, :]
        )


def resynth(u_ref, out_ref, inv_real_ref, inv_ref, quarter):
    blockwise(u_ref, out_ref, inv_real_ref, inv_ref, quarter)


def each_bin(quarter, body, tile=64):
    half = quarter // 2
    body(0, half, True)

    def run(base, span, skip):
        def step(i):
            start = base + (i + skip) * tile
            body(start, start + span, False)

        loop(span // tile - skip, step)

    run(0, half, 1)
    run(quarter, half, 0)
    for k in range(3):
        run(2 * quarter + 2 * k * quarter, quarter, 0)


def recombine(o_ref, lanes, i, tile, quarter):
    def part(k):
        return o_ref[pl.ds(pl.multiple_of(k * quarter + i * tile, tile), tile), lanes]

    u0, u4, a1, b1, a2, b2, a3, b3 = [part(k) for k in range(8)]
    even, odd = u0 + u4, u0 - u4
    return (
        even + a1 + a2 + a3,
        odd + (a1 - b1 - a3 - b3) * ROOT_HALF - b2,
        even - b1 - a2 + b3,
        odd + (a3 - b3 - a1 - b1) * ROOT_HALF + b2,
    )


def conv_back(ref, t, tile, weights, split):
    block = ref[pl.ds(pl.multiple_of(t, tile), tile + 8), :]
    width = block.shape[1]
    position = t + lax.broadcasted_iota(jnp.int32, (tile, width), 0)
    one, two = same_masks(position, split)
    return (
        weights[0:1, :] * block[8 : tile + 8]
        + jnp.where(one, weights[1:2, :] * block[7 : tile + 7], 0.0)
        + jnp.where(two, weights[2:3, :] * block[6 : tile + 6], 0.0)
    )


def mixer_forward_kernel(
    first_row, earlier, split_ref, keep_ref, x_ref, norm_gain_ref, wq_ref, wk_ref, wv_ref, fq_ref, fv_ref, fk_ref, slope_ref, shift_ref,
    skip_ref, wo_ref, ffn_gain_ref, fwd_real_ref, fwd_ref, inv_real_ref, inv_ref,
    *refs,
):
    first_ref, q_ref, k_ref, v_ref, mixed_ref, gated_ref, resid_ref, second_ref = refs[earlier : earlier + 8]
    qs, ks, vs, xv, xc, y_s, spec_s, u_s, o_s, qc = refs[earlier + 8 :]
    r, j = first_row + pl.program_id(0), pl.program_id(1)
    length, width = q_ref.shape
    quarter = length // 4
    split, keep = split_ref[r], keep_ref[r]
    tile = 128

    @pl.when(j == 0)
    def _():
        def body(i):
            rows = rows_of(i, tile)
            v = x_ref[rows, :].astype(F32)
            n, _ = norm_stats(v)
            first_ref[rows, :] = (n * norm_gain_ref[...]).astype(BF)
            resid_ref[rows, :] = v

        loop(length // tile, body, 2)
        for ref in (qs, ks, vs):
            ref[0:8, :] = jnp.zeros((8, width), F32)

    for w_ref, out_ref, ref in ((wq_ref, q_ref, qs), (wk_ref, k_ref, ks), (wv_ref, v_ref, vs)):
        value = mm(first_ref[...], w_ref[...]).astype(BF)
        out_ref[...] = value
        ref[8 : 8 + length, :] = value.astype(F32)

    def conv(i):
        t = i * tile
        rows = rows_of(i, tile)
        kept = t + lax.broadcasted_iota(jnp.int32, (tile, width), 0) < keep
        qc[rows, :] = conv_back(qs, t, tile, fq_ref, split)
        xv[rows, :] = jnp.where(kept, conv_back(vs, t, tile, fv_ref, split), 0.0).astype(BF)
        xc[rows, :] = jnp.where(kept, conv_back(ks, t, tile, fk_ref, split), 0.0).astype(BF)

    loop(length // tile, conv)
    butterfly(xv, y_s, 0, width, quarter)
    butterfly(xc, y_s, width, width, quarter)
    blockwise(y_s, spec_s, fwd_real_ref, fwd_ref, quarter)

    def bins(re, im, first):
        n = 64
        re, im = pl.ds(pl.multiple_of(re, n), n), pl.ds(pl.multiple_of(im, n), n)
        vr, vi = spec_s[re, 0:width], spec_s[im, 0:width]
        cr, ci = spec_s[re, width : 2 * width], spec_s[im, width : 2 * width]
        slope, shift = slope_ref[...], shift_ref[...]
        rr, ii = cr * cr, ci * ci
        if first:
            edge = lax.broadcasted_iota(jnp.int32, (n, width), 0) == 0
            hr = cr * jax.nn.sigmoid(slope * jnp.where(edge, rr, rr + ii) + shift)
            hi = ci * jax.nn.sigmoid(slope * jnp.where(edge, ii, rr + ii) + shift)
            ur = vr * hr - jnp.where(edge, 0.0, vi * hi)
            ui = jnp.where(edge, vi * hi, vr * hi + vi * hr)
        else:
            gain = jax.nn.sigmoid(slope * (rr + ii) + shift)
            hr, hi = cr * gain, ci * gain
            ur, ui = vr * hr - vi * hi, vr * hi + vi * hr
        u_s[re, :] = ur.astype(BF)
        u_s[im, :] = ui.astype(BF)

    each_bin(quarter, bins)
    resynth(u_s, o_s, inv_real_ref, inv_ref, quarter)

    def finish(i):
        n = 32
        parts = recombine(o_s, slice(0, width), i, n, quarter)
        for k, part in enumerate(parts):
            rows = pl.ds(pl.multiple_of(k * quarter + i * n, n), n)
            mixed = (part + skip_ref[...] * xv[rows, :].astype(F32)).astype(BF)
            mixed_ref[rows, :] = mixed
            gated_ref[rows, :] = (qc[rows, :] * mixed.astype(F32)).astype(BF)

    loop(quarter // 32, finish)
    resid_ref[...] += mm(gated_ref[...], wo_ref[...])

    @pl.when(j == pl.num_programs(1) - 1)
    def _():
        def body(i):
            rows = rows_of(i, tile)
            n, _ = norm_stats(resid_ref[rows, :])
            second_ref[rows, :] = (n * ffn_gain_ref[...]).astype(BF)

        loop(length // tile, body, 2)


def once(shape, index):
    return pl.BlockSpec(shape, index, pipeline_mode=pl.Buffered(1))


def mixer_specs(length, model, width, first_row):
    blocks = model // width
    row = pl.BlockSpec((None, length, model), lambda r, j, *_: (r + first_row, 0, 0))
    part = pl.BlockSpec((None, length, width), lambda r, j, *_: (r + first_row, 0, j))

    def columns(rows, offset):
        return pl.BlockSpec((rows, width), lambda r, j, *_: (0, j + offset * blocks))

    out_rows = pl.BlockSpec((width, model), lambda r, j, *_: (j, 0))
    gain = once((1, model), lambda r, j, *_: (0, 0))
    q = length // 4
    tables = [once((2 * q, q), lambda r, j, *_: (0, 0)), once((6 * q, 2 * q), lambda r, j, *_: (0, 0))]
    return blocks, row, part, columns, out_rows, gain, tables + tables


def mixer_forward(x, split, keep, norm_gain, proj_in, short_filter, cond_filter, slope, shift, skip, proj_out, ffn_gain, tables, first_row, total_rows, earlier, width=256):
    rows, length, model = x.shape
    blocks, row, part, columns, out_rows, gain, table_specs = mixer_specs(length, model, width, first_row)
    x_row = pl.BlockSpec((None, length, model), lambda r, j, *_: (r, 0, 0))
    one = columns(1, 0)
    shape = jax.ShapeDtypeStruct
    low, full = shape((total_rows, length, model), BF), shape((total_rows, length, model), F32)
    pad = pltpu.VMEM((length + 8, width), F32)
    flops = rows * (2 * length * model * (3 * model + model) + 2 * 3 * model * (2 * length) * length // 2)
    operands = (split, keep, x, norm_gain, proj_in, proj_in, proj_in, short_filter, short_filter, cond_filter, slope, shift, skip, proj_out, ffn_gain, *tables)
    return pl.pallas_call(
        functools.partial(mixer_forward_kernel, first_row, len(earlier)),
        out_shape=[low, low, low, low, low, low, full, low],
        grid_spec=pltpu.PrefetchScalarGridSpec(
            num_scalar_prefetch=2,
            grid=(rows, blocks),
            in_specs=[x_row, gain, columns(model, 0), columns(model, 1), columns(model, 2), columns(3, 0), columns(3, 1), columns(3, 0), one, one, one, out_rows, gain] + table_specs + [pl.BlockSpec(memory_space=pl.ANY)] * len(earlier),
            out_specs=[row, part, part, part, part, part, row, row],
            scratch_shapes=[pad, pad, pad] + [pltpu.VMEM((length, width), BF)] * 2 + [
                pltpu.VMEM((2 * length, 2 * width), BF),
                pltpu.VMEM((2 * length, 2 * width), F32),
                pltpu.VMEM((2 * length, width), BF),
                pltpu.VMEM((2 * length, width), F32),
                pltpu.VMEM((length, width), F32),
            ],
        ),
        compiler_params=pltpu.CompilerParams(dimension_semantics=("arbitrary", "arbitrary"), vmem_limit_bytes=LIMIT),
        cost_estimate=pl.CostEstimate(flops=flops, bytes_accessed=rows * length * model * 20, transcendentals=rows * length * model),
        input_output_aliases={len(operands) + k: k for k in range(len(earlier))},
        name="mixer_forward",
    )(*operands, *earlier)


def normal_cdf_pdf(x):
    z = jnp.abs(x) * ROOT_HALF
    t = 1.0 / (1.0 + 0.3275911 * z)
    e = jnp.exp(-z * z)
    poly = t * (0.127414796 + t * (-0.142248368 + t * (0.7107068705 + t * (-0.7265760135 + t * 0.5307027145))))
    tail = poly * e
    return jnp.where(x >= 0, 1.0 - tail, tail), x * e * (1.0 / math.sqrt(2.0 * math.pi))


def ffn_kernel(
    sa_ref, og_ref, sat_ref, ogt_ref, wg_ref, wu_ref, wo_ref, out_low_ref, back_low_ref, grads_ref, out_ref, back_ref, *scratch
):
    j = pl.program_id(0)
    tokens, model = sa_ref.shape
    streams = [scratch[6 * n : 6 * n + 6] for n in range(2)]
    tile = streams[0][0].shape[0]
    half = tokens // 2
    steps = half // tile
    chunk = 32

    @pl.when(j == 0)
    def _():
        def body(i):
            out_ref[rows_of(i, tile), :] = jnp.zeros((tile, model), F32)
            back_ref[rows_of(i, tile), :] = jnp.zeros((tile, model), F32)

        loop(tokens // tile, body)

    def place(n, i, size=tile, offset=0):
        return pl.ds(pl.multiple_of(n * half + i * tile + offset, size), size)

    def products(n, i):
        gs, us, ds = streams[n][:3]
        rows = place(n, i)
        sa = sa_ref[rows, :]
        gs[...] = mm(sa, wg_ref[...])
        us[...] = mm(sa, wu_ref[...])
        ds[...] = mm_t(og_ref[rows, :], wo_ref[...])

    def elementwise(n, i):
        gs, us, ds, hid, gg, ug = streams[n]
        for c in range(tile // chunk):
            part = slice(c * chunk, (c + 1) * chunk)
            gate, up, dh = gs[part, :], us[part, :], ds[part, :]
            cdf, xpdf = normal_cdf_pdf(gate)
            act = gate * cdf
            target = place(0, i, chunk, c * chunk)
            hid[target, :] = (act * up).astype(BF)
            gg[target, :] = (dh * up * (cdf + xpdf)).astype(BF)
            ug[target, :] = (dh * act).astype(BF)

    def sums(n, i):
        hid, gg, ug = streams[n][3:]
        rows, source = place(n, i), place(0, i)
        out_ref[rows, :] += mm(hid[source, :], wo_ref[...])
        back_ref[rows, :] += mm_t(gg[source, :], wg_ref[...]) + mm_t(ug[source, :], wu_ref[...])

    products(0, 0)
    products(1, 0)
    elementwise(0, 0)

    def body(i):
        products(0, i + 1)
        sums(0, i)
        elementwise(1, i)
        products(1, i + 1)
        sums(1, i)
        elementwise(0, i + 1)

    loop(steps - 1, body)
    last = steps - 1
    sums(0, last)
    elementwise(1, last)
    sums(1, last)
    (hid0, gg0, ug0), (hid1, gg1, ug1) = streams[0][3:], streams[1][3:]
    for k, (ref, first, second) in enumerate(((sat_ref, gg0, gg1), (sat_ref, ug0, ug1), (ogt_ref, hid0, hid1))):
        grads_ref[k] = (mm(ref[:, 0:half], first[...]) + mm(ref[:, half:tokens], second[...])).astype(BF)

    @pl.when(j == pl.num_programs(0) - 1)
    def _():
        def leave(i):
            rows = rows_of(i, 64)
            out_low_ref[rows, :] = out_ref[rows, :].astype(BF)
            back_low_ref[rows, :] = back_ref[rows, :].astype(BF)

        loop(tokens // 64, leave)


def ffn_both(second_act, out_grad, second_turned, grad_turned, ffn_in, ffn_out, share, width=512, tile=512):
    tokens, model = second_act.shape
    total_blocks = ffn_out.shape[0] // width
    first, last = (total_blocks * n // 3 for n in share)
    blocks = last - first
    hidden = blocks * width
    shape = jax.ShapeDtypeStruct
    whole = once((tokens, model), lambda j: (0, 0))
    turned = once((model, tokens), lambda j: (0, 0))
    return pl.pallas_call(
        ffn_kernel,
        out_shape=[shape((tokens, model), BF), shape((tokens, model), BF), shape((3, model, hidden), BF)],
        grid=(blocks,),
        in_specs=[
            whole, whole, turned, turned,
            pl.BlockSpec((model, width), lambda j: (0, j + first)),
            pl.BlockSpec((model, width), lambda j: (0, j + first + total_blocks)),
            pl.BlockSpec((width, model), lambda j: (j + first, 0)),
        ],
        out_specs=[whole, whole, pl.BlockSpec((3, model, width), lambda j: (0, 0, j))],
        scratch_shapes=[pltpu.VMEM((tokens, model), F32)] * 2 + ([pltpu.VMEM((tile, width), F32)] * 3 + [pltpu.VMEM((tokens // 2, width), BF)] * 3) * 2,
        compiler_params=pltpu.CompilerParams(dimension_semantics=("arbitrary",), vmem_limit_bytes=LIMIT),
        cost_estimate=pl.CostEstimate(flops=18 * tokens * model * hidden, bytes_accessed=tokens * model * 24 + model * hidden * 12, transcendentals=tokens * hidden),
        name="ffn_both",
    )(second_act, out_grad, second_turned, grad_turned, ffn_in, ffn_in, ffn_out)


def norm_back_kernel(pieces, resid_ref, *refs):
    sum_refs, back_refs = refs[:pieces], refs[pieces : 2 * pieces]
    og_ref, gain_ref, out_ref, grad_ref, low_ref, gain_grad_ref = refs[2 * pieces :]

    @pl.when(pl.program_id(0) == 0)
    def _():
        gain_grad_ref[...] = jnp.zeros_like(gain_grad_ref)

    tile = 64

    def body(i):
        rows = rows_of(i, tile)
        resid = resid_ref[rows, :]
        n, scale = norm_stats(resid)
        u = sum(ref[rows, :].astype(F32) for ref in back_refs)
        ug = u * gain_ref[...]
        un = u * n
        part = ug - jnp.mean(ug, axis=-1, keepdims=True) - n * jnp.mean(ug * n, axis=-1, keepdims=True)
        grad = og_ref[rows, :].astype(F32) + scale * part
        out_ref[rows, :] = (resid + sum(ref[rows, :].astype(F32) for ref in sum_refs)).astype(BF)
        grad_ref[rows, :] = grad
        low_ref[rows, :] = grad.astype(BF)
        gain_grad_ref[...] += jnp.sum(un.reshape(tile // 8, 8, un.shape[1]), axis=0)

    loop(resid_ref.shape[0] // tile, body)


def norm_back(resid, totals, backs, out_grad, gain, tile=512):
    tokens, model = resid.shape
    pieces = len(totals)
    shape = jax.ShapeDtypeStruct
    block = pl.BlockSpec((tile, model), lambda i: (i, 0))
    fixed = pl.BlockSpec((8, model), lambda i: (0, 0))
    return pl.pallas_call(
        functools.partial(norm_back_kernel, pieces),
        out_shape=[shape((tokens, model), BF), shape((tokens, model), F32), shape((tokens, model), BF), shape((8, model), F32)],
        grid=(tokens // tile,),
        in_specs=[block] * (2 * pieces + 2) + [pl.BlockSpec((1, model), lambda i: (0, 0))],
        out_specs=[block, block, block, fixed],
        compiler_params=pltpu.CompilerParams(dimension_semantics=("arbitrary",), vmem_limit_bytes=LIMIT),
        cost_estimate=pl.CostEstimate(flops=20 * tokens * model, bytes_accessed=tokens * model * 22, transcendentals=tokens),
        name="norm_back",
    )(resid, *totals, *backs, out_grad, gain)


def eight_sum(v):
    return jnp.sum(v.reshape(v.shape[0] // 8, 8, v.shape[1]), axis=0)


def mixer_backward_kernel(
    split_ref, keep_ref, low_ref, q_ref, k_ref, v_ref, mixed_ref, wo_ref,
    fq_ref, fv_ref, fk_ref, slope_ref, shift_ref, skip_ref, fwd_real_ref, fwd_ref, inv_real_ref, inv_ref,
    p_ref, chan_ref,
    qs, ks, vs, xv, xc, xy, y_s, spec_s, u_s, o_s,
):
    r = pl.program_id(1)
    length, width = q_ref.shape
    quarter = length // 4
    split, keep = split_ref[r], keep_ref[r]
    tile = 128

    @pl.when(r == 0)
    def _():
        chan_ref[...] = jnp.zeros_like(chan_ref)

    for ref, source in ((qs, q_ref), (ks, k_ref), (vs, v_ref)):
        ref[0:8, :] = jnp.zeros((8, width), F32)

        def widen(i, ref=ref, source=source):
            ref[pl.ds(pl.multiple_of(8 + i * tile, 8), tile), :] = source[rows_of(i, tile), :].astype(F32)

        loop(length // tile, widen)

    o_s[0:length, 0:width] = mm_t(low_ref[...], wo_ref[...])

    def conv(i):
        t = i * tile
        rows = rows_of(i, tile)
        kept = t + lax.broadcasted_iota(jnp.int32, (tile, width), 0) < keep
        gated_grad = o_s[rows, 0:width]
        low = (gated_grad * conv_back(qs, t, tile, fq_ref, split)).astype(BF)
        xy[rows, :] = low
        value = jnp.where(kept, conv_back(vs, t, tile, fv_ref, split), 0.0).astype(BF)
        xv[rows, :] = value
        xc[rows, :] = jnp.where(kept, conv_back(ks, t, tile, fk_ref, split), 0.0).astype(BF)
        chan_ref[2, :, :] += eight_sum(low.astype(F32) * value.astype(F32))

    loop(length // tile, conv)
    butterfly(xv, y_s, 0, width, quarter)
    butterfly(xc, y_s, width, width, quarter)
    butterfly(xy, y_s, 2 * width, width, quarter)

    def query(i):
        rows = rows_of(i, tile)
        qs[rows, :] = o_s[rows, 0:width] * mixed_ref[rows, :].astype(F32)

    loop(length // tile, query)
    blockwise(y_s, spec_s, fwd_real_ref, fwd_ref, quarter)

    def bins(re, im, first):
        n = 64
        re, im = pl.ds(pl.multiple_of(re, n), n), pl.ds(pl.multiple_of(im, n), n)
        vr, vi = spec_s[re, 0:width], spec_s[im, 0:width]
        cr, ci = spec_s[re, width : 2 * width], spec_s[im, width : 2 * width]
        yr, yi = spec_s[re, 2 * width : 3 * width], spec_s[im, 2 * width : 3 * width]
        slope, shift = slope_ref[...], shift_ref[...]
        rr, ii = cr * cr, ci * ci
        if first:
            edge = lax.broadcasted_iota(jnp.int32, (n, width), 0) == 0
            pr, pi = jnp.where(edge, rr, rr + ii), jnp.where(edge, ii, rr + ii)
            gr, gi = jax.nn.sigmoid(slope * pr + shift), jax.nn.sigmoid(slope * pi + shift)
            ar = vr * yr + jnp.where(edge, 0.0, vi * yi)
            ai = jnp.where(edge, -vi * yi, vi * yr - vr * yi)
            br = ar * cr - jnp.where(edge, 0.0, ai * ci)
            bi = jnp.where(edge, -ai * ci, br)
            wr, wi = br * gr * (1.0 - gr), bi * gi * (1.0 - gi)
            ws = jnp.where(edge, 0.5 * (wr + wi), wr)
            wp = jnp.where(edge, 0.5 * (wr * pr + wi * pi), wr * pr)
            hr, hi = gr * cr, gi * ci
            er = hr * yr + jnp.where(edge, 0.0, hi * yi)
            ei = jnp.where(edge, hi * yi, hr * yi - hi * yr)
            dr = gr * ar + 2.0 * slope * wr * cr
            di = 2.0 * slope * wi * ci - gi * ai
        else:
            p = rr + ii
            g = jax.nn.sigmoid(slope * p + shift)
            ar, ai = vr * yr + vi * yi, vi * yr - vr * yi
            ws = (ar * cr - ai * ci) * (g * (1.0 - g))
            wp = ws * p
            hr, hi = g * cr, g * ci
            er, ei = hr * yr + hi * yi, hr * yi - hi * yr
            k = 2.0 * slope * ws
            dr, di = g * ar + k * cr, k * ci - g * ai
        chan_ref[0, :, :] += eight_sum(wp)
        chan_ref[1, :, :] += eight_sum(ws)
        u_s[re, 0:width] = er.astype(BF)
        u_s[im, 0:width] = ei.astype(BF)
        u_s[re, width : 2 * width] = dr.astype(BF)
        u_s[im, width : 2 * width] = di.astype(BF)

    each_bin(quarter, bins)
    resynth(u_s, o_s, inv_real_ref, inv_ref, quarter)

    def finish(i):
        n = 32
        value = recombine(o_s, slice(0, width), i, n, quarter)
        cond = recombine(o_s, slice(width, 2 * width), i, n, quarter)
        for k in range(4):
            rows = pl.ds(pl.multiple_of(k * quarter + i * n, n), n)
            kept = k * quarter + i * n + lax.broadcasted_iota(jnp.int32, (n, width), 0) < keep
            grad = (value[k] + skip_ref[...] * xy[rows, :].astype(F32)).astype(BF).astype(F32)
            vs[rows, :] = jnp.where(kept, grad, 0.0)
            ks[rows, :] = jnp.where(kept, cond[k].astype(BF).astype(F32), 0.0)

    loop(quarter // 32, finish)
    for ref in (qs, ks, vs):
        ref[length : length + 8, :] = jnp.zeros((8, width), F32)

    for slot, (ref, source, f_ref) in enumerate(((qs, q_ref, fq_ref), (vs, v_ref, fv_ref), (ks, k_ref, fk_ref))):

        def adjoint(i, slot=slot, ref=ref, source=source, f_ref=f_ref):
            t = i * tile
            rows = rows_of(i, tile)
            block = ref[pl.ds(pl.multiple_of(t, tile), tile + 8), :]
            position = t + lax.broadcasted_iota(jnp.int32, (tile, width), 0)
            g0 = block[0:tile]
            g1 = jnp.where(position + 1 != split, block[1 : tile + 1], 0.0)
            g2 = jnp.where((position + 2 != split) & (position + 1 != split), block[2 : tile + 2], 0.0)
            s = source[rows, :].astype(F32)
            place = slice((0, 2, 1)[slot] * width, ((0, 2, 1)[slot] + 1) * width)
            p_ref[rows, place] = (f_ref[0:1, :] * g0 + f_ref[1:2, :] * g1 + f_ref[2:3, :] * g2).astype(BF)
            for k, g in enumerate((g0, g1, g2)):
                chan_ref[3 + 3 * slot + k, :, :] += eight_sum(g * s)

        loop(length // tile, adjoint)


def mixer_backward(branch_low, split, keep, q, k, v, mixed, proj_out, short_filter, cond_filter, slope, shift, skip, tables, width=256):
    rows, length, model = q.shape
    blocks = model // width
    shape = jax.ShapeDtypeStruct
    pad = pltpu.VMEM((length + 8, width), F32)
    quarter = length // 4
    row = pl.BlockSpec((None, length, model), lambda j, r, *_: (r, 0, 0))
    part = pl.BlockSpec((None, length, width), lambda j, r, *_: (r, 0, j))

    def columns(size, offset):
        return pl.BlockSpec((size, width), lambda j, r, *_: (0, j + offset * blocks))

    fixed = lambda j, r, *_: (0, 0)
    table_specs = [once((2 * quarter, quarter), fixed), once((6 * quarter, 2 * quarter), fixed)] * 2
    one = columns(1, 0)
    flops = rows * (2 * length * model * model + 2 * 5 * model * (2 * length) * length // 2)
    return pl.pallas_call(
        mixer_backward_kernel,
        out_shape=[shape((rows, length, 3 * model), BF), shape((12, 8, model), F32)],
        grid_spec=pltpu.PrefetchScalarGridSpec(
            num_scalar_prefetch=2,
            grid=(blocks, rows),
            in_specs=[row, part, part, part, part, pl.BlockSpec((width, model), lambda j, r, *_: (j, 0)), columns(3, 0), columns(3, 1), columns(3, 0), one, one, one] + table_specs,
            out_specs=[pl.BlockSpec((None, length, 3 * width), lambda j, r, *_: (r, 0, j)), pl.BlockSpec((12, 8, width), lambda j, r, *_: (0, 0, j))],
            scratch_shapes=[pad, pad, pad] + [pltpu.VMEM((length, width), BF)] * 3 + [
                pltpu.VMEM((2 * length, 3 * width), BF),
                pltpu.VMEM((2 * length, 3 * width), F32),
                pltpu.VMEM((2 * length, 2 * width), BF),
                pltpu.VMEM((2 * length, 2 * width), F32),
            ],
        ),
        compiler_params=pltpu.CompilerParams(dimension_semantics=("arbitrary", "arbitrary"), vmem_limit_bytes=LIMIT),
        cost_estimate=pl.CostEstimate(flops=flops, bytes_accessed=rows * length * (model * 2 * blocks + model * 14), transcendentals=rows * length * model),
        name="mixer_backward",
    )(split, keep, branch_low, q, k, v, mixed, proj_out, short_filter, short_filter, cond_filter, slope, shift, skip, *tables)


def input_back_kernel(width, x_ref, grad_ref, gain_ref, w_ref, p_ref, in_grad_ref, gain_grad_ref, acc):
    model = x_ref.shape[1]
    tile = 64

    @pl.when(pl.program_id(0) == 0)
    def _():
        gain_grad_ref[...] = jnp.zeros_like(gain_grad_ref)

    total = None
    for b in range(model // width):
        for k in range(3):
            place = (3 * b + k) * width
            term = mm_t(p_ref[:, place : place + width], w_ref[:, k * model + b * width : k * model + (b + 1) * width])
            total = term if total is None else total + term
    acc[...] = total

    def body(i):
        rows = rows_of(i, tile)
        n, scale = norm_stats(x_ref[rows, :].astype(F32))
        u = acc[rows, :]
        ug = u * gain_ref[...]
        part = ug - jnp.mean(ug, axis=-1, keepdims=True) - n * jnp.mean(ug * n, axis=-1, keepdims=True)
        in_grad_ref[rows, :] = (grad_ref[rows, :] + scale * part).astype(in_grad_ref.dtype)
        gain_grad_ref[...] += eight_sum(u * n)

    loop(x_ref.shape[0] // tile, body)


def input_back(x, resid_grad, gain, proj_in, proj_grad, width, tile=512):
    tokens, model = x.shape
    shape = jax.ShapeDtypeStruct
    block = pl.BlockSpec((tile, model), lambda i: (i, 0))
    return pl.pallas_call(
        functools.partial(input_back_kernel, width),
        out_shape=[shape((tokens, model), BF), shape((8, model), F32)],
        grid=(tokens // tile,),
        in_specs=[block, block, once((1, model), lambda i: (0, 0)), once((model, 3 * model), lambda i: (0, 0)), pl.BlockSpec((tile, 3 * model), lambda i: (i, 0))],
        out_specs=[block, pl.BlockSpec((8, model), lambda i: (0, 0))],
        scratch_shapes=[pltpu.VMEM((tile, model), F32)],
        compiler_params=pltpu.CompilerParams(dimension_semantics=("arbitrary",), vmem_limit_bytes=LIMIT),
        cost_estimate=pl.CostEstimate(flops=6 * tokens * model * model, bytes_accessed=tokens * model * 14, transcendentals=tokens),
        name="input_back",
    )(x, resid_grad, gain, proj_in, proj_grad)


def turn(a, b):
    return lax.dot_general(a, b, (((0,), (0,)), ((), ())), preferred_element_type=F32).astype(BF)


def after(value, earlier):
    return lax.optimization_barrier((value, earlier))[0]


def exchange_sum_kernel(rows, seq, x_ref, send_ref, out_ref, other_ref, slots, total, send_sem, recv_sem, far_send_sem, far_recv_sem):
    r, s = lax.axis_index("rows"), lax.axis_index("seq")
    partners = []
    bit = 1
    while bit < rows:
        partners.append((r + bit - 2 * bit * (lax.rem(r // bit, 2)), s))
        bit *= 2
    bit = 1
    while bit < seq:
        partners.append((r, s + bit - 2 * bit * (lax.rem(s // bit, 2))))
        bit *= 2
    barrier = pltpu.get_barrier_semaphore()
    for partner in partners:
        pl.semaphore_signal(barrier, inc=1, device_id=partner, device_id_type=pl.DeviceIdType.MESH)
    pl.semaphore_wait(barrier, len(partners))
    part = other_ref.shape[1]
    far = pltpu.make_async_remote_copy(
        src_ref=send_ref.at[:, pl.ds(pl.multiple_of((1 - s) * part, part), part)], dst_ref=other_ref,
        send_sem=far_send_sem, recv_sem=far_recv_sem, device_id=(r, 1 - s), device_id_type=pl.DeviceIdType.MESH,
    )
    far.start()
    total[0] = x_ref[...]
    for step, partner in enumerate(partners):
        copy = pltpu.make_async_remote_copy(
            src_ref=total.at[step], dst_ref=slots.at[step], send_sem=send_sem.at[step], recv_sem=recv_sem.at[step],
            device_id=partner, device_id_type=pl.DeviceIdType.MESH,
        )
        copy.start()
        copy.wait()
        total[step + 1] = total[step] + slots[step]
    out_ref[...] = total[len(partners)]
    far.wait()


def power_of_two(n):
    return n & (n - 1) == 0


def exchange_sum(value, whole_rows):
    rows, seq = lax.axis_size("rows"), lax.axis_size("seq")
    if not (power_of_two(rows) and seq == 2):
        return lax.psum(value, ("rows", "seq")), scatter_rows(whole_rows).astype(F32)
    steps = rows.bit_length()
    own, length, model = whole_rows.shape
    part = length // 2
    shape = jax.ShapeDtypeStruct
    total, other = pl.pallas_call(
        functools.partial(exchange_sum_kernel, rows, seq),
        out_shape=[shape(value.shape, value.dtype), shape((own, part, model), whole_rows.dtype)],
        in_specs=[pl.BlockSpec(memory_space=pltpu.VMEM), pl.BlockSpec(memory_space=pl.ANY)],
        out_specs=[pl.BlockSpec(memory_space=pltpu.VMEM), pl.BlockSpec(memory_space=pl.ANY)],
        scratch_shapes=[
            pltpu.VMEM((steps, *value.shape), value.dtype),
            pltpu.VMEM((steps + 1, *value.shape), value.dtype),
            pltpu.SemaphoreType.DMA((steps,)),
            pltpu.SemaphoreType.DMA((steps,)),
            pltpu.SemaphoreType.DMA,
            pltpu.SemaphoreType.DMA,
        ],
        compiler_params=pltpu.CompilerParams(collective_id=7, has_side_effects=True),
        cost_estimate=pl.CostEstimate(flops=20_000_000_000, bytes_accessed=0, transcendentals=0),
        name="exchange_sum",
    )(value, whole_rows)
    return total, assemble(whole_rows, other)


def assemble_kernel(own, s_ref, mine_ref, other_ref, out_ref):
    out_ref[...] = jnp.where(pl.program_id(0) // own == s_ref[0], mine_ref[...], other_ref[...]).astype(F32)


def assemble(whole_rows, other):
    own, part, model = other.shape
    block = (None, part, model)
    return pl.pallas_call(
        functools.partial(assemble_kernel, own),
        out_shape=jax.ShapeDtypeStruct((2 * own, part, model), F32),
        grid_spec=pltpu.PrefetchScalarGridSpec(
            num_scalar_prefetch=1,
            grid=(2 * own,),
            in_specs=[pl.BlockSpec(block, lambda i, s: (i % own, s[0], 0)), pl.BlockSpec(block, lambda i, s: (i % own, 0, 0))],
            out_specs=pl.BlockSpec(block, lambda i, s: (i, 0, 0)),
        ),
        compiler_params=pltpu.CompilerParams(dimension_semantics=("arbitrary",), vmem_limit_bytes=LIMIT),
        name="assemble",
    )(lax.axis_index("seq").astype(jnp.int32)[None], whole_rows, other)


def swapped(value):
    count = lax.axis_size("seq")
    return lax.ppermute(value, "seq", [(i, (i + 1) % count) for i in range(count)])


def gather_rows(value, first=0, count=None):
    own = value.shape[0] // lax.axis_size("seq")
    count = own if count is None else count
    if lax.axis_size("seq") != 2:
        whole = lax.all_to_all(value, "seq", split_axis=0, concat_axis=1, tiled=True)
        return whole[first : first + count]
    s = lax.axis_index("seq")
    mine = lax.dynamic_slice_in_dim(value, s * own + first, count)
    other = swapped(lax.dynamic_slice_in_dim(value, (1 - s) * own + first, count))
    return jnp.concatenate([jnp.where(s == 0, mine, other), jnp.where(s == 0, other, mine)], axis=1)


def scatter_rows(value):
    if lax.axis_size("seq") != 2:
        return lax.all_to_all(value, "seq", split_axis=1, concat_axis=0, tiled=True)
    s = lax.axis_index("seq")
    part = value.shape[1] // 2
    mine = lax.dynamic_slice_in_dim(value, s * part, part, axis=1)
    other = swapped(lax.dynamic_slice_in_dim(value, (1 - s) * part, part, axis=1))
    return jnp.concatenate([jnp.where(s == 0, mine, other), jnp.where(s == 0, other, mine)], axis=0)


def seq_sum(value):
    if lax.axis_size("seq") != 2:
        return lax.psum(value, "seq").astype(F32)
    return value.astype(F32) + swapped(value).astype(F32)


def per_device_rows(inputs, split_point, keep_mask, norm_gain, proj_in, short_filter, cond_filter, spec_slope, spec_shift, skip_gain, proj_out, ffn_gain, ffn_in, ffn_out, out_grad):
    local_rows, local_len, model = inputs.shape
    count = lax.axis_size("seq")
    own = local_rows // count
    length = local_len * count
    tokens = own * length
    width = 256
    first_row = lax.axis_index("seq") * own
    flat = lambda a: a.reshape(tokens, model)
    flat_wide = lambda a: a.reshape(tokens, 3 * model)
    shaped = lambda a: a.reshape(own, length, model)
    lift = lambda a: a.reshape(1, -1)

    pieces = [(0, 1), (1, own - 1)] if own > 1 else [(0, own)]
    xs = []
    for start, size in pieces:
        xs.append(gather_rows(after(inputs, xs) if xs else inputs, start, size))
    kept = jnp.sum(keep_mask, axis=1)
    kept = kept + swapped(kept) if count == 2 else lax.psum(kept, "seq")
    keep = lax.dynamic_slice_in_dim(kept, first_row, own)
    split = lax.dynamic_slice_in_dim(split_point, first_row, own)
    tables = spectral_tables(length, lax.axis_index("seq") * (2 * length))
    slope, shift, skip = lift(spec_slope), lift(spec_shift), lift(skip_gain)

    held = ()
    for x, (start, size) in zip(xs, pieces):
        held = mixer_forward(
            x, split, keep, lift(norm_gain), proj_in, short_filter, cond_filter, slope, shift, skip, proj_out, lift(ffn_gain), tables, start, own, held
        )
        if start == 0:
            whole_grad = flat(gather_rows(after(out_grad, (xs[-1], held[-1]))))
    first, q, k, v, mixed, gated, resid, second = held
    x = jnp.concatenate(xs, axis=0)
    second = flat(second)
    second_turned, grad_turned = second.T, whole_grad.T
    totals, backs, grads = [], [], []
    for share in ((0, 1), (1, 3)):
        total, back, grad = ffn_both(second, whole_grad, second_turned, grad_turned, ffn_in, ffn_out, share)
        totals.append(total)
        backs.append(back)
        grads.append(grad)
    early_share = lax.psum_scatter(grads[0], "rows", scatter_dimension=1, tiled=True)
    output, resid_grad, branch_low, ffn_gain_part = norm_back(flat(resid), totals, backs, whole_grad, lift(ffn_gain))
    output = scatter_rows(shaped(output))
    out_part = turn(flat(gated), branch_low)
    grad, branch_low, early_share = lax.optimization_barrier((grads[1], branch_low, early_share))
    late_share = lax.psum_scatter(grad, "rows", scatter_dimension=1, tiled=True)
    proj_grad, chan = mixer_backward(shaped(branch_low), split, keep, q, k, v, mixed, proj_out, short_filter, cond_filter, slope, shift, skip, tables)
    proj_grad = flat_wide(proj_grad)
    mix_part = jnp.concatenate([out_part, turn(flat(first), proj_grad)], axis=1)
    mix_part, late_share = lax.optimization_barrier((mix_part, late_share))
    mix_share = lax.psum_scatter(mix_part, "rows", scatter_dimension=0, tiled=True)
    proj_grad = after(proj_grad, mix_part)
    input_grad, norm_gain_part = input_back(flat(x), resid_grad, lift(norm_gain), proj_in, proj_grad, width)
    ffn_shares = [seq_sum(early_share), seq_sum(late_share)]
    small = jnp.sum(jnp.concatenate([ffn_gain_part[None], norm_gain_part[None], chan], 0), axis=1)
    small, input_grad = exchange_sum(small, shaped(input_grad))
    scale = 1.0 / length
    mix_share = seq_sum(mix_share)
    in_share = mix_share[:, model:].reshape(-1, model // width, 3, width).transpose(0, 2, 1, 3)
    return (
        output,
        input_grad,
        small[1],
        in_share.reshape(-1, 3 * model),
        jnp.concatenate([small[5:8], small[8:11]], axis=1),
        small[11:14],
        small[2] * scale,
        small[3] * scale,
        small[4],
        mix_share[:, :model],
        small[0],
        jnp.concatenate([share[k] for k in range(2) for share in ffn_shares], axis=1),
        jnp.concatenate([share[2] for share in ffn_shares], axis=1).T,
    )


PRECISE = lax.Precision.HIGH


def passed_along(value, axis, steps):
    count = lax.axis_size(axis)
    leading, last = (max(0, -steps), min(count, count - steps))
    return lax.ppermute(value, axis, [(source, source + steps) for source in range(leading, last)])


def layer_norm(values, scaling):
    center = values - jnp.mean(values, axis=-1, keepdims=True)
    spread = jnp.mean(center * center, axis=-1, keepdims=True)
    return center * lax.rsqrt(spread + EPSILON) * scaling


def conv_three(extended, weights, same_one, same_two):
    length = extended.shape[1] - 2
    return (
        weights[0] * extended[:, 2:]
        + weights[1] * extended[:, 1 : length + 1] * same_one
        + weights[2] * extended[:, :length] * same_two
    )


def dft_tables(seq_length):
    table_shape = (seq_length + 1, seq_length)
    product = lax.broadcasted_iota(jnp.int32, table_shape, 0) * lax.broadcasted_iota(
        jnp.int32, table_shape, 1
    )
    angles = (product % (2 * seq_length)).astype(jnp.float32) * (math.pi / seq_length)
    freq = lax.broadcasted_iota(jnp.int32, (seq_length + 1, 1), 0)
    edge = jnp.logical_or(freq == 0, freq == seq_length)
    weights = jnp.where(edge, 1.0, 2.0).astype(jnp.float32) / (2.0 * seq_length)
    return (jnp.cos(angles), jnp.sin(angles), weights)


def analyze(values, conds, cos_table, sin_table):
    value_real = jnp.einsum("ft,ktd->kfd", cos_table, values, precision=PRECISE)
    value_imag = -jnp.einsum("ft,ktd->kfd", sin_table, values, precision=PRECISE)
    cond_real = jnp.einsum("ft,ktd->kfd", cos_table, conds, precision=PRECISE)
    cond_imag = -jnp.einsum("ft,ktd->kfd", sin_table, conds, precision=PRECISE)
    return (value_real, value_imag, cond_real, cond_imag)


def synth(
    value_real,
    value_imag,
    cond_real,
    cond_imag,
    values,
    slopes,
    shifts,
    skip_gains,
    cos_table,
    sin_table,
    freq_weights,
):
    factor = jax.nn.sigmoid(slopes * (cond_real * cond_real + cond_imag * cond_imag) + shifts)
    filter_real = cond_real * factor
    filter_imag = cond_imag * factor
    prod_real = (value_real * filter_real - value_imag * filter_imag) * freq_weights
    prod_imag = (value_real * filter_imag + value_imag * filter_real) * freq_weights
    mixed_out = jnp.einsum("ft,kfd->ktd", cos_table, prod_real, precision=PRECISE) - jnp.einsum(
        "ft,kfd->ktd", sin_table, prod_imag, precision=PRECISE
    )
    return mixed_out + skip_gains * values


def times_transpose(left, right):
    return lax.dot_general(
        left, right, (((1,), (1,)), ((), ())), preferred_element_type=jnp.float32
    )


def transpose_times(left, right):
    return lax.dot_general(
        left, right, (((0,), (0,)), ((), ())), preferred_element_type=jnp.float32
    )


def per_device(
    inputs,
    split_point,
    keep_mask,
    norm_gain,
    proj_in,
    short_filter,
    cond_filter,
    spec_slope,
    spec_shift,
    skip_gain,
    proj_out,
    ffn_gain,
    ffn_in,
    ffn_out,
    out_grad,
):
    local_rows, local_len, model_width = inputs.shape
    hidden_width = ffn_out.shape[0]
    seq_count = lax.axis_size("seq")
    seq_index = lax.axis_index("seq")
    full_len = local_len * seq_count
    chan_width = model_width // seq_count
    token_count = local_rows * local_len
    positions = seq_index * local_len + lax.broadcasted_iota(jnp.int32, (local_rows, local_len), 1)
    splits = split_point[:, None]
    segment = positions >= splits
    same_one = (segment == (positions - 1 >= splits)).astype(jnp.float32)[:, :, None]
    same_two = (segment == (positions - 2 >= splits)).astype(jnp.float32)[:, :, None]
    keep_float = keep_mask.astype(jnp.float32)[:, :, None]
    flat_in = inputs.reshape(token_count, model_width).astype(jnp.float32)
    normed_one, norm_one_back = jax.vjp(layer_norm, flat_in, norm_gain)
    first_act = normed_one.astype(jnp.bfloat16)
    projected = jnp.dot(first_act, proj_in, preferred_element_type=jnp.float32).astype(jnp.bfloat16)
    proj_rows = projected.reshape(local_rows, local_len, 3 * model_width)
    edge_values = passed_along(proj_rows[:, local_len - 2 :, :], "seq", 1)
    extended = jnp.concatenate([edge_values, proj_rows], axis=1).astype(jnp.float32)

    def mixer_local(ext_values, short_weights, cond_weights):
        query_value = jnp.concatenate(
            [ext_values[:, :, :model_width], ext_values[:, :, 2 * model_width :]], axis=2
        )
        conv_both = conv_three(query_value, short_weights, same_one, same_two)
        cond_conv = conv_three(
            ext_values[:, :, model_width : 2 * model_width], cond_weights, same_one, same_two
        )
        return (
            conv_both[:, :, :model_width],
            conv_both[:, :, model_width:] * keep_float,
            cond_conv * keep_float,
        )

    (query_conv, value_masked, cond_masked), mixer_back = jax.vjp(
        mixer_local, extended, short_filter, cond_filter
    )
    value_low = value_masked.astype(jnp.bfloat16)
    cond_low = cond_masked.astype(jnp.bfloat16)
    slope_part = lax.dynamic_slice_in_dim(spec_slope, seq_index * chan_width, chan_width)
    shift_part = lax.dynamic_slice_in_dim(spec_shift, seq_index * chan_width, chan_width)
    skip_part = lax.dynamic_slice_in_dim(skip_gain, seq_index * chan_width, chan_width)
    cos_table, sin_table, freq_weights = dft_tables(full_len)

    def synth_local(
        value_real, value_imag, cond_real, cond_imag, values, slopes, shifts, skip_gains
    ):
        return synth(
            value_real,
            value_imag,
            cond_real,
            cond_imag,
            values,
            slopes,
            shifts,
            skip_gains,
            cos_table,
            sin_table,
            freq_weights,
        )

    value_chan = lax.all_to_all(value_low, "seq", split_axis=2, concat_axis=1, tiled=True)
    cond_chan = lax.all_to_all(cond_low, "seq", split_axis=2, concat_axis=1, tiled=True)
    value_float = value_chan.astype(jnp.float32)
    spectra = analyze(value_float, cond_chan.astype(jnp.float32), cos_table, sin_table)
    mixed_chan = synth_local(
        spectra[0],
        spectra[1],
        spectra[2],
        spectra[3],
        value_float,
        slope_part,
        shift_part,
        skip_part,
    ).astype(jnp.bfloat16)
    mixed_home = lax.all_to_all(mixed_chan, "seq", split_axis=1, concat_axis=2, tiled=True)
    mixed_float = mixed_home.astype(jnp.float32)
    gated = (query_conv * mixed_float).astype(jnp.bfloat16).reshape(token_count, model_width)
    branch = jnp.dot(gated, proj_out, preferred_element_type=jnp.float32)
    resid = flat_in + branch
    normed_two, norm_two_back = jax.vjp(layer_norm, resid, ffn_gain)
    second_act = normed_two.astype(jnp.bfloat16)
    gate_up = jnp.dot(second_act, ffn_in, preferred_element_type=jnp.float32)

    def glu_local(both_parts):
        return (
            jax.nn.gelu(both_parts[:, :hidden_width], approximate=False)
            * both_parts[:, hidden_width:]
        )

    hidden, glu_back = jax.vjp(glu_local, gate_up)
    hidden_low = hidden.astype(jnp.bfloat16)
    result = resid + jnp.dot(hidden_low, ffn_out, preferred_element_type=jnp.float32)
    output = result.astype(jnp.bfloat16).reshape(local_rows, local_len, model_width)
    flat_grad = out_grad.reshape(token_count, model_width)
    hidden_grad = times_transpose(flat_grad, ffn_out)
    (gate_up_grad,) = glu_back(hidden_grad)
    gate_up_low = gate_up_grad.astype(jnp.bfloat16)
    second_grad = times_transpose(gate_up_low, ffn_in)
    resid_part, ffn_gain_part = norm_two_back(second_grad)
    resid_grad = flat_grad.astype(jnp.float32) + resid_part
    branch_low = resid_grad.astype(jnp.bfloat16)
    gated_grad = times_transpose(branch_low, proj_out).reshape(local_rows, local_len, model_width)
    query_grad = gated_grad * mixed_float
    mixed_grad = (gated_grad * query_conv).astype(jnp.bfloat16)
    grad_chan = lax.all_to_all(mixed_grad, "seq", split_axis=2, concat_axis=1, tiled=True)
    grad_float = grad_chan.astype(jnp.float32)
    item_count = grad_chan.shape[0]
    slope_items = jnp.broadcast_to(slope_part, (item_count, 1, chan_width))
    shift_items = jnp.broadcast_to(shift_part, (item_count, 1, chan_width))
    skip_items = jnp.broadcast_to(skip_part, (item_count, 1, chan_width))
    value_float = value_chan.astype(jnp.float32)

    def spectral(values, conds, slopes, shifts, skip_gains):
        spectra = analyze(values, conds, cos_table, sin_table)
        return synth_local(
            spectra[0], spectra[1], spectra[2], spectra[3], values, slopes, shifts, skip_gains
        )

    unused, pull = jax.vjp(
        spectral, value_float, cond_chan.astype(jnp.float32), slope_items, shift_items, skip_items
    )
    value_back, cond_back, slope_rows, shift_rows, skip_rows = pull(grad_float)
    value_grad, cond_grad = (
        lax.all_to_all(
            value_back.astype(jnp.bfloat16), "seq", split_axis=1, concat_axis=2, tiled=True
        ),
        lax.all_to_all(
            cond_back.astype(jnp.bfloat16), "seq", split_axis=1, concat_axis=2, tiled=True
        ),
    )
    start_chan = (seq_index * chan_width,)
    empty_width = jnp.zeros((model_width,), jnp.float32)
    slope_full = lax.dynamic_update_slice(empty_width, jnp.sum(slope_rows, axis=(0, 1)), start_chan)
    shift_full = lax.dynamic_update_slice(empty_width, jnp.sum(shift_rows, axis=(0, 1)), start_chan)
    skip_full = lax.dynamic_update_slice(empty_width, jnp.sum(skip_rows, axis=(0, 1)), start_chan)
    ext_grad, short_grad, cond_weight_grad = mixer_back(
        (query_grad, value_grad.astype(jnp.float32), cond_grad.astype(jnp.float32))
    )
    incoming = passed_along(ext_grad[:, :2, :].astype(jnp.bfloat16), "seq", -1).astype(jnp.float32)
    proj_grad = ext_grad[:, 2:, :] + jnp.pad(incoming, ((0, 0), (local_len - 2, 0), (0, 0)))
    proj_low = proj_grad.astype(jnp.bfloat16).reshape(token_count, 3 * model_width)
    first_grad = times_transpose(proj_low, proj_in)
    input_part, norm_gain_part = norm_one_back(first_grad)
    input_grad = (resid_grad + input_part).reshape(local_rows, local_len, model_width)
    share = lax.psum_scatter(
        jnp.concatenate(
            [
                transpose_times(first_act, proj_low),
                transpose_times(gated, branch_low),
                transpose_times(second_act, gate_up_low),
                transpose_times(flat_grad, hidden_low),
            ],
            axis=1,
        ).astype(jnp.bfloat16),
        "rows",
        scatter_dimension=0,
        tiled=True,
    )
    summed = lax.psum(share, "seq").astype(jnp.float32)
    small_sums = lax.psum(
        (
            norm_gain_part,
            short_grad,
            cond_weight_grad,
            slope_full,
            shift_full,
            skip_full,
            ffn_gain_part,
        ),
        ("rows", "seq"),
    )
    proj_in_grad = summed[:, : 3 * model_width]
    proj_out_grad = summed[:, 3 * model_width : 4 * model_width]
    ffn_in_grad = summed[:, 4 * model_width : 4 * model_width + 2 * hidden_width]
    ffn_out_grad = jnp.transpose(summed[:, 4 * model_width + 2 * hidden_width :])
    return (
        output,
        input_grad,
        small_sums[0],
        proj_in_grad,
        small_sums[1],
        small_sums[2],
        small_sums[3],
        small_sums[4],
        small_sums[5],
        proj_out_grad,
        small_sums[6],
        ffn_in_grad,
        ffn_out_grad,
    )


def per_device_any(*args):
    rows, width = args[0].shape[0], args[0].shape[2]
    even = rows % lax.axis_size("seq") == 0 and width % 256 == 0
    return (per_device_rows if even else per_device)(*args)


def solution(mesh):
    in_specs = (
        P("rows", "seq", None),
        P("rows"),
        P("rows", "seq"),
        P(),
        P(),
        P(),
        P(),
        P(),
        P(),
        P(),
        P(),
        P(),
        P(),
        P(),
        P("rows", "seq", None),
    )
    out_specs = (
        P("rows", "seq", None),
        P("rows", "seq", None),
        P(),
        P("rows", None),
        P(),
        P(),
        P(),
        P(),
        P(),
        P("rows", None),
        P(),
        P("rows", None),
        P(None, "rows"),
    )
    return jax.shard_map(
        per_device_any, mesh=mesh, in_specs=in_specs, out_specs=out_specs, check_vma=False
    )
```

```python
import functools
import math

import jax
import jax.numpy as jnp
from jax import lax
from jax.experimental import pallas as pl
from jax.experimental.pallas import tpu as pltpu
from jax.sharding import PartitionSpec as P

EPSILON = 1e-05
BF = jnp.bfloat16
F32 = jnp.float32
ROOT_HALF = math.sqrt(0.5)
LIMIT = 67043328


def mm(a, b):
    return lax.dot_general(a, b, (((1,), (0,)), ((), ())), preferred_element_type=F32)


def mm_t(a, b):
    return lax.dot_general(a, b, (((1,), (1,)), ((), ())), preferred_element_type=F32)


def spectral_tables(length, offset):
    quarter = length // 4
    two_n = 2 * length
    m = lax.broadcasted_iota(jnp.int32, (quarter, quarter), 0)
    s = lax.broadcasted_iota(jnp.int32, (quarter, quarter), 1)

    def cos_sin(freq):
        angle = ((freq * s + offset) % two_n).astype(F32) * (2.0 * math.pi / two_n)
        return jnp.cos(angle), jnp.sin(angle)

    half = quarter // 2
    forward, inverse = [], []
    for r in (1, 2, 3):
        c, sn = cos_sin(8 * m + r)
        forward.append(jnp.concatenate([jnp.concatenate([c, sn], 1), jnp.concatenate([-sn, c], 1)], 0))
        inverse.append(forward[-1].T * (2.0 / two_n))
    row = m % half
    low = m < half
    c, sn = cos_sin(8 * jnp.where(m == half, half, row))
    zero = jnp.where(low | (m == half), c, -sn)
    c4, sn4 = cos_sin(8 * row + 4)
    four = jnp.where(low, c4, -sn4)
    edge = jnp.where((m == 0) | (m == half), 1.0, 2.0) / two_n
    fwd_real = jnp.concatenate([zero, four], 0)
    inv_real = jnp.concatenate([(zero * edge).T, four.T * (2.0 / two_n)], 0)
    return (
        fwd_real.astype(BF),
        jnp.concatenate(forward, 0).astype(BF),
        inv_real.astype(BF),
        jnp.concatenate(inverse, 0).astype(BF),
    )


def loop(count, body, unroll=1):
    lax.fori_loop(0, count, lambda i, c: (body(i), c)[1], 0, unroll=unroll)


def rows_of(i, size):
    return pl.ds(pl.multiple_of(i * size, size), size)


def norm_stats(v):
    center = v - jnp.mean(v, axis=-1, keepdims=True)
    scale = lax.rsqrt(jnp.mean(center * center, axis=-1, keepdims=True) + EPSILON)
    return center * scale, scale


def same_masks(position, split):
    same_one = position != split
    return same_one, same_one & (position != split + 1)


def butterfly(x_ref, y_ref, lane, width, quarter):
    tile = 32
    lanes = slice(lane, lane + width)

    def body(i):
        x0, x1, x2, x3 = [
            x_ref[pl.ds(pl.multiple_of(q * quarter + i * tile, tile), tile), :].astype(F32) for q in range(4)
        ]
        a, b, c, d = x0 + x2, x1 + x3, x0 - x2, x1 - x3
        sd, sb = d * ROOT_HALF, b * ROOT_HALF
        out = (a + b, a - b, x0 + sd, -x2 - sb, c, -d, x0 - sd, x2 - sb)
        for k, value in enumerate(out):
            y_ref[pl.ds(pl.multiple_of(k * quarter + i * tile, tile), tile), lanes] = value.astype(BF)

    loop(quarter // tile, body)


def blockwise(y_ref, spec_ref, fwd_real_ref, fwd_ref, quarter):
    q = quarter
    for k in range(2):
        spec_ref[k * q : (k + 1) * q, :] = mm(fwd_real_ref[k * q : (k + 1) * q, :], y_ref[k * q : (k + 1) * q, :])
    for k in range(3):
        spec_ref[2 * q + 2 * k * q : 2 * q + 2 * (k + 1) * q, :] = mm(
            fwd_ref[2 * k * q : 2 * (k + 1) * q, :], y_ref[2 * q + 2 * k * q : 2 * q + 2 * (k + 1) * q, :]
        )


def resynth(u_ref, out_ref, inv_real_ref, inv_ref, quarter):
    blockwise(u_ref, out_ref, inv_real_ref, inv_ref, quarter)


def each_bin(quarter, body, tile=64):
    half = quarter // 2
    body(0, half, True)

    def run(base, span, skip):
        def step(i):
            start = base + (i + skip) * tile
            body(start, start + span, False)

        loop(span // tile - skip, step)

    run(0, half, 1)
    run(quarter, half, 0)
    for k in range(3):
        run(2 * quarter + 2 * k * quarter, quarter, 0)


def recombine(o_ref, lanes, i, tile, quarter):
    def part(k):
        return o_ref[pl.ds(pl.multiple_of(k * quarter + i * tile, tile), tile), lanes]

    u0, u4, a1, b1, a2, b2, a3, b3 = [part(k) for k in range(8)]
    even, odd = u0 + u4, u0 - u4
    return (
        even + a1 + a2 + a3,
        odd + (a1 - b1 - a3 - b3) * ROOT_HALF - b2,
        even - b1 - a2 + b3,
        odd + (a3 - b3 - a1 - b1) * ROOT_HALF + b2,
    )


def conv_back(ref, t, tile, weights, split):
    block = ref[pl.ds(pl.multiple_of(t, tile), tile + 8), :]
    width = block.shape[1]
    position = t + lax.broadcasted_iota(jnp.int32, (tile, width), 0)
    one, two = same_masks(position, split)
    return (
        weights[0:1, :] * block[8 : tile + 8]
        + jnp.where(one, weights[1:2, :] * block[7 : tile + 7], 0.0)
        + jnp.where(two, weights[2:3, :] * block[6 : tile + 6], 0.0)
    )


def mixer_forward_kernel(
    first_row, earlier, split_ref, keep_ref, x_ref, norm_gain_ref, wq_ref, wk_ref, wv_ref, fq_ref, fv_ref, fk_ref, slope_ref, shift_ref,
    skip_ref, wo_ref, ffn_gain_ref, fwd_real_ref, fwd_ref, inv_real_ref, inv_ref,
    *refs,
):
    first_ref, q_ref, k_ref, v_ref, mixed_ref, gated_ref, resid_ref, second_ref = refs[earlier : earlier + 8]
    qs, ks, vs, xv, xc, y_s, spec_s, u_s, o_s, qc = refs[earlier + 8 :]
    r, j = first_row + pl.program_id(0), pl.program_id(1)
    length, width = q_ref.shape
    quarter = length // 4
    split, keep = split_ref[r], keep_ref[r]
    tile = 128

    @pl.when(j == 0)
    def _():
        def body(i):
            rows = rows_of(i, tile)
            v = x_ref[rows, :].astype(F32)
            n, _ = norm_stats(v)
            first_ref[rows, :] = (n * norm_gain_ref[...]).astype(BF)
            resid_ref[rows, :] = v

        loop(length // tile, body, 2)
        for ref in (qs, ks, vs):
            ref[0:8, :] = jnp.zeros((8, width), F32)

    for w_ref, out_ref, ref in ((wq_ref, q_ref, qs), (wk_ref, k_ref, ks), (wv_ref, v_ref, vs)):
        value = mm(first_ref[...], w_ref[...]).astype(BF)
        out_ref[...] = value
        ref[8 : 8 + length, :] = value.astype(F32)

    def conv(i):
        t = i * tile
        rows = rows_of(i, tile)
        kept = t + lax.broadcasted_iota(jnp.int32, (tile, width), 0) < keep
        qc[rows, :] = conv_back(qs, t, tile, fq_ref, split)
        xv[rows, :] = jnp.where(kept, conv_back(vs, t, tile, fv_ref, split), 0.0).astype(BF)
        xc[rows, :] = jnp.where(kept, conv_back(ks, t, tile, fk_ref, split), 0.0).astype(BF)

    loop(length // tile, conv)
    butterfly(xv, y_s, 0, width, quarter)
    butterfly(xc, y_s, width, width, quarter)
    blockwise(y_s, spec_s, fwd_real_ref, fwd_ref, quarter)

    def bins(re, im, first):
        n = 64
        re, im = pl.ds(pl.multiple_of(re, n), n), pl.ds(pl.multiple_of(im, n), n)
        vr, vi = spec_s[re, 0:width], spec_s[im, 0:width]
        cr, ci = spec_s[re, width : 2 * width], spec_s[im, width : 2 * width]
        slope, shift = slope_ref[...], shift_ref[...]
        rr, ii = cr * cr, ci * ci
        if first:
            edge = lax.broadcasted_iota(jnp.int32, (n, width), 0) == 0
            hr = cr * jax.nn.sigmoid(slope * jnp.where(edge, rr, rr + ii) + shift)
            hi = ci * jax.nn.sigmoid(slope * jnp.where(edge, ii, rr + ii) + shift)
            ur = vr * hr - jnp.where(edge, 0.0, vi * hi)
            ui = jnp.where(edge, vi * hi, vr * hi + vi * hr)
        else:
            gain = jax.nn.sigmoid(slope * (rr + ii) + shift)
            hr, hi = cr * gain, ci * gain
            ur, ui = vr * hr - vi * hi, vr * hi + vi * hr
        u_s[re, :] = ur.astype(BF)
        u_s[im, :] = ui.astype(BF)

    each_bin(quarter, bins)
    resynth(u_s, o_s, inv_real_ref, inv_ref, quarter)

    def finish(i):
        n = 32
        parts = recombine(o_s, slice(0, width), i, n, quarter)
        for k, part in enumerate(parts):
            rows = pl.ds(pl.multiple_of(k * quarter + i * n, n), n)
            mixed = (part + skip_ref[...] * xv[rows, :].astype(F32)).astype(BF)
            mixed_ref[rows, :] = mixed
            gated_ref[rows, :] = (qc[rows, :] * mixed.astype(F32)).astype(BF)

    loop(quarter // 32, finish)
    resid_ref[...] += mm(gated_ref[...], wo_ref[...])

    @pl.when(j == pl.num_programs(1) - 1)
    def _():
        def body(i):
            rows = rows_of(i, tile)
            n, _ = norm_stats(resid_ref[rows, :])
            second_ref[rows, :] = (n * ffn_gain_ref[...]).astype(BF)

        loop(length // tile, body, 2)


def once(shape, index):
    return pl.BlockSpec(shape, index, pipeline_mode=pl.Buffered(1))


def mixer_specs(length, model, width, first_row):
    blocks = model // width
    row = pl.BlockSpec((None, length, model), lambda r, j, *_: (r + first_row, 0, 0))
    part = pl.BlockSpec((None, length, width), lambda r, j, *_: (r + first_row, 0, j))

    def columns(rows, offset):
        return pl.BlockSpec((rows, width), lambda r, j, *_: (0, j + offset * blocks))

    out_rows = pl.BlockSpec((width, model), lambda r, j, *_: (j, 0))
    gain = once((1, model), lambda r, j, *_: (0, 0))
    q = length // 4
    tables = [once((2 * q, q), lambda r, j, *_: (0, 0)), once((6 * q, 2 * q), lambda r, j, *_: (0, 0))]
    return blocks, row, part, columns, out_rows, gain, tables + tables


def mixer_forward(x, split, keep, norm_gain, proj_in, short_filter, cond_filter, slope, shift, skip, proj_out, ffn_gain, tables, first_row, total_rows, earlier, width=256):
    rows, length, model = x.shape
    blocks, row, part, columns, out_rows, gain, table_specs = mixer_specs(length, model, width, first_row)
    x_row = pl.BlockSpec((None, length, model), lambda r, j, *_: (r, 0, 0))
    one = columns(1, 0)
    shape = jax.ShapeDtypeStruct
    low, full = shape((total_rows, length, model), BF), shape((total_rows, length, model), F32)
    pad = pltpu.VMEM((length + 8, width), F32)
    flops = rows * (2 * length * model * (3 * model + model) + 2 * 3 * model * (2 * length) * length // 2)
    operands = (split, keep, x, norm_gain, proj_in, proj_in, proj_in, short_filter, short_filter, cond_filter, slope, shift, skip, proj_out, ffn_gain, *tables)
    return pl.pallas_call(
        functools.partial(mixer_forward_kernel, first_row, len(earlier)),
        out_shape=[low, low, low, low, low, low, full, low],
        grid_spec=pltpu.PrefetchScalarGridSpec(
            num_scalar_prefetch=2,
            grid=(rows, blocks),
            in_specs=[x_row, gain, columns(model, 0), columns(model, 1), columns(model, 2), columns(3, 0), columns(3, 1), columns(3, 0), one, one, one, out_rows, gain] + table_specs + [pl.BlockSpec(memory_space=pl.ANY)] * len(earlier),
            out_specs=[row, part, part, part, part, part, row, row],
            scratch_shapes=[pad, pad, pad] + [pltpu.VMEM((length, width), BF)] * 2 + [
                pltpu.VMEM((2 * length, 2 * width), BF),
                pltpu.VMEM((2 * length, 2 * width), F32),
                pltpu.VMEM((2 * length, width), BF),
                pltpu.VMEM((2 * length, width), F32),
                pltpu.VMEM((length, width), F32),
            ],
        ),
        compiler_params=pltpu.CompilerParams(dimension_semantics=("arbitrary", "arbitrary"), vmem_limit_bytes=LIMIT),
        cost_estimate=pl.CostEstimate(flops=flops, bytes_accessed=rows * length * model * 20, transcendentals=rows * length * model),
        input_output_aliases={len(operands) + k: k for k in range(len(earlier))},
        name="mixer_forward",
    )(*operands, *earlier)


def normal_cdf_pdf(x):
    z = jnp.abs(x) * ROOT_HALF
    t = 1.0 / (1.0 + 0.3275911 * z)
    e = jnp.exp(-z * z)
    poly = t * (0.127414796 + t * (-0.142248368 + t * (0.7107068705 + t * (-0.7265760135 + t * 0.5307027145))))
    tail = poly * e
    return jnp.where(x >= 0, 1.0 - tail, tail), x * e * (1.0 / math.sqrt(2.0 * math.pi))


def ffn_kernel(
    sa_ref, og_ref, sat_ref, ogt_ref, wg_ref, wu_ref, wo_ref, out_ref, back_ref, grads_ref, *scratch
):
    j = pl.program_id(0)
    tokens, model = sa_ref.shape
    streams = [scratch[6 * n : 6 * n + 6] for n in range(2)]
    tile = streams[0][0].shape[0]
    half = tokens // 2
    steps = half // tile
    chunk = 32

    @pl.when(j == 0)
    def _():
        def body(i):
            out_ref[rows_of(i, tile), :] = jnp.zeros((tile, model), F32)
            back_ref[rows_of(i, tile), :] = jnp.zeros((tile, model), F32)

        loop(tokens // tile, body)

    def place(n, i, size=tile, offset=0):
        return pl.ds(pl.multiple_of(n * half + i * tile + offset, size), size)

    def products(n, i):
        gs, us, ds = streams[n][:3]
        rows = place(n, i)
        sa = sa_ref[rows, :]
        gs[...] = mm(sa, wg_ref[...])
        us[...] = mm(sa, wu_ref[...])
        ds[...] = mm_t(og_ref[rows, :], wo_ref[...])

    def elementwise(n, i):
        gs, us, ds, hid, gg, ug = streams[n]
        for c in range(tile // chunk):
            part = slice(c * chunk, (c + 1) * chunk)
            gate, up, dh = gs[part, :], us[part, :], ds[part, :]
            cdf, xpdf = normal_cdf_pdf(gate)
            act = gate * cdf
            target = place(0, i, chunk, c * chunk)
            hid[target, :] = (act * up).astype(BF)
            gg[target, :] = (dh * up * (cdf + xpdf)).astype(BF)
            ug[target, :] = (dh * act).astype(BF)

    def sums(n, i):
        hid, gg, ug = streams[n][3:]
        rows, source = place(n, i), place(0, i)
        out_ref[rows, :] += mm(hid[source, :], wo_ref[...])
        back_ref[rows, :] += mm_t(gg[source, :], wg_ref[...]) + mm_t(ug[source, :], wu_ref[...])

    products(0, 0)
    products(1, 0)
    elementwise(0, 0)

    def body(i):
        products(0, i + 1)
        sums(0, i)
        elementwise(1, i)
        products(1, i + 1)
        sums(1, i)
        elementwise(0, i + 1)

    loop(steps - 1, body)
    last = steps - 1
    sums(0, last)
    elementwise(1, last)
    sums(1, last)
    (hid0, gg0, ug0), (hid1, gg1, ug1) = streams[0][3:], streams[1][3:]
    for k, (ref, first, second) in enumerate(((sat_ref, gg0, gg1), (sat_ref, ug0, ug1), (ogt_ref, hid0, hid1))):
        grads_ref[k] = (mm(ref[:, 0:half], first[...]) + mm(ref[:, half:tokens], second[...])).astype(BF)


def ffn_both(second_act, out_grad, second_turned, grad_turned, ffn_in, ffn_out, share, width=512, tile=512):
    tokens, model = second_act.shape
    total_blocks = ffn_out.shape[0] // width
    first, last = (total_blocks * n // 3 for n in share)
    blocks = last - first
    hidden = blocks * width
    shape = jax.ShapeDtypeStruct
    whole = once((tokens, model), lambda j: (0, 0))
    turned = once((model, tokens), lambda j: (0, 0))
    return pl.pallas_call(
        ffn_kernel,
        out_shape=[shape((tokens, model), F32), shape((tokens, model), F32), shape((3, model, hidden), BF)],
        grid=(blocks,),
        in_specs=[
            whole, whole, turned, turned,
            pl.BlockSpec((model, width), lambda j: (0, j + first)),
            pl.BlockSpec((model, width), lambda j: (0, j + first + total_blocks)),
            pl.BlockSpec((width, model), lambda j: (j + first, 0)),
        ],
        out_specs=[whole, whole, pl.BlockSpec((3, model, width), lambda j: (0, 0, j))],
        scratch_shapes=([pltpu.VMEM((tile, width), F32)] * 3 + [pltpu.VMEM((tokens // 2, width), BF)] * 3) * 2,
        compiler_params=pltpu.CompilerParams(dimension_semantics=("arbitrary",), vmem_limit_bytes=LIMIT),
        cost_estimate=pl.CostEstimate(flops=18 * tokens * model * hidden, bytes_accessed=tokens * model * 24 + model * hidden * 12, transcendentals=tokens * hidden),
        name="ffn_both",
    )(second_act, out_grad, second_turned, grad_turned, ffn_in, ffn_in, ffn_out)


def norm_back_kernel(pieces, resid_ref, *refs):
    sum_refs, back_refs = refs[:pieces], refs[pieces : 2 * pieces]
    og_ref, gain_ref, out_ref, grad_ref, low_ref, gain_grad_ref = refs[2 * pieces :]

    @pl.when(pl.program_id(0) == 0)
    def _():
        gain_grad_ref[...] = jnp.zeros_like(gain_grad_ref)

    tile = 64

    def body(i):
        rows = rows_of(i, tile)
        resid = resid_ref[rows, :]
        n, scale = norm_stats(resid)
        u = sum(ref[rows, :] for ref in back_refs)
        ug = u * gain_ref[...]
        un = u * n
        part = ug - jnp.mean(ug, axis=-1, keepdims=True) - n * jnp.mean(ug * n, axis=-1, keepdims=True)
        grad = og_ref[rows, :].astype(F32) + scale * part
        out_ref[rows, :] = (resid + sum(ref[rows, :] for ref in sum_refs)).astype(BF)
        grad_ref[rows, :] = grad
        low_ref[rows, :] = grad.astype(BF)
        gain_grad_ref[...] += jnp.sum(un.reshape(tile // 8, 8, un.shape[1]), axis=0)

    loop(resid_ref.shape[0] // tile, body)


def norm_back(resid, totals, backs, out_grad, gain, tile=512):
    tokens, model = resid.shape
    pieces = len(totals)
    shape = jax.ShapeDtypeStruct
    block = pl.BlockSpec((tile, model), lambda i: (i, 0))
    fixed = pl.BlockSpec((8, model), lambda i: (0, 0))
    return pl.pallas_call(
        functools.partial(norm_back_kernel, pieces),
        out_shape=[shape((tokens, model), BF), shape((tokens, model), F32), shape((tokens, model), BF), shape((8, model), F32)],
        grid=(tokens // tile,),
        in_specs=[block] * (2 * pieces + 2) + [pl.BlockSpec((1, model), lambda i: (0, 0))],
        out_specs=[block, block, block, fixed],
        compiler_params=pltpu.CompilerParams(dimension_semantics=("arbitrary",), vmem_limit_bytes=LIMIT),
        cost_estimate=pl.CostEstimate(flops=20 * tokens * model, bytes_accessed=tokens * model * 22, transcendentals=tokens),
        name="norm_back",
    )(resid, *totals, *backs, out_grad, gain)


def eight_sum(v):
    return jnp.sum(v.reshape(v.shape[0] // 8, 8, v.shape[1]), axis=0)


def mixer_backward_kernel(
    split_ref, keep_ref, low_ref, q_ref, k_ref, v_ref, mixed_ref, wo_ref,
    fq_ref, fv_ref, fk_ref, slope_ref, shift_ref, skip_ref, fwd_real_ref, fwd_ref, inv_real_ref, inv_ref,
    p_ref, chan_ref,
    qs, ks, vs, xv, xc, xy, y_s, spec_s, u_s, o_s,
):
    r = pl.program_id(1)
    length, width = q_ref.shape
    quarter = length // 4
    split, keep = split_ref[r], keep_ref[r]
    tile = 128

    @pl.when(r == 0)
    def _():
        chan_ref[...] = jnp.zeros_like(chan_ref)

    for ref, source in ((qs, q_ref), (ks, k_ref), (vs, v_ref)):
        ref[0:8, :] = jnp.zeros((8, width), F32)

        def widen(i, ref=ref, source=source):
            ref[pl.ds(pl.multiple_of(8 + i * tile, 8), tile), :] = source[rows_of(i, tile), :].astype(F32)

        loop(length // tile, widen)

    o_s[0:length, 0:width] = mm_t(low_ref[...], wo_ref[...])

    def conv(i):
        t = i * tile
        rows = rows_of(i, tile)
        kept = t + lax.broadcasted_iota(jnp.int32, (tile, width), 0) < keep
        gated_grad = o_s[rows, 0:width]
        low = (gated_grad * conv_back(qs, t, tile, fq_ref, split)).astype(BF)
        xy[rows, :] = low
        value = jnp.where(kept, conv_back(vs, t, tile, fv_ref, split), 0.0).astype(BF)
        xv[rows, :] = value
        xc[rows, :] = jnp.where(kept, conv_back(ks, t, tile, fk_ref, split), 0.0).astype(BF)
        chan_ref[2, :, :] += eight_sum(low.astype(F32) * value.astype(F32))

    loop(length // tile, conv)
    butterfly(xv, y_s, 0, width, quarter)
    butterfly(xc, y_s, width, width, quarter)
    butterfly(xy, y_s, 2 * width, width, quarter)

    def query(i):
        rows = rows_of(i, tile)
        qs[rows, :] = o_s[rows, 0:width] * mixed_ref[rows, :].astype(F32)

    loop(length // tile, query)
    blockwise(y_s, spec_s, fwd_real_ref, fwd_ref, quarter)

    def bins(re, im, first):
        n = 64
        re, im = pl.ds(pl.multiple_of(re, n), n), pl.ds(pl.multiple_of(im, n), n)
        vr, vi = spec_s[re, 0:width], spec_s[im, 0:width]
        cr, ci = spec_s[re, width : 2 * width], spec_s[im, width : 2 * width]
        yr, yi = spec_s[re, 2 * width : 3 * width], spec_s[im, 2 * width : 3 * width]
        slope, shift = slope_ref[...], shift_ref[...]
        rr, ii = cr * cr, ci * ci
        if first:
            edge = lax.broadcasted_iota(jnp.int32, (n, width), 0) == 0
            pr, pi = jnp.where(edge, rr, rr + ii), jnp.where(edge, ii, rr + ii)
            gr, gi = jax.nn.sigmoid(slope * pr + shift), jax.nn.sigmoid(slope * pi + shift)
            ar = vr * yr + jnp.where(edge, 0.0, vi * yi)
            ai = jnp.where(edge, -vi * yi, vi * yr - vr * yi)
            br = ar * cr - jnp.where(edge, 0.0, ai * ci)
            bi = jnp.where(edge, -ai * ci, br)
            wr, wi = br * gr * (1.0 - gr), bi * gi * (1.0 - gi)
            ws = jnp.where(edge, 0.5 * (wr + wi), wr)
            wp = jnp.where(edge, 0.5 * (wr * pr + wi * pi), wr * pr)
            hr, hi = gr * cr, gi * ci
            er = hr * yr + jnp.where(edge, 0.0, hi * yi)
            ei = jnp.where(edge, hi * yi, hr * yi - hi * yr)
            dr = gr * ar + 2.0 * slope * wr * cr
            di = 2.0 * slope * wi * ci - gi * ai
        else:
            p = rr + ii
            g = jax.nn.sigmoid(slope * p + shift)
            ar, ai = vr * yr + vi * yi, vi * yr - vr * yi
            ws = (ar * cr - ai * ci) * (g * (1.0 - g))
            wp = ws * p
            hr, hi = g * cr, g * ci
            er, ei = hr * yr + hi * yi, hr * yi - hi * yr
            k = 2.0 * slope * ws
            dr, di = g * ar + k * cr, k * ci - g * ai
        chan_ref[0, :, :] += eight_sum(wp)
        chan_ref[1, :, :] += eight_sum(ws)
        u_s[re, 0:width] = er.astype(BF)
        u_s[im, 0:width] = ei.astype(BF)
        u_s[re, width : 2 * width] = dr.astype(BF)
        u_s[im, width : 2 * width] = di.astype(BF)

    each_bin(quarter, bins)
    resynth(u_s, o_s, inv_real_ref, inv_ref, quarter)

    def finish(i):
        n = 32
        value = recombine(o_s, slice(0, width), i, n, quarter)
        cond = recombine(o_s, slice(width, 2 * width), i, n, quarter)
        for k in range(4):
            rows = pl.ds(pl.multiple_of(k * quarter + i * n, n), n)
            kept = k * quarter + i * n + lax.broadcasted_iota(jnp.int32, (n, width), 0) < keep
            grad = (value[k] + skip_ref[...] * xy[rows, :].astype(F32)).astype(BF).astype(F32)
            vs[rows, :] = jnp.where(kept, grad, 0.0)
            ks[rows, :] = jnp.where(kept, cond[k].astype(BF).astype(F32), 0.0)

    loop(quarter // 32, finish)
    for ref in (qs, ks, vs):
        ref[length : length + 8, :] = jnp.zeros((8, width), F32)

    for slot, (ref, source, f_ref) in enumerate(((qs, q_ref, fq_ref), (vs, v_ref, fv_ref), (ks, k_ref, fk_ref))):

        def adjoint(i, slot=slot, ref=ref, source=source, f_ref=f_ref):
            t = i * tile
            rows = rows_of(i, tile)
            block = ref[pl.ds(pl.multiple_of(t, tile), tile + 8), :]
            position = t + lax.broadcasted_iota(jnp.int32, (tile, width), 0)
            g0 = block[0:tile]
            g1 = jnp.where(position + 1 != split, block[1 : tile + 1], 0.0)
            g2 = jnp.where((position + 2 != split) & (position + 1 != split), block[2 : tile + 2], 0.0)
            s = source[rows, :].astype(F32)
            place = slice((0, 2, 1)[slot] * width, ((0, 2, 1)[slot] + 1) * width)
            p_ref[rows, place] = (f_ref[0:1, :] * g0 + f_ref[1:2, :] * g1 + f_ref[2:3, :] * g2).astype(BF)
            for k, g in enumerate((g0, g1, g2)):
                chan_ref[3 + 3 * slot + k, :, :] += eight_sum(g * s)

        loop(length // tile, adjoint)


def mixer_backward(branch_low, split, keep, q, k, v, mixed, proj_out, short_filter, cond_filter, slope, shift, skip, tables, width=256):
    rows, length, model = q.shape
    blocks = model // width
    shape = jax.ShapeDtypeStruct
    pad = pltpu.VMEM((length + 8, width), F32)
    quarter = length // 4
    row = pl.BlockSpec((None, length, model), lambda j, r, *_: (r, 0, 0))
    part = pl.BlockSpec((None, length, width), lambda j, r, *_: (r, 0, j))

    def columns(size, offset):
        return pl.BlockSpec((size, width), lambda j, r, *_: (0, j + offset * blocks))

    fixed = lambda j, r, *_: (0, 0)
    table_specs = [once((2 * quarter, quarter), fixed), once((6 * quarter, 2 * quarter), fixed)] * 2
    one = columns(1, 0)
    flops = rows * (2 * length * model * model + 2 * 5 * model * (2 * length) * length // 2)
    return pl.pallas_call(
        mixer_backward_kernel,
        out_shape=[shape((rows, length, 3 * model), BF), shape((12, 8, model), F32)],
        grid_spec=pltpu.PrefetchScalarGridSpec(
            num_scalar_prefetch=2,
            grid=(blocks, rows),
            in_specs=[row, part, part, part, part, pl.BlockSpec((width, model), lambda j, r, *_: (j, 0)), columns(3, 0), columns(3, 1), columns(3, 0), one, one, one] + table_specs,
            out_specs=[pl.BlockSpec((None, length, 3 * width), lambda j, r, *_: (r, 0, j)), pl.BlockSpec((12, 8, width), lambda j, r, *_: (0, 0, j))],
            scratch_shapes=[pad, pad, pad] + [pltpu.VMEM((length, width), BF)] * 3 + [
                pltpu.VMEM((2 * length, 3 * width), BF),
                pltpu.VMEM((2 * length, 3 * width), F32),
                pltpu.VMEM((2 * length, 2 * width), BF),
                pltpu.VMEM((2 * length, 2 * width), F32),
            ],
        ),
        compiler_params=pltpu.CompilerParams(dimension_semantics=("arbitrary", "arbitrary"), vmem_limit_bytes=LIMIT),
        cost_estimate=pl.CostEstimate(flops=flops, bytes_accessed=rows * length * (model * 2 * blocks + model * 14), transcendentals=rows * length * model),
        name="mixer_backward",
    )(split, keep, branch_low, q, k, v, mixed, proj_out, short_filter, short_filter, cond_filter, slope, shift, skip, *tables)


def input_back_kernel(width, x_ref, grad_ref, gain_ref, w_ref, p_ref, in_grad_ref, gain_grad_ref, acc):
    model = x_ref.shape[1]
    tile = 64

    @pl.when(pl.program_id(0) == 0)
    def _():
        gain_grad_ref[...] = jnp.zeros_like(gain_grad_ref)

    total = None
    for b in range(model // width):
        for k in range(3):
            place = (3 * b + k) * width
            term = mm_t(p_ref[:, place : place + width], w_ref[:, k * model + b * width : k * model + (b + 1) * width])
            total = term if total is None else total + term
    acc[...] = total

    def body(i):
        rows = rows_of(i, tile)
        n, scale = norm_stats(x_ref[rows, :].astype(F32))
        u = acc[rows, :]
        ug = u * gain_ref[...]
        part = ug - jnp.mean(ug, axis=-1, keepdims=True) - n * jnp.mean(ug * n, axis=-1, keepdims=True)
        in_grad_ref[rows, :] = (grad_ref[rows, :] + scale * part).astype(in_grad_ref.dtype)
        gain_grad_ref[...] += eight_sum(u * n)

    loop(x_ref.shape[0] // tile, body, 2)


def input_back(x, resid_grad, gain, proj_in, proj_grad, width, tile=512):
    tokens, model = x.shape
    shape = jax.ShapeDtypeStruct
    block = pl.BlockSpec((tile, model), lambda i: (i, 0))
    return pl.pallas_call(
        functools.partial(input_back_kernel, width),
        out_shape=[shape((tokens, model), BF), shape((8, model), F32)],
        grid=(tokens // tile,),
        in_specs=[block, block, once((1, model), lambda i: (0, 0)), once((model, 3 * model), lambda i: (0, 0)), pl.BlockSpec((tile, 3 * model), lambda i: (i, 0))],
        out_specs=[block, pl.BlockSpec((8, model), lambda i: (0, 0))],
        scratch_shapes=[pltpu.VMEM((tile, model), F32)],
        compiler_params=pltpu.CompilerParams(dimension_semantics=("arbitrary",), vmem_limit_bytes=LIMIT),
        cost_estimate=pl.CostEstimate(flops=6 * tokens * model * model, bytes_accessed=tokens * model * 14, transcendentals=tokens),
        name="input_back",
    )(x, resid_grad, gain, proj_in, proj_grad)


def turn(a, b):
    return lax.dot_general(a, b, (((0,), (0,)), ((), ())), preferred_element_type=F32).astype(BF)


def after(value, earlier):
    return lax.optimization_barrier((value, earlier))[0]


def exchange_sum_kernel(rows, seq, x_ref, send_ref, out_ref, other_ref, slots, total, send_sem, recv_sem, far_send_sem, far_recv_sem):
    r, s = lax.axis_index("rows"), lax.axis_index("seq")
    partners = []
    bit = 1
    while bit < rows:
        partners.append((r + bit - 2 * bit * (lax.rem(r // bit, 2)), s))
        bit *= 2
    bit = 1
    while bit < seq:
        partners.append((r, s + bit - 2 * bit * (lax.rem(s // bit, 2))))
        bit *= 2
    barrier = pltpu.get_barrier_semaphore()
    for partner in partners:
        pl.semaphore_signal(barrier, inc=1, device_id=partner, device_id_type=pl.DeviceIdType.MESH)
    pl.semaphore_wait(barrier, len(partners))
    part = other_ref.shape[1]
    far = pltpu.make_async_remote_copy(
        src_ref=send_ref.at[:, pl.ds(pl.multiple_of((1 - s) * part, part), part)], dst_ref=other_ref,
        send_sem=far_send_sem, recv_sem=far_recv_sem, device_id=(r, 1 - s), device_id_type=pl.DeviceIdType.MESH,
    )
    far.start()
    total[0] = x_ref[...]
    for step, partner in enumerate(partners):
        copy = pltpu.make_async_remote_copy(
            src_ref=total.at[step], dst_ref=slots.at[step], send_sem=send_sem.at[step], recv_sem=recv_sem.at[step],
            device_id=partner, device_id_type=pl.DeviceIdType.MESH,
        )
        copy.start()
        copy.wait()
        total[step + 1] = total[step] + slots[step]
    out_ref[...] = total[len(partners)]
    far.wait()


def power_of_two(n):
    return n & (n - 1) == 0


def exchange_sum(value, whole_rows):
    rows, seq = lax.axis_size("rows"), lax.axis_size("seq")
    if not (power_of_two(rows) and seq == 2):
        return lax.psum(value, ("rows", "seq")), scatter_rows(whole_rows).astype(F32)
    steps = rows.bit_length()
    own, length, model = whole_rows.shape
    part = length // 2
    shape = jax.ShapeDtypeStruct
    total, other = pl.pallas_call(
        functools.partial(exchange_sum_kernel, rows, seq),
        out_shape=[shape(value.shape, value.dtype), shape((own, part, model), whole_rows.dtype)],
        in_specs=[pl.BlockSpec(memory_space=pltpu.VMEM), pl.BlockSpec(memory_space=pl.ANY)],
        out_specs=[pl.BlockSpec(memory_space=pltpu.VMEM), pl.BlockSpec(memory_space=pl.ANY)],
        scratch_shapes=[
            pltpu.VMEM((steps, *value.shape), value.dtype),
            pltpu.VMEM((steps + 1, *value.shape), value.dtype),
            pltpu.SemaphoreType.DMA((steps,)),
            pltpu.SemaphoreType.DMA((steps,)),
            pltpu.SemaphoreType.DMA,
            pltpu.SemaphoreType.DMA,
        ],
        compiler_params=pltpu.CompilerParams(collective_id=7, has_side_effects=True),
        cost_estimate=pl.CostEstimate(flops=20_000_000_000, bytes_accessed=0, transcendentals=0),
        name="exchange_sum",
    )(value, whole_rows)
    return total, assemble(whole_rows, other)


def assemble_kernel(own, s_ref, mine_ref, other_ref, out_ref):
    out_ref[...] = jnp.where(pl.program_id(0) // own == s_ref[0], mine_ref[...], other_ref[...]).astype(F32)


def assemble(whole_rows, other):
    own, part, model = other.shape
    block = (None, part, model)
    return pl.pallas_call(
        functools.partial(assemble_kernel, own),
        out_shape=jax.ShapeDtypeStruct((2 * own, part, model), F32),
        grid_spec=pltpu.PrefetchScalarGridSpec(
            num_scalar_prefetch=1,
            grid=(2 * own,),
            in_specs=[pl.BlockSpec(block, lambda i, s: (i % own, s[0], 0)), pl.BlockSpec(block, lambda i, s: (i % own, 0, 0))],
            out_specs=pl.BlockSpec(block, lambda i, s: (i, 0, 0)),
        ),
        compiler_params=pltpu.CompilerParams(dimension_semantics=("arbitrary",), vmem_limit_bytes=LIMIT),
        name="assemble",
    )(lax.axis_index("seq").astype(jnp.int32)[None], whole_rows, other)


def swapped(value):
    count = lax.axis_size("seq")
    return lax.ppermute(value, "seq", [(i, (i + 1) % count) for i in range(count)])


def gather_rows(value, first=0, count=None):
    own = value.shape[0] // lax.axis_size("seq")
    count = own if count is None else count
    if lax.axis_size("seq") != 2:
        whole = lax.all_to_all(value, "seq", split_axis=0, concat_axis=1, tiled=True)
        return whole[first : first + count]
    s = lax.axis_index("seq")
    mine = lax.dynamic_slice_in_dim(value, s * own + first, count)
    other = swapped(lax.dynamic_slice_in_dim(value, (1 - s) * own + first, count))
    return jnp.concatenate([jnp.where(s == 0, mine, other), jnp.where(s == 0, other, mine)], axis=1)


def scatter_rows(value):
    if lax.axis_size("seq") != 2:
        return lax.all_to_all(value, "seq", split_axis=1, concat_axis=0, tiled=True)
    s = lax.axis_index("seq")
    part = value.shape[1] // 2
    mine = lax.dynamic_slice_in_dim(value, s * part, part, axis=1)
    other = swapped(lax.dynamic_slice_in_dim(value, (1 - s) * part, part, axis=1))
    return jnp.concatenate([jnp.where(s == 0, mine, other), jnp.where(s == 0, other, mine)], axis=0)


def seq_sum(value):
    if lax.axis_size("seq") != 2:
        return lax.psum(value, "seq").astype(F32)
    return value.astype(F32) + swapped(value).astype(F32)


def per_device_rows(inputs, split_point, keep_mask, norm_gain, proj_in, short_filter, cond_filter, spec_slope, spec_shift, skip_gain, proj_out, ffn_gain, ffn_in, ffn_out, out_grad):
    local_rows, local_len, model = inputs.shape
    count = lax.axis_size("seq")
    own = local_rows // count
    length = local_len * count
    tokens = own * length
    width = 256
    first_row = lax.axis_index("seq") * own
    flat = lambda a: a.reshape(tokens, model)
    flat_wide = lambda a: a.reshape(tokens, 3 * model)
    shaped = lambda a: a.reshape(own, length, model)
    lift = lambda a: a.reshape(1, -1)

    pieces = [(0, 1), (1, own - 1)] if own > 1 else [(0, own)]
    xs = []
    for start, size in pieces:
        xs.append(gather_rows(after(inputs, xs) if xs else inputs, start, size))
    kept = jnp.sum(keep_mask, axis=1)
    kept = kept + swapped(kept) if count == 2 else lax.psum(kept, "seq")
    keep = lax.dynamic_slice_in_dim(kept, first_row, own)
    split = lax.dynamic_slice_in_dim(split_point, first_row, own)
    tables = spectral_tables(length, lax.axis_index("seq") * (2 * length))
    slope, shift, skip = lift(spec_slope), lift(spec_shift), lift(skip_gain)

    held = ()
    for x, (start, size) in zip(xs, pieces):
        held = mixer_forward(
            x, split, keep, lift(norm_gain), proj_in, short_filter, cond_filter, slope, shift, skip, proj_out, lift(ffn_gain), tables, start, own, held
        )
        if start == 0:
            whole_grad = flat(gather_rows(after(out_grad, (xs[-1], held[-1]))))
    first, q, k, v, mixed, gated, resid, second = held
    x = jnp.concatenate(xs, axis=0)
    second = flat(second)
    second_turned, grad_turned = second.T, whole_grad.T
    totals, backs, grads = [], [], []
    for share in ((0, 1), (1, 3)):
        total, back, grad = ffn_both(second, whole_grad, second_turned, grad_turned, ffn_in, ffn_out, share)
        totals.append(total)
        backs.append(back)
        grads.append(grad)
    early_share = lax.psum_scatter(grads[0], "rows", scatter_dimension=1, tiled=True)
    output, resid_grad, branch_low, ffn_gain_part = norm_back(flat(resid), totals, backs, whole_grad, lift(ffn_gain))
    output = scatter_rows(shaped(output))
    out_part = turn(flat(gated), branch_low)
    grad, branch_low, early_share = lax.optimization_barrier((grads[1], branch_low, early_share))
    late_share = lax.psum_scatter(grad, "rows", scatter_dimension=1, tiled=True)
    proj_grad, chan = mixer_backward(shaped(branch_low), split, keep, q, k, v, mixed, proj_out, short_filter, cond_filter, slope, shift, skip, tables)
    proj_grad = flat_wide(proj_grad)
    mix_part = jnp.concatenate([out_part, turn(flat(first), proj_grad)], axis=1)
    mix_part, late_share = lax.optimization_barrier((mix_part, late_share))
    mix_share = lax.psum_scatter(mix_part, "rows", scatter_dimension=0, tiled=True)
    proj_grad = after(proj_grad, mix_part)
    input_grad, norm_gain_part = input_back(flat(x), resid_grad, lift(norm_gain), proj_in, proj_grad, width)
    ffn_shares = [seq_sum(early_share), seq_sum(late_share)]
    small = jnp.sum(jnp.concatenate([ffn_gain_part[None], norm_gain_part[None], chan], 0), axis=1)
    small, input_grad = exchange_sum(small, shaped(input_grad))
    scale = 1.0 / length
    mix_share = seq_sum(mix_share)
    in_share = mix_share[:, model:].reshape(-1, model // width, 3, width).transpose(0, 2, 1, 3)
    return (
        output,
        input_grad,
        small[1],
        in_share.reshape(-1, 3 * model),
        jnp.concatenate([small[5:8], small[8:11]], axis=1),
        small[11:14],
        small[2] * scale,
        small[3] * scale,
        small[4],
        mix_share[:, :model],
        small[0],
        jnp.concatenate([share[k] for k in range(2) for share in ffn_shares], axis=1),
        jnp.concatenate([share[2] for share in ffn_shares], axis=1).T,
    )


PRECISE = lax.Precision.HIGH


def passed_along(value, axis, steps):
    count = lax.axis_size(axis)
    leading, last = (max(0, -steps), min(count, count - steps))
    return lax.ppermute(value, axis, [(source, source + steps) for source in range(leading, last)])


def layer_norm(values, scaling):
    center = values - jnp.mean(values, axis=-1, keepdims=True)
    spread = jnp.mean(center * center, axis=-1, keepdims=True)
    return center * lax.rsqrt(spread + EPSILON) * scaling


def conv_three(extended, weights, same_one, same_two):
    length = extended.shape[1] - 2
    return (
        weights[0] * extended[:, 2:]
        + weights[1] * extended[:, 1 : length + 1] * same_one
        + weights[2] * extended[:, :length] * same_two
    )


def dft_tables(seq_length):
    table_shape = (seq_length + 1, seq_length)
    product = lax.broadcasted_iota(jnp.int32, table_shape, 0) * lax.broadcasted_iota(
        jnp.int32, table_shape, 1
    )
    angles = (product % (2 * seq_length)).astype(jnp.float32) * (math.pi / seq_length)
    freq = lax.broadcasted_iota(jnp.int32, (seq_length + 1, 1), 0)
    edge = jnp.logical_or(freq == 0, freq == seq_length)
    weights = jnp.where(edge, 1.0, 2.0).astype(jnp.float32) / (2.0 * seq_length)
    return (jnp.cos(angles), jnp.sin(angles), weights)


def analyze(values, conds, cos_table, sin_table):
    value_real = jnp.einsum("ft,ktd->kfd", cos_table, values, precision=PRECISE)
    value_imag = -jnp.einsum("ft,ktd->kfd", sin_table, values, precision=PRECISE)
    cond_real = jnp.einsum("ft,ktd->kfd", cos_table, conds, precision=PRECISE)
    cond_imag = -jnp.einsum("ft,ktd->kfd", sin_table, conds, precision=PRECISE)
    return (value_real, value_imag, cond_real, cond_imag)


def synth(
    value_real,
    value_imag,
    cond_real,
    cond_imag,
    values,
    slopes,
    shifts,
    skip_gains,
    cos_table,
    sin_table,
    freq_weights,
):
    factor = jax.nn.sigmoid(slopes * (cond_real * cond_real + cond_imag * cond_imag) + shifts)
    filter_real = cond_real * factor
    filter_imag = cond_imag * factor
    prod_real = (value_real * filter_real - value_imag * filter_imag) * freq_weights
    prod_imag = (value_real * filter_imag + value_imag * filter_real) * freq_weights
    mixed_out = jnp.einsum("ft,kfd->ktd", cos_table, prod_real, precision=PRECISE) - jnp.einsum(
        "ft,kfd->ktd", sin_table, prod_imag, precision=PRECISE
    )
    return mixed_out + skip_gains * values


def times_transpose(left, right):
    return lax.dot_general(
        left, right, (((1,), (1,)), ((), ())), preferred_element_type=jnp.float32
    )


def transpose_times(left, right):
    return lax.dot_general(
        left, right, (((0,), (0,)), ((), ())), preferred_element_type=jnp.float32
    )


def per_device(
    inputs,
    split_point,
    keep_mask,
    norm_gain,
    proj_in,
    short_filter,
    cond_filter,
    spec_slope,
    spec_shift,
    skip_gain,
    proj_out,
    ffn_gain,
    ffn_in,
    ffn_out,
    out_grad,
):
    local_rows, local_len, model_width = inputs.shape
    hidden_width = ffn_out.shape[0]
    seq_count = lax.axis_size("seq")
    seq_index = lax.axis_index("seq")
    full_len = local_len * seq_count
    chan_width = model_width // seq_count
    token_count = local_rows * local_len
    positions = seq_index * local_len + lax.broadcasted_iota(jnp.int32, (local_rows, local_len), 1)
    splits = split_point[:, None]
    segment = positions >= splits
    same_one = (segment == (positions - 1 >= splits)).astype(jnp.float32)[:, :, None]
    same_two = (segment == (positions - 2 >= splits)).astype(jnp.float32)[:, :, None]
    keep_float = keep_mask.astype(jnp.float32)[:, :, None]
    flat_in = inputs.reshape(token_count, model_width).astype(jnp.float32)
    normed_one, norm_one_back = jax.vjp(layer_norm, flat_in, norm_gain)
    first_act = normed_one.astype(jnp.bfloat16)
    projected = jnp.dot(first_act, proj_in, preferred_element_type=jnp.float32).astype(jnp.bfloat16)
    proj_rows = projected.reshape(local_rows, local_len, 3 * model_width)
    edge_values = passed_along(proj_rows[:, local_len - 2 :, :], "seq", 1)
    extended = jnp.concatenate([edge_values, proj_rows], axis=1).astype(jnp.float32)

    def mixer_local(ext_values, short_weights, cond_weights):
        query_value = jnp.concatenate(
            [ext_values[:, :, :model_width], ext_values[:, :, 2 * model_width :]], axis=2
        )
        conv_both = conv_three(query_value, short_weights, same_one, same_two)
        cond_conv = conv_three(
            ext_values[:, :, model_width : 2 * model_width], cond_weights, same_one, same_two
        )
        return (
            conv_both[:, :, :model_width],
            conv_both[:, :, model_width:] * keep_float,
            cond_conv * keep_float,
        )

    (query_conv, value_masked, cond_masked), mixer_back = jax.vjp(
        mixer_local, extended, short_filter, cond_filter
    )
    value_low = value_masked.astype(jnp.bfloat16)
    cond_low = cond_masked.astype(jnp.bfloat16)
    slope_part = lax.dynamic_slice_in_dim(spec_slope, seq_index * chan_width, chan_width)
    shift_part = lax.dynamic_slice_in_dim(spec_shift, seq_index * chan_width, chan_width)
    skip_part = lax.dynamic_slice_in_dim(skip_gain, seq_index * chan_width, chan_width)
    cos_table, sin_table, freq_weights = dft_tables(full_len)

    def synth_local(
        value_real, value_imag, cond_real, cond_imag, values, slopes, shifts, skip_gains
    ):
        return synth(
            value_real,
            value_imag,
            cond_real,
            cond_imag,
            values,
            slopes,
            shifts,
            skip_gains,
            cos_table,
            sin_table,
            freq_weights,
        )

    value_chan = lax.all_to_all(value_low, "seq", split_axis=2, concat_axis=1, tiled=True)
    cond_chan = lax.all_to_all(cond_low, "seq", split_axis=2, concat_axis=1, tiled=True)
    value_float = value_chan.astype(jnp.float32)
    spectra = analyze(value_float, cond_chan.astype(jnp.float32), cos_table, sin_table)
    mixed_chan = synth_local(
        spectra[0],
        spectra[1],
        spectra[2],
        spectra[3],
        value_float,
        slope_part,
        shift_part,
        skip_part,
    ).astype(jnp.bfloat16)
    mixed_home = lax.all_to_all(mixed_chan, "seq", split_axis=1, concat_axis=2, tiled=True)
    mixed_float = mixed_home.astype(jnp.float32)
    gated = (query_conv * mixed_float).astype(jnp.bfloat16).reshape(token_count, model_width)
    branch = jnp.dot(gated, proj_out, preferred_element_type=jnp.float32)
    resid = flat_in + branch
    normed_two, norm_two_back = jax.vjp(layer_norm, resid, ffn_gain)
    second_act = normed_two.astype(jnp.bfloat16)
    gate_up = jnp.dot(second_act, ffn_in, preferred_element_type=jnp.float32)

    def glu_local(both_parts):
        return (
            jax.nn.gelu(both_parts[:, :hidden_width], approximate=False)
            * both_parts[:, hidden_width:]
        )

    hidden, glu_back = jax.vjp(glu_local, gate_up)
    hidden_low = hidden.astype(jnp.bfloat16)
    result = resid + jnp.dot(hidden_low, ffn_out, preferred_element_type=jnp.float32)
    output = result.astype(jnp.bfloat16).reshape(local_rows, local_len, model_width)
    flat_grad = out_grad.reshape(token_count, model_width)
    hidden_grad = times_transpose(flat_grad, ffn_out)
    (gate_up_grad,) = glu_back(hidden_grad)
    gate_up_low = gate_up_grad.astype(jnp.bfloat16)
    second_grad = times_transpose(gate_up_low, ffn_in)
    resid_part, ffn_gain_part = norm_two_back(second_grad)
    resid_grad = flat_grad.astype(jnp.float32) + resid_part
    branch_low = resid_grad.astype(jnp.bfloat16)
    gated_grad = times_transpose(branch_low, proj_out).reshape(local_rows, local_len, model_width)
    query_grad = gated_grad * mixed_float
    mixed_grad = (gated_grad * query_conv).astype(jnp.bfloat16)
    grad_chan = lax.all_to_all(mixed_grad, "seq", split_axis=2, concat_axis=1, tiled=True)
    grad_float = grad_chan.astype(jnp.float32)
    item_count = grad_chan.shape[0]
    slope_items = jnp.broadcast_to(slope_part, (item_count, 1, chan_width))
    shift_items = jnp.broadcast_to(shift_part, (item_count, 1, chan_width))
    skip_items = jnp.broadcast_to(skip_part, (item_count, 1, chan_width))
    value_float = value_chan.astype(jnp.float32)

    def spectral(values, conds, slopes, shifts, skip_gains):
        spectra = analyze(values, conds, cos_table, sin_table)
        return synth_local(
            spectra[0], spectra[1], spectra[2], spectra[3], values, slopes, shifts, skip_gains
        )

    unused, pull = jax.vjp(
        spectral, value_float, cond_chan.astype(jnp.float32), slope_items, shift_items, skip_items
    )
    value_back, cond_back, slope_rows, shift_rows, skip_rows = pull(grad_float)
    value_grad, cond_grad = (
        lax.all_to_all(
            value_back.astype(jnp.bfloat16), "seq", split_axis=1, concat_axis=2, tiled=True
        ),
        lax.all_to_all(
            cond_back.astype(jnp.bfloat16), "seq", split_axis=1, concat_axis=2, tiled=True
        ),
    )
    start_chan = (seq_index * chan_width,)
    empty_width = jnp.zeros((model_width,), jnp.float32)
    slope_full = lax.dynamic_update_slice(empty_width, jnp.sum(slope_rows, axis=(0, 1)), start_chan)
    shift_full = lax.dynamic_update_slice(empty_width, jnp.sum(shift_rows, axis=(0, 1)), start_chan)
    skip_full = lax.dynamic_update_slice(empty_width, jnp.sum(skip_rows, axis=(0, 1)), start_chan)
    ext_grad, short_grad, cond_weight_grad = mixer_back(
        (query_grad, value_grad.astype(jnp.float32), cond_grad.astype(jnp.float32))
    )
    incoming = passed_along(ext_grad[:, :2, :].astype(jnp.bfloat16), "seq", -1).astype(jnp.float32)
    proj_grad = ext_grad[:, 2:, :] + jnp.pad(incoming, ((0, 0), (local_len - 2, 0), (0, 0)))
    proj_low = proj_grad.astype(jnp.bfloat16).reshape(token_count, 3 * model_width)
    first_grad = times_transpose(proj_low, proj_in)
    input_part, norm_gain_part = norm_one_back(first_grad)
    input_grad = (resid_grad + input_part).reshape(local_rows, local_len, model_width)
    share = lax.psum_scatter(
        jnp.concatenate(
            [
                transpose_times(first_act, proj_low),
                transpose_times(gated, branch_low),
                transpose_times(second_act, gate_up_low),
                transpose_times(flat_grad, hidden_low),
            ],
            axis=1,
        ).astype(jnp.bfloat16),
        "rows",
        scatter_dimension=0,
        tiled=True,
    )
    summed = lax.psum(share, "seq").astype(jnp.float32)
    small_sums = lax.psum(
        (
            norm_gain_part,
            short_grad,
            cond_weight_grad,
            slope_full,
            shift_full,
            skip_full,
            ffn_gain_part,
        ),
        ("rows", "seq"),
    )
    proj_in_grad = summed[:, : 3 * model_width]
    proj_out_grad = summed[:, 3 * model_width : 4 * model_width]
    ffn_in_grad = summed[:, 4 * model_width : 4 * model_width + 2 * hidden_width]
    ffn_out_grad = jnp.transpose(summed[:, 4 * model_width + 2 * hidden_width :])
    return (
        output,
        input_grad,
        small_sums[0],
        proj_in_grad,
        small_sums[1],
        small_sums[2],
        small_sums[3],
        small_sums[4],
        small_sums[5],
        proj_out_grad,
        small_sums[6],
        ffn_in_grad,
        ffn_out_grad,
    )


def per_device_any(*args):
    rows, width = args[0].shape[0], args[0].shape[2]
    even = rows % lax.axis_size("seq") == 0 and width % 256 == 0
    return (per_device_rows if even else per_device)(*args)


def solution(mesh):
    in_specs = (
        P("rows", "seq", None),
        P("rows"),
        P("rows", "seq"),
        P(),
        P(),
        P(),
        P(),
        P(),
        P(),
        P(),
        P(),
        P(),
        P(),
        P(),
        P("rows", "seq", None),
    )
    out_specs = (
        P("rows", "seq", None),
        P("rows", "seq", None),
        P(),
        P("rows", None),
        P(),
        P(),
        P(),
        P(),
        P(),
        P("rows", None),
        P(),
        P("rows", None),
        P(None, "rows"),
    )
    return jax.shard_map(
        per_device_any, mesh=mesh, in_specs=in_specs, out_specs=out_specs, check_vma=False
    )
```
